32 devices in a mesh: dp: 4 (over z), row: 4 (over y, core), col: 2 (over x).
Axes of the slice: x: 2, y: 2, z: 4, core: 2. Of those that a mesh axis runs over, the one named last changes fastest.
Arguments:
- tokens: bfloat16 [8192, 2048], P(('dp', 'col'), 'row'), may hold values from -6 to 6
- seq_ids: int32 [8192], P('dp'), may hold values from 0 to 7, as said below
- block_ids: int32 [8192], P('dp'), may hold values from 0 to 5, as said below
- positions: int32 [8192], P('dp'), may hold values from 0 to 1535, as said below
- norm1_gain: float32 [2048], P('row'), may hold values from 0.5 to 1.5
- norm2_gain: float32 [2048], P('row'), may hold values from 0.5 to 1.5
- w_query: bfloat16 [2048, 2048], P('row', 'col'), may hold values from -0.1875 to 0.1875
- w_kv: bfloat16 [2048, 256], P('row'), may hold values from -0.1875 to 0.1875
- w_out: bfloat16 [2048, 2048], P('col', 'row'), may hold values from -2 to 2
- w_gate: bfloat16 [2048, 5632], P('row', 'col'), may hold values from -0.125 to 0.125
- w_up: bfloat16 [2048, 5632], P('row', 'col'), may hold values from -0.125 to 0.125
- w_down: bfloat16 [5632, 2048], P('col', 'row'), may hold values from -0.078125 to 0.078125
- grad_output: float32 [8192, 2048], P(('dp', 'col'), 'row'), may hold values from -6 to 6
Outputs:
- output: float32 [8192, 2048], P(('dp', 'col'), 'row')
- input_grad: float32 [8192, 2048], P(('dp', 'col'), 'row')
- grad_query: float32 [4, 512, 2048], P('row', 'dp', 'col')
- grad_kv: float32 [4, 512, 256], P('row', ('dp', 'col'))
- grad_out: float32 [2, 1024, 2048], P('col', 'dp', 'row')
- grad_gate: float32 [4, 512, 5632], P('row', 'dp', 'col')
- grad_up: float32 [4, 512, 5632], P('row', 'dp', 'col')
- grad_down: float32 [2, 2816, 2048], P('col', 'dp', 'row')
- grad_norm1: float32 [4, 512], P('row', ('dp', 'col'))
- grad_norm2: float32 [4, 512], P('row', ('dp', 'col'))
The draws below stay inside these ranges and needn't reach their ends.
Inputs may be any that keep to these rules, and one draw needn't show every extreme that they name: `seq_ids`: tokens of one sequence lie in one aligned run of 2048 tokens; each run holds two sequences of whole 256-token blocks, each a quarter of the run or more; in the first run the first sequence has exactly 2 blocks. block_ids equal positions // 256. positions count from 0 at each sequence's first token.
All inputs are finite; a program needn't handle non-finite values.
Results may differ from the reference program's by a relative error of at most 0.023.
Values may be sent and summed in bfloat16 or wider, within the bound.
No kernel may reach another device: no remote copies, remote signals or barrier semaphores. Data moves between devices by JAX's collectives and lax.ppermute only.
A program may use at most 256 MiB of HBM per device.

```python
import jax
import jax.numpy as jnp
from jax import lax

D = 2048
HEADS = 16
HDIM = 128
FF = 5632
TOK_DP = 2048
BLOCK = 256
QW = 2048
TOKENS = 8192
N_ROW = 4
N_COL = 2


def index_tables(key):
    shard_count = TOKENS // TOK_DP
    block_count = TOK_DP // BLOCK
    drawn_cuts = jax.random.randint(jax.random.fold_in(key, 11), (shard_count,), block_count // 4, block_count - block_count // 4 + 1)
    shard_rank = jnp.arange(shard_count, dtype=jnp.int32)
    cut_points = jnp.where(shard_rank == 0, block_count // 4, drawn_cuts).astype(jnp.int32) * BLOCK
    local_rows = jnp.arange(TOK_DP, dtype=jnp.int32)
    second_doc = (local_rows[None, :] >= cut_points[:, None]).astype(jnp.int32)
    sequence = 2 * shard_rank[:, None] + second_doc
    position = local_rows[None, :] - second_doc * cut_points[:, None]
    return (sequence.reshape(-1), (position // BLOCK).reshape(-1), position.reshape(-1))


def draw_seq_ids(key, part):
    return index_tables(key)[0]


def draw_block_ids(key, part):
    return index_tables(key)[1]


def draw_positions(key, part):
    return index_tables(key)[2]


def level_of(own_key, shape, cuts, least, high):
    level = 1.0
    for dim, blocks in cuts:
        draws = jax.random.uniform(jax.random.fold_in(jax.random.fold_in(own_key, 6), dim), (blocks,), jnp.float32, least / len(cuts), high / len(cuts))
        level = level * jnp.repeat(jnp.exp(draws), shape[dim] // blocks).reshape((-1,) + (1,) * (len(shape) - 1 - dim))
    return level


def normal_values(rng, extent, deviation, limit, shards=(), held_as=jnp.bfloat16):
    drawn = deviation * jax.random.normal(rng, extent, jnp.float32)
    if shards:
        drawn = drawn * level_of(rng, extent, shards, -0.22, 0.18)
    return jnp.clip(drawn, -limit, limit).astype(held_as)


def setup_inputs(seed: int = 0) -> dict:
    seeds = jax.random.split(jax.random.key(seed), 14)
    return {
        "tokens": normal_values(seeds[0], (TOKENS, D), 1.0, 6.0, ((0, 8), (1, 4))),
        "seq_ids": draw_seq_ids(jax.random.fold_in(seeds[13], 71), 0),
        "block_ids": draw_block_ids(jax.random.fold_in(seeds[13], 71), 0),
        "positions": draw_positions(jax.random.fold_in(seeds[13], 71), 0),
        "norm1_gain": jnp.clip(1.0 + 0.1 * jax.random.normal(seeds[4], (D,), jnp.float32), 0.5, 1.5),
        "norm2_gain": jnp.clip(1.0 + 0.1 * jax.random.normal(seeds[5], (D,), jnp.float32), 0.5, 1.5),
        "w_query": normal_values(seeds[6], (D, QW), (D // 2) ** -0.5, 0.1875, ((0, 4), (1, 2))),
        "w_kv": normal_values(seeds[7], (D, 2 * HDIM), (D // 2) ** -0.5, 0.1875, ((0, 4),)),
        "w_out": normal_values(seeds[8], (QW, D), (max(QW // 256, 1)) ** -0.5, 2.0, ((0, 2), (1, 4))),
        "w_gate": normal_values(seeds[9], (D, FF), D ** -0.5, 0.125, ((0, 4), (1, 2))),
        "w_up": normal_values(seeds[10], (D, FF), D ** -0.5, 0.125, ((0, 4), (1, 2))),
        "w_down": normal_values(seeds[11], (FF, D), FF ** -0.5, 0.078125, ((0, 2), (1, 4))),
        "grad_output": normal_values(seeds[12], (TOKENS, D), 1.0, 6.0, ((0, 8), (1, 4)), jnp.float32),
    }


EPS = 1e-05
ROPE_BASE = 500000.0
MASKED = -1e+30

@jax.custom_vjp
def low(v):
    return lax.optimization_barrier(v.astype(jnp.bfloat16)).astype(jnp.float32)

@jax.custom_vjp
def low_back(v):
    return v

def low_keep(v):
    return (low(v), None)

def low_pass(kept, grad):
    return (grad,)

def back_keep(v):
    return (v, None)

def back_low(kept, grad):
    return (low(grad),)
low.defvjp(low_keep, low_pass)
low_back.defvjp(back_keep, back_low)

def rope_tables(positions, head_width):
    halfway = head_width // 2
    frequency = ROPE_BASE ** (-2.0 * jnp.arange(halfway, dtype=jnp.float32) / head_width)
    angles = positions.astype(jnp.float32)[:, None] * frequency[None, :]
    return (jnp.cos(angles), jnp.sin(angles))

def rotate(operand, cosine, sine_part):
    halfway = operand.shape[-1] // 2
    first_half = operand[..., :halfway]
    second_half = operand[..., halfway:]
    return jnp.concatenate([first_half * cosine - second_half * sine_part, second_half * cosine + first_half * sine_part], axis=-1)

def matmul(left_side, right_side):
    return jnp.dot(left_side, right_side, precision=lax.Precision.HIGHEST, preferred_element_type=jnp.float32)

def rms_scale(operand):
    return lax.rsqrt(lax.optimization_barrier(jnp.mean(operand * operand, axis=-1, keepdims=True)) + EPS)

def attention(queries, key_rows, values, seq_ids, block_ids):
    shard_count = seq_ids.shape[0] // TOK_DP
    q_block = min(512, TOK_DP)
    block_count = TOK_DP // q_block
    score_scale = HDIM ** (-0.5)

    def one_shard(shard_args):
        shard_q, shard_k, shard_v, shard_seq, shard_blk = shard_args

        def one_block(block_args):
            part_q, part_seq, part_blk = block_args
            scores = score_scale * jnp.einsum('qhd,kd->hqk', part_q, shard_k, precision=lax.Precision.HIGHEST)
            scores = low_back(scores)
            allowed = (part_seq[:, None] == shard_seq[None, :]) & (shard_blk[None, :] <= part_blk[:, None])
            scores = jnp.where(allowed[None], scores, MASKED)
            row_max = lax.optimization_barrier(jnp.max(scores, axis=-1, keepdims=True))
            weights_exp = jnp.exp(scores - row_max)
            probability = low(weights_exp / lax.optimization_barrier(jnp.sum(weights_exp, axis=-1, keepdims=True)))
            return jnp.einsum('hqk,kd->qhd', probability, shard_v, precision=lax.Precision.HIGHEST)
        result = lax.map(jax.checkpoint(one_block), (shard_q.reshape(block_count, q_block, HEADS, HDIM), shard_seq.reshape(block_count, q_block), shard_blk.reshape(block_count, q_block)))
        return result.reshape(TOK_DP, HEADS, HDIM)
    outcome = lax.map(one_shard, (queries.reshape(shard_count, TOK_DP, HEADS, HDIM), key_rows.reshape(shard_count, TOK_DP, HDIM), values.reshape(shard_count, TOK_DP, HDIM), seq_ids.reshape(shard_count, TOK_DP), block_ids.reshape(shard_count, TOK_DP)))
    return outcome.reshape(-1, HEADS * HDIM)

def reference(tokens, seq_ids, block_ids, positions, norm1_gain, norm2_gain, w_query, w_kv, w_out, w_gate, w_up, w_down, grad_output):

    def forward(tokens32, gain_one, gain_two, query_w, kv_w, out_w, gate_w, up_w, down_w):
        normed = low(tokens32 * rms_scale(tokens32) * gain_one)
        query_pre = low_back(matmul(normed, query_w))
        kv_pre = low_back(matmul(normed, kv_w))
        cosine, sine_part = rope_tables(positions, HDIM)
        queries = low(rotate(query_pre.reshape(-1, HEADS, HDIM), cosine[:, None, :], sine_part[:, None, :]))
        key_rows = low(rotate(kv_pre[:, :HDIM], cosine, sine_part))
        values = low(kv_pre[:, HDIM:])
        attended = low(low_back(attention(queries, key_rows, values, seq_ids, block_ids)))
        hidden = tokens32 + low_back(matmul(attended, out_w))
        normed_two = low(hidden * rms_scale(hidden) * gain_two)
        gate_proj = low_back(matmul(normed_two, gate_w))
        up_proj = low_back(matmul(normed_two, up_w))
        mixed_act = low(jax.nn.silu(gate_proj) * up_proj)
        return hidden + low_back(matmul(mixed_act, down_w))
    output, pullback = jax.vjp(forward, tokens.astype(jnp.float32), norm1_gain, norm2_gain, w_query.astype(jnp.float32), w_kv.astype(jnp.float32), w_out.astype(jnp.float32), w_gate.astype(jnp.float32), w_up.astype(jnp.float32), w_down.astype(jnp.float32))
    grads = pullback(grad_output)
    return (output, grads[0], grads[3].reshape(N_ROW, D // N_ROW, QW), grads[4].reshape(N_ROW, D // N_ROW, 2 * HDIM), grads[5].reshape(N_COL, QW // N_COL, D), grads[6].reshape(N_ROW, D // N_ROW, FF), grads[7].reshape(N_ROW, D // N_ROW, FF), grads[8].reshape(N_COL, FF // N_COL, D), grads[1].reshape(N_ROW, D // N_ROW), grads[2].reshape(N_ROW, D // N_ROW))
```

```python
import functools

import jax
import jax.numpy as jnp
from jax import lax
from jax.experimental import pallas as pl
from jax.experimental.pallas import tpu as pltpu
from jax.sharding import PartitionSpec as P

D = 2048
EPS = 1e-05
ROPE_BASE = 500000.0
BLOCK = 256
LOG2E = 1.4426950408889634
BF = jnp.bfloat16
F32 = jnp.float32
HEADS_PER_STEP = 2


def dot_nn(a, b):
    return lax.dot_general(a, b, (((1,), (0,)), ((), ())), preferred_element_type=F32)


def dot_nt(a, b):
    return lax.dot_general(a, b, (((1,), (1,)), ((), ())), preferred_element_type=F32)


def dot_tn(a, b):
    return lax.dot_general(a, b, (((0,), (0,)), ((), ())), preferred_element_type=F32)


def attend_body(meta, q_ref, cos_ref, sin_ref, k_ref, vt_ref, att_ref, rot_ref, lse_ref, *, factor, width):
    cosine = cos_ref[...]
    sine = sin_ref[...]
    rows = q_ref.shape[0]
    for head in range(HEADS_PER_STEP):
        cols = slice(head * width, (head + 1) * width)
        pre = q_ref[:, cols]
        rot = (pre * cosine + pltpu.roll(pre, width // 2, 1) * sine).astype(BF)
        rot_ref[:, cols] = rot

        def step(t, carry):
            top, total, acc = carry
            chunk = meta[2 + meta[0] + t]
            scores = dot_nt(k_ref[chunk], rot) * factor
            new_top = jnp.maximum(top, jnp.max(scores, axis=0, keepdims=True))
            decay = jnp.exp2(top - new_top)
            weights = jnp.exp2(scores - new_top)
            total = total * decay + jnp.sum(weights, axis=0, keepdims=True)
            acc = acc * decay + dot_nn(vt_ref[chunk], weights.astype(BF))
            return (new_top, total, acc)

        top, total, acc = lax.fori_loop(
            0,
            meta[1],
            step,
            (
                jnp.full((1, rows), -1e30, F32),
                jnp.zeros((1, rows), F32),
                jnp.zeros((width, rows), F32),
            ),
        )
        att_ref[:, cols] = (acc / total).T.astype(BF)
        lse_ref[head] = top + jnp.log2(total)


def attend(meta, q_pre, cosine, sine, keys, values_t, width):
    rows, columns = q_pre.shape
    heads = columns // width
    chunks = keys.shape[0]
    span = HEADS_PER_STEP * width
    whole2 = lambda i, m: (0, 0)
    whole3 = lambda i, m: (0, 0, 0)
    return pl.pallas_call(
        functools.partial(attend_body, factor=width**-0.5 * LOG2E, width=width),
        grid_spec=pltpu.PrefetchScalarGridSpec(
            num_scalar_prefetch=1,
            grid=(heads // HEADS_PER_STEP,),
            in_specs=[
                pl.BlockSpec((rows, span), lambda i, m: (0, i)),
                pl.BlockSpec((rows, width), whole2),
                pl.BlockSpec((rows, width), whole2),
                pl.BlockSpec((chunks, rows, width), whole3),
                pl.BlockSpec((chunks, width, rows), whole3),
            ],
            out_specs=[
                pl.BlockSpec((rows, span), lambda i, m: (0, i)),
                pl.BlockSpec((rows, span), lambda i, m: (0, i)),
                pl.BlockSpec((HEADS_PER_STEP, 1, rows), lambda i, m: (i, 0, 0)),
            ],
        ),
        out_shape=[
            jax.ShapeDtypeStruct((rows, columns), BF),
            jax.ShapeDtypeStruct((rows, columns), BF),
            jax.ShapeDtypeStruct((heads, 1, rows), F32),
        ],
        name="attend",
    )(meta, q_pre, cosine, sine, keys, values_t)


def attend_back_body(
    meta, rot_ref, grad_ref, att_ref, lse_ref, cos_ref, sin_ref, k_ref, kt_ref, v_ref,
    qpg_ref, dk_ref, dv_ref, *, factor, scale, width,
):
    @pl.when(pl.program_id(0) == 0)
    def _():
        dk_ref[...] = jnp.zeros_like(dk_ref)
        dv_ref[...] = jnp.zeros_like(dv_ref)

    cosine = cos_ref[...]
    sine = sin_ref[...]
    rows = rot_ref.shape[0]
    for head in range(HEADS_PER_STEP):
        cols = slice(head * width, (head + 1) * width)
        rot = rot_ref[:, cols]
        grad = grad_ref[:, cols]
        inner = (grad.astype(F32) * att_ref[:, cols].astype(F32)).T
        inner = jnp.sum(inner, axis=0, keepdims=True)
        lse = lse_ref[head]

        def step(t, dq):
            chunk = meta[2 + meta[0] + t]
            probs = jnp.exp2(dot_nt(k_ref[chunk], rot) * factor - lse)
            back = dot_nt(v_ref[chunk], grad)
            score_grad = (probs * (back - inner)).astype(BF)
            dv_ref[chunk] += dot_nn(probs.astype(BF), grad)
            dk_ref[chunk] += dot_nn(score_grad, rot)
            return dq + dot_nn(kt_ref[chunk], score_grad)

        dq = lax.fori_loop(0, meta[1], step, jnp.zeros((width, rows), F32)).T * scale
        qpg_ref[:, cols] = (dq * cosine - pltpu.roll(dq, width // 2, 1) * sine).astype(BF)


def attend_back(meta, rot, grad, att, lse, cosine, sine, keys, keys_t, values, width):
    rows, columns = rot.shape
    heads = columns // width
    chunks = keys.shape[0]
    span = HEADS_PER_STEP * width
    whole2 = lambda i, m: (0, 0)
    whole3 = lambda i, m: (0, 0, 0)
    by_head = lambda i, m: (0, i)
    return pl.pallas_call(
        functools.partial(
            attend_back_body, factor=width**-0.5 * LOG2E, scale=width**-0.5, width=width
        ),
        grid_spec=pltpu.PrefetchScalarGridSpec(
            num_scalar_prefetch=1,
            grid=(heads // HEADS_PER_STEP,),
            in_specs=[
                pl.BlockSpec((rows, span), by_head),
                pl.BlockSpec((rows, span), by_head),
                pl.BlockSpec((rows, span), by_head),
                pl.BlockSpec((HEADS_PER_STEP, 1, rows), lambda i, m: (i, 0, 0)),
                pl.BlockSpec((rows, width), whole2),
                pl.BlockSpec((rows, width), whole2),
                pl.BlockSpec((chunks, rows, width), whole3),
                pl.BlockSpec((chunks, width, rows), whole3),
                pl.BlockSpec((chunks, rows, width), whole3),
            ],
            out_specs=[
                pl.BlockSpec((rows, span), by_head),
                pl.BlockSpec((chunks, rows, width), whole3),
                pl.BlockSpec((chunks, rows, width), whole3),
            ],
        ),
        out_shape=[
            jax.ShapeDtypeStruct((rows, columns), BF),
            jax.ShapeDtypeStruct((chunks, rows, width), F32),
            jax.ShapeDtypeStruct((chunks, rows, width), F32),
        ],
        name="attend_back",
    )(meta, rot, grad, att, lse, cosine, sine, keys, keys_t, values)


def per_device(
    rows_n,
    tokens,
    seq_ids,
    block_ids,
    positions,
    norm1_gain,
    norm2_gain,
    w_query,
    w_kv,
    w_out,
    w_gate,
    w_up,
    w_down,
    grad_output,
):
    R = rows_n
    bits = []
    while (1 << len(bits)) < R:
        bits.append(1 << len(bits))
    nbits = len(bits)

    def reverse(v):
        out = 0
        for b in range(nbits):
            out = out | (((v >> b) & 1) << (nbits - 1 - b))
        return out

    order = [reverse(v) for v in range(R)]
    row = lax.axis_index("row")
    col = lax.axis_index("col")
    half_rows, dslice = tokens.shape
    B = half_rows // R
    full_rows = 2 * half_rows
    width = w_kv.shape[1] // 2
    dp_n = lax.axis_size("dp")

    def swap_row(a, bit):
        return lax.ppermute(a, "row", [(i, i ^ bit) for i in range(R)])

    def swap_col(a):
        return lax.ppermute(a, "col", [(0, 1), (1, 0)])

    def psum_row(a):
        for bit in bits:
            a = a + swap_row(a, bit)
        return a

    def pick(a, index, size):
        return lax.dynamic_slice_in_dim(a, index * size, size, 0)

    def to_order(a):
        return jnp.concatenate([pick(a, row ^ order[p], B) for p in range(R)], axis=0)

    def from_order(a):
        return jnp.concatenate([pick(a, reverse(row ^ b), B) for b in range(R)], axis=0)

    def reduce_row(a):
        a = a.astype(BF)
        for bit in bits:
            half = a.shape[0] // 2
            total = a[:half].astype(F32) + swap_row(a[half:], bit).astype(F32)
            a = total.astype(BF)
        return total

    def gather_row(a):
        for bit in reversed(bits):
            a = jnp.concatenate([a, swap_row(a, bit)], axis=0)
        return a

    def spread(pieces, bit):
        out = dict(pieces)
        for (a, k), value in pieces.items():
            out[(a, k ^ bit)] = swap_row(value, bit)
        return out

    def spread_col(pieces):
        out = dict(pieces)
        for (a, k), value in pieces.items():
            out[(1 - a, k)] = swap_col(value)
        return out

    def gather_plane(mine):
        half = half_rows // 2
        first = spread_col({(0, 0): mine[:half]})
        for bit in reversed(bits[1:]):
            first = spread(first, bit)
        second = {(0, 0): mine[half:]}
        for bit in reversed(bits[1:]):
            second = spread(second, bit)
        second = spread_col(second)
        first = spread(first, 1)
        second = spread(second, 1)
        rows_out = []
        for a in range(2):
            for part in (first, second):
                rows_out.append(jnp.concatenate([part[(a, k)] for k in range(R)], axis=1))
        return jnp.concatenate(rows_out, axis=0)

    def add(a, b):
        return (a.astype(F32) + b.astype(F32)).astype(BF)

    def reduce_plane(blocks):
        keep = {k: add(blocks[k], swap_row(blocks[k ^ 1], 1)) for k in range(0, R, 2)}
        half = half_rows // 2
        outs = []
        for part in range(2):
            cur = {
                (a, k): v[a * half_rows + part * half : a * half_rows + (part + 1) * half]
                for k, v in keep.items()
                for a in range(2)
            }

            def by_col(cur):
                return {
                    (0, k): add(cur[(0, k)], swap_col(cur[(1, k)])) for (a, k) in cur if a == 0
                }

            def by_rows(cur):
                for bit in bits[1:]:
                    cur = {
                        (a, k): add(v, swap_row(cur[(a, k ^ bit)], bit))
                        for (a, k), v in cur.items()
                        if not k & bit
                    }
                return cur

            cur = by_rows(by_col(cur)) if part == 0 else by_col(by_rows(cur))
            outs.append(cur[(0, 0)])
        return jnp.concatenate(outs, axis=0).astype(F32)

    def split_ff(w, axis):
        size = w.shape[axis] // R
        return [
            lax.dynamic_slice_in_dim(w, (row ^ k) * size, size, axis) for k in range(R)
        ]

    def exchange(parts):
        return [parts[0]] + [swap_row(parts[k], k) for k in range(1, R)]

    residual = tokens.astype(F32)
    scale_one = lax.rsqrt(psum_row(jnp.sum(residual * residual, axis=1)) / D + EPS)
    weighted_in = (residual * norm1_gain[None, :]).astype(BF)
    ordered_in = to_order(weighted_in)
    w_query_far = swap_col(w_query)
    own = col * R + row
    own_scale = lax.dynamic_slice_in_dim(scale_one, row * B, B)[:, None]

    kv_pre = reduce_row(dot_nn(ordered_in, w_kv)) * own_scale
    query_near = reduce_row(dot_nn(ordered_in, w_query))
    query_far = reduce_row(dot_nn(ordered_in, w_query_far))
    query_pre = jnp.concatenate([query_near, query_far], axis=1) * own_scale

    half_width = width // 2
    frequency = ROPE_BASE ** (-2.0 * jnp.arange(half_width, dtype=F32) / width)
    own_positions = lax.dynamic_slice_in_dim(positions, own * B, B)
    angles = own_positions.astype(F32)[:, None] * frequency[None, :]
    cosine = jnp.concatenate([jnp.cos(angles)] * 2, axis=1)
    sine_half = jnp.sin(angles)
    sine = jnp.concatenate([-sine_half, sine_half], axis=1)

    key_pre = kv_pre[:, :width]
    key_turned = jnp.concatenate([key_pre[:, half_width:], key_pre[:, :half_width]], axis=1)
    key_own = key_pre * cosine + key_turned * sine
    kv_own = jnp.concatenate([key_own, kv_pre[:, width:]], axis=1).astype(BF)
    kv_pieces = spread_col({(0, 0): kv_own})
    for bit in reversed(bits):
        kv_pieces = spread(kv_pieces, bit)
    kv_all = jnp.stack([kv_pieces[(a, k)] for a in range(2) for k in range(R)])
    keys = kv_all[:, :, :width]
    values = kv_all[:, :, width:]
    keys_t = keys.transpose(0, 2, 1)
    values_t = values.transpose(0, 2, 1)

    chunks = 2 * R
    chunk_seq = seq_ids[::B]
    chunk_block = block_ids[::B]
    numbers = jnp.arange(chunks, dtype=jnp.int32)
    my_seq = lax.dynamic_slice_in_dim(chunk_seq, own, 1)
    my_block = lax.dynamic_slice_in_dim(chunk_block, own, 1)
    visible = (chunk_seq == my_seq) & (chunk_block <= my_block)
    first_chunk = jnp.min(jnp.where(visible, numbers, chunks))
    count = jnp.sum(visible.astype(jnp.int32))
    place = ((numbers // R) ^ col) * R + ((numbers % R) ^ row)
    meta = jnp.concatenate([first_chunk[None], count[None], place]).astype(jnp.int32)

    att_own, rot_own, lse = attend(meta, query_pre, cosine, sine, keys, values_t, width)

    w_out_far = swap_col(w_out)
    w_out_all = jnp.concatenate([w_out, w_out_far], axis=0)
    w_query_all = jnp.concatenate([w_query, w_query_far], axis=1)
    att_all = gather_row(att_own)
    hidden = residual + from_order(dot_nn(att_all, w_out_all))

    down_grad = grad_output.astype(BF)
    grad_full = gather_plane(down_grad)
    gate_parts = exchange(split_ff(w_gate, 1))
    up_parts = exchange(split_ff(w_up, 1))
    down_parts = exchange(split_ff(w_down, 0))
    gate_full = jnp.concatenate(gate_parts, axis=0)
    up_full = jnp.concatenate(up_parts, axis=0)
    down_full = jnp.concatenate(down_parts, axis=1)

    scale_two = lax.rsqrt(psum_row(jnp.sum(hidden * hidden, axis=1)) / D + EPS)[:, None]
    normed_two = (hidden * scale_two * norm2_gain[None, :]).astype(BF)
    normed_full = gather_plane(normed_two)

    mixed_grad = dot_nt(grad_full, down_full)
    gate_proj = dot_nn(normed_full, gate_full)
    up_proj = dot_nn(normed_full, up_full)
    sigmoid_gate = jax.nn.sigmoid(gate_proj)
    silu_gate = gate_proj * sigmoid_gate
    mixed_act = (silu_gate * up_proj).astype(BF)
    gate_grad = (
        mixed_grad * up_proj * sigmoid_gate * (1.0 + gate_proj * (1.0 - sigmoid_gate))
    ).astype(BF)
    up_grad = (mixed_grad * silu_gate).astype(BF)

    normed2_grad = reduce_plane(
        [
            (dot_nt(gate_grad, gate_parts[k]) + dot_nt(up_grad, up_parts[k])).astype(BF)
            for k in range(R)
        ]
    )

    def ff_input_grad(grad):
        local = dot_tn(normed_full, grad).astype(BF)
        quarter = dslice // dp_n
        local = local.reshape(R, dp_n, quarter, grad.shape[1]).transpose(1, 0, 2, 3)
        return lax.psum_scatter(local, "dp", scatter_dimension=0, tiled=True)[0]

    def ff_input_place(piece):
        moved = jnp.stack(exchange([piece[k] for k in range(R)]))
        ordered = jnp.concatenate(
            [lax.dynamic_index_in_dim(moved, row ^ s, 0, keepdims=False) for s in range(R)], axis=1
        )
        return ordered.astype(F32)[None]

    gate_piece = ff_input_grad(gate_grad)
    up_piece = ff_input_grad(up_grad)
    down_local = [
        dot_tn(mixed_act, grad_full[:, k * dslice : (k + 1) * dslice]).astype(BF) for k in range(R)
    ]
    down_moved = jnp.stack(exchange(down_local))
    down_ordered = jnp.concatenate(
        [lax.dynamic_index_in_dim(down_moved, row ^ s, 0, keepdims=False) for s in range(R)], axis=0
    )
    grad_down = lax.psum_scatter(down_ordered, "dp", scatter_dimension=0, tiled=True)

    output = hidden + reduce_plane([dot_nn(mixed_act, down_parts[k]).astype(BF) for k in range(R)])

    weighted = normed2_grad * norm2_gain[None, :]
    inner_two = psum_row(jnp.sum(weighted * hidden, axis=1))[:, None]
    hidden_grad = grad_output + (
        scale_two * weighted - hidden * (scale_two * scale_two * scale_two) * inner_two / D
    )
    gain_two = jnp.sum(normed2_grad * hidden * scale_two, axis=0)
    branch_ordered = to_order(hidden_grad.astype(BF))
    att_grad = jnp.concatenate(
        [
            reduce_row(dot_nt(branch_ordered, w_out)),
            reduce_row(dot_nt(branch_ordered, w_out_far)),
        ],
        axis=1,
    ).astype(BF)
    columns = w_query.shape[1]

    def over_col(far, near):
        return add(near, swap_col(far.astype(BF)))

    grad_out_local = over_col(
        dot_tn(att_all[:, columns:], branch_ordered), dot_tn(att_all[:, :columns], branch_ordered)
    )
    grad_out = lax.psum_scatter(grad_out_local, "dp", scatter_dimension=0, tiled=True)

    qpg_own, dk, dv = attend_back(
        meta, rot_own, att_grad, att_own, lse, cosine, sine, keys, keys_t, values, width
    )
    dkv = jnp.concatenate([dk * width**-0.5, dv], axis=2).astype(BF)
    cur = {(a, k): dkv[a * R + k] for a in range(2) for k in range(R)}
    for bit in bits:
        cur = {
            (a, k): add(v, swap_row(cur[(a, k ^ bit)], bit))
            for (a, k), v in cur.items()
            if not k & bit
        }
    dkv_own = cur[(0, 0)].astype(F32) + swap_col(cur[(1, 0)]).astype(F32)
    dk_own = dkv_own[:, :width]
    dk_turned = jnp.concatenate([dk_own[:, half_width:], dk_own[:, :half_width]], axis=1)
    kvg_own = jnp.concatenate(
        [dk_own * cosine - dk_turned * sine, dkv_own[:, width:]], axis=1
    ).astype(BF)

    qpg_all = gather_row(qpg_own)
    kvg_all = gather_row(kvg_own)
    normed1_grad = from_order(dot_nt(qpg_all, w_query_all) + dot_nt(kvg_all, w_kv))
    weighted_one = normed1_grad * norm1_gain[None, :]
    inner_one = psum_row(jnp.sum(weighted_one * residual, axis=1))[:, None]
    scale_col = scale_one[:, None]
    input_grad = hidden_grad + (
        scale_col * weighted_one - residual * (scale_col * scale_col * scale_col) * inner_one / D
    )
    gain_one = jnp.sum(normed1_grad * residual * scale_col, axis=0)

    normed_ordered = to_order((residual * scale_col * norm1_gain[None, :]).astype(BF))
    grad_query_local = over_col(
        dot_tn(normed_ordered, qpg_all[:, columns:]), dot_tn(normed_ordered, qpg_all[:, :columns])
    )
    grad_query = lax.psum_scatter(grad_query_local, "dp", scatter_dimension=0, tiled=True)
    grad_kv = lax.psum_scatter(
        dot_tn(normed_ordered, kvg_all).astype(BF),
        ("dp", "col"),
        scatter_dimension=0,
        tiled=True,
    )
    gains = lax.psum_scatter(
        jnp.stack([gain_one, gain_two], axis=1).astype(BF),
        ("dp", "col"),
        scatter_dimension=0,
        tiled=True,
    ).astype(F32)
    return (
        output,
        input_grad,
        grad_query.astype(F32)[None],
        grad_kv.astype(F32)[None],
        grad_out.astype(F32)[None],
        ff_input_place(gate_piece),
        ff_input_place(up_piece),
        grad_down.astype(F32)[None],
        gains[:, 0][None, :],
        gains[:, 1][None, :],
    )


def solution(mesh):
    placed = (
        P(("dp", "col"), "row"),
        P("dp"),
        P("dp"),
        P("dp"),
        P("row"),
        P("row"),
        P("row", "col"),
        P("row", None),
        P("col", "row"),
        P("row", "col"),
        P("row", "col"),
        P("col", "row"),
        P(("dp", "col"), "row"),
    )
    return jax.shard_map(
        functools.partial(per_device, mesh.shape["row"]),
        mesh=mesh,
        in_specs=placed,
        out_specs=(
            P(("dp", "col"), "row"),
            P(("dp", "col"), "row"),
            P("row", "dp", "col"),
            P("row", ("dp", "col"), None),
            P("col", "dp", "row"),
            P("row", "dp", "col"),
            P("row", "dp", "col"),
            P("col", "dp", "row"),
            P("row", ("dp", "col")),
            P("row", ("dp", "col")),
        ),
        check_vma=False,
    )
```

```python
import functools

import jax
import jax.numpy as jnp
from jax import lax
from jax.experimental import pallas as pl
from jax.experimental.pallas import tpu as pltpu
from jax.sharding import PartitionSpec as P

D = 2048
EPS = 1e-05
ROPE_BASE = 500000.0
BLOCK = 256
LOG2E = 1.4426950408889634
BF = jnp.bfloat16
F32 = jnp.float32
HEADS_PER_STEP = 4


def dot_nn(a, b):
    return lax.dot_general(a, b, (((1,), (0,)), ((), ())), preferred_element_type=F32)


def dot_nt(a, b):
    return lax.dot_general(a, b, (((1,), (1,)), ((), ())), preferred_element_type=F32)


def dot_tn(a, b):
    return lax.dot_general(a, b, (((0,), (0,)), ((), ())), preferred_element_type=F32)


def list_visible(where, seq_ref, block_ref, list_ref, *, rows_n, rows):
    row, col = where[0], where[1]
    chunks = 2 * rows_n
    own = (col * rows_n + row) * rows
    count = jnp.int32(0)
    for j in range(chunks):
        seen = (seq_ref[j * rows] == seq_ref[own]) & (block_ref[j * rows] <= block_ref[own])

        @pl.when(seen)
        def _(j=j, count=count):
            list_ref[count] = ((j // rows_n) ^ col) * rows_n + ((j % rows_n) ^ row)

        count = count + seen.astype(jnp.int32)
    list_ref[chunks] = count


def attend_body(
    where, seq_ref, block_ref, q_ref, cos_ref, sin_ref, k_ref, vt_ref,
    att_ref, rot_ref, lse_ref, list_ref, *, factor, width, rows_n,
):
    @pl.when(pl.program_id(0) == 0)
    def _():
        list_visible(where, seq_ref, block_ref, list_ref, rows_n=rows_n, rows=q_ref.shape[0])

    cosine = cos_ref[...]
    sine = sin_ref[...]
    rows = q_ref.shape[0]
    heads = [slice(h * width, (h + 1) * width) for h in range(HEADS_PER_STEP)]
    for cols in heads:
        pre = q_ref[:, cols]
        rot_ref[:, cols] = (pre * cosine + pltpu.roll(pre, width // 2, 1) * sine).astype(BF)

    def step(t, carry):
        chunk = list_ref[t]
        key = k_ref[chunk]
        value_t = vt_ref[chunk]
        all_scores = [dot_nt(key, rot_ref[:, cols]) * factor for cols in heads]
        out = []
        for (top, total, acc), scores in zip(carry, all_scores):
            new_top = jnp.maximum(top, jnp.max(scores, axis=0, keepdims=True))
            decay = jnp.exp2(top - new_top)
            weights = jnp.exp2(scores - new_top)
            total = total * decay + jnp.sum(weights, axis=0, keepdims=True)
            acc = acc * decay + dot_nn(value_t, weights.astype(BF))
            out.append((new_top, total, acc))
        return out

    start = (
        jnp.full((1, rows), -1e30, F32),
        jnp.zeros((1, rows), F32),
        jnp.zeros((width, rows), F32),
    )
    done = lax.fori_loop(0, list_ref[2 * rows_n], step, [start] * HEADS_PER_STEP)
    for head, (top, total, acc) in enumerate(done):
        att_ref[:, heads[head]] = (acc / total).T.astype(BF)
        lse_ref[head] = top + jnp.log2(total)


def attend(meta, q_pre, cosine, sine, keys, values_t, width, rows_n):
    where, seq_ids, block_ids = meta
    rows, columns = q_pre.shape
    heads = columns // width
    chunks = keys.shape[0]
    span = HEADS_PER_STEP * width
    whole2 = lambda i, m: (0, 0)
    whole3 = lambda i, m: (0, 0, 0)
    return pl.pallas_call(
        functools.partial(attend_body, factor=width**-0.5 * LOG2E, width=width, rows_n=rows_n),
        grid_spec=pltpu.PrefetchScalarGridSpec(
            num_scalar_prefetch=1,
            grid=(heads // HEADS_PER_STEP,),
            in_specs=[
                pl.BlockSpec(memory_space=pltpu.SMEM),
                pl.BlockSpec(memory_space=pltpu.SMEM),
                pl.BlockSpec((rows, span), lambda i, m: (0, i)),
                pl.BlockSpec((rows, width), whole2),
                pl.BlockSpec((rows, width), whole2),
                pl.BlockSpec((chunks, rows, width), whole3),
                pl.BlockSpec((chunks, width, rows), whole3),
            ],
            out_specs=[
                pl.BlockSpec((rows, span), lambda i, m: (0, i)),
                pl.BlockSpec((rows, span), lambda i, m: (0, i)),
                pl.BlockSpec((HEADS_PER_STEP, 1, rows), lambda i, m: (i, 0, 0)),
            ],
            scratch_shapes=[pltpu.SMEM((chunks + 1,), jnp.int32)],
        ),
        out_shape=[
            jax.ShapeDtypeStruct((rows, columns), BF),
            jax.ShapeDtypeStruct((rows, columns), BF),
            jax.ShapeDtypeStruct((heads, 1, rows), F32),
        ],
        cost_estimate=pl.CostEstimate(
            flops=4 * rows * columns * chunks * rows // 2,
            transcendentals=heads * rows * chunks * rows // 2,
            bytes_accessed=8 * rows * columns + 4 * chunks * rows * width,
        ),
        name="attend",
    )(where, seq_ids, block_ids, q_pre, cosine, sine, keys, values_t)


def attend_back_body(
    where, seq_ref, block_ref, rot_ref, grad_ref, att_ref, lse_ref, cos_ref, sin_ref, k_ref, kt_ref, v_ref,
    *outs, factor, scale, width, rows_n,
):
    qpg_ref, dk_ref, dv_ref, list_ref = outs[-4:]

    @pl.when(pl.program_id(0) == 0)
    def _():
        list_visible(where, seq_ref, block_ref, list_ref, rows_n=rows_n, rows=rot_ref.shape[0])
        dk_ref[...] = jnp.zeros_like(dk_ref) if len(outs) == 4 else outs[0][...]
        dv_ref[...] = jnp.zeros_like(dv_ref) if len(outs) == 4 else outs[1][...]

    cosine = cos_ref[...]
    sine = sin_ref[...]
    rows = rot_ref.shape[0]
    heads = [slice(h * width, (h + 1) * width) for h in range(HEADS_PER_STEP)]
    inners = []
    for cols in heads:
        inner = (grad_ref[:, cols].astype(F32) * att_ref[:, cols].astype(F32)).T
        inners.append(jnp.sum(inner, axis=0, keepdims=True))

    def step(t, dqs):
        chunk = list_ref[t]
        key = k_ref[chunk]
        key_t = kt_ref[chunk]
        value = v_ref[chunk]
        all_scores = [dot_nt(key, rot_ref[:, cols]) for cols in heads]
        backs = [dot_nt(value, grad_ref[:, cols]) for cols in heads]
        dv = dv_ref[chunk]
        dk = dk_ref[chunk]
        out = []
        for h, cols in enumerate(heads):
            probs = jnp.exp2(all_scores[h] * factor - lse_ref[h])
            score_grad = (probs * (backs[h] - inners[h])).astype(BF)
            dv = dv + dot_nn(probs.astype(BF), grad_ref[:, cols])
            dk = dk + dot_nn(score_grad, rot_ref[:, cols])
            out.append(dqs[h] + dot_nn(key_t, score_grad))
        dv_ref[chunk] = dv
        dk_ref[chunk] = dk
        return out

    dqs = lax.fori_loop(0, list_ref[2 * rows_n], step, [jnp.zeros((width, rows), F32)] * HEADS_PER_STEP)
    for h, cols in enumerate(heads):
        dq = dqs[h].T * scale
        qpg_ref[:, cols] = (dq * cosine - pltpu.roll(dq, width // 2, 1) * sine).astype(BF)


def attend_back(meta, rot, grad, att, lse, cosine, sine, keys, keys_t, values, width, rows_n, running=()):
    where, seq_ids, block_ids = meta
    rows, columns = rot.shape
    heads = columns // width
    chunks = keys.shape[0]
    span = HEADS_PER_STEP * width
    whole2 = lambda i, m: (0, 0)
    whole3 = lambda i, m: (0, 0, 0)
    by_head = lambda i, m: (0, i)
    return pl.pallas_call(
        functools.partial(
            attend_back_body,
            factor=width**-0.5 * LOG2E,
            scale=width**-0.5,
            width=width,
            rows_n=rows_n,
        ),
        grid_spec=pltpu.PrefetchScalarGridSpec(
            num_scalar_prefetch=1,
            grid=(heads // HEADS_PER_STEP,),
            in_specs=[
                pl.BlockSpec(memory_space=pltpu.SMEM),
                pl.BlockSpec(memory_space=pltpu.SMEM),
                pl.BlockSpec((rows, span), by_head),
                pl.BlockSpec((rows, span), by_head),
                pl.BlockSpec((rows, span), by_head),
                pl.BlockSpec((HEADS_PER_STEP, 1, rows), lambda i, m: (i, 0, 0)),
                pl.BlockSpec((rows, width), whole2),
                pl.BlockSpec((rows, width), whole2),
                pl.BlockSpec((chunks, rows, width), whole3),
                pl.BlockSpec((chunks, width, rows), whole3),
                pl.BlockSpec((chunks, rows, width), whole3),
            ]
            + [pl.BlockSpec((chunks, rows, width), whole3)] * len(running),
            out_specs=[
                pl.BlockSpec((rows, span), by_head),
                pl.BlockSpec((chunks, rows, width), whole3),
                pl.BlockSpec((chunks, rows, width), whole3),
            ],
            scratch_shapes=[pltpu.SMEM((chunks + 1,), jnp.int32)],
        ),
        out_shape=[
            jax.ShapeDtypeStruct((rows, columns), BF),
            jax.ShapeDtypeStruct((chunks, rows, width), F32),
            jax.ShapeDtypeStruct((chunks, rows, width), F32),
        ],
        cost_estimate=pl.CostEstimate(
            flops=10 * rows * columns * chunks * rows // 2,
            transcendentals=heads * rows * chunks * rows // 2,
            bytes_accessed=8 * rows * columns + 12 * chunks * rows * width,
        ),
        name="attend_back",
    )(where, seq_ids, block_ids, rot, grad, att, lse, cosine, sine, keys, keys_t, values, *running)


def feed_body(*refs, rows_n, parts, near, shared):
    R = rows_n
    refs = list(refs)
    take = lambda n: [refs.pop(0) for _ in range(n)]
    normed = take(parts * R)
    grads = take(R)
    close_in, close_down = take(near), take(near)
    far_in = take(1 if shared[0] else R - near)
    far_down = take(1 if shared[1] else R - near)
    act_ref, gate_grad_ref, up_grad_ref = take(3)
    back_refs = take(R)
    normed_out, grads_out = take(2)
    x_ref, g_ref, wg_ref, wu_ref, wd_ref, x_sem, g_sem, w_sem, o_sem = refs
    step = pl.program_id(0)
    tile, span = normed[0].shape

    def x_copy(p, k):
        return pltpu.make_async_copy(
            normed[p * R + k], x_ref.at[p, :, pl.ds(k * span, span)], x_sem.at[p, k]
        )

    def g_copy(p, k):
        return pltpu.make_async_copy(
            grads[k].at[pl.ds(p * tile, tile)], g_ref.at[p, :, pl.ds(k * span, span)], g_sem.at[p, k]
        )

    def w_copies(j, k):
        target = (wg_ref, wu_ref, wd_ref)[j].at[k]
        if k < near or not shared[j // 2]:
            whole = (close_in + far_in, close_down + far_down)[j // 2][k]
            whole = whole if j == 2 else whole.at[j]
            return [pltpu.make_async_copy(whole, target, w_sem.at[j, k, 0])]
        source = far_down[0] if j == 2 else far_in[0]
        copies = []
        for z in range(source.shape[0]):
            if j == 2:
                size = source.shape[-2]
                share, place = source.at[z, k - near], target.at[pl.ds(z * size, size)]
            else:
                size = source.shape[-1]
                share, place = source.at[z, k - near, j], target.at[:, pl.ds(z * size, size)]
            copies.append(pltpu.make_async_copy(share, place, w_sem.at[j, k, z]))
        return copies

    def x_out(p):
        return pltpu.make_async_copy(
            x_ref.at[p], normed_out.at[pl.ds(p * tile, tile)], o_sem.at[0, p]
        )

    def g_out(p):
        return pltpu.make_async_copy(
            g_ref.at[p], grads_out.at[pl.ds(p * tile, tile)], o_sem.at[1, p]
        )

    @pl.when(step == 0)
    def _():
        weights = [w_copies(j, k) for j in range(3) for k in range(R)]
        for k in range(R):
            x_copy(0, k).start()
            g_copy(0, k).start()
        for group in weights:
            for copy in group:
                copy.start()
        for p in range(1, parts):
            for k in range(R):
                x_copy(p, k).start()
                g_copy(p, k).start()
        for k in range(R):
            x_copy(0, k).wait()
            g_copy(0, k).wait()
        for group in weights:
            for copy in group:
                copy.wait()
        x_out(0).start()
        g_out(0).start()

    for p in range(1, parts):

        @pl.when(step == p)
        def _(p=p):
            for k in range(R):
                x_copy(p, k).wait()
                g_copy(p, k).wait()
            x_out(p).start()
            g_out(p).start()

    def over_parts(left, right, dot):
        total = None
        for k in range(R):
            value = dot(left[step, :, pl.ds(k * span, span)], right[k])
            total = value if total is None else total + value
        return total

    gate = over_parts(x_ref, wg_ref, dot_nt)
    up = over_parts(x_ref, wu_ref, dot_nt)
    mixed_grad = over_parts(g_ref, wd_ref, dot_nt)
    sig = 1.0 / (1.0 + jnp.exp(-gate))
    silu = gate * sig
    act_ref[...] = (silu * up).astype(BF)
    gate_grad = (mixed_grad * up * sig * (1.0 + gate * (1.0 - sig))).astype(BF)
    up_grad = (mixed_grad * silu).astype(BF)
    gate_grad_ref[...] = gate_grad
    up_grad_ref[...] = up_grad
    for k in range(R):
        back_refs[k][...] = (dot_nn(gate_grad, wg_ref[k]) + dot_nn(up_grad, wu_ref[k])).astype(BF)

    @pl.when(step == parts - 1)
    def _():
        for p in range(parts):
            x_out(p).wait()
            g_out(p).wait()


def feed(normed, grads, close_in, close_down, far_in, far_down, shared, slots):
    parts = len(normed)
    R = len(grads)
    near = len(close_in)
    tile, span = normed[0][0].shape
    hidden_n = close_in[0].shape[1]
    total = parts * tile
    operands = [a for p in normed for a in p] + list(grads)
    operands += [*close_in, *close_down, *far_in, *far_down]
    by_tile = pl.BlockSpec((tile, hidden_n), lambda i: (i, 0))
    anywhere = pl.BlockSpec(memory_space=pl.ANY)
    return pl.pallas_call(
        functools.partial(feed_body, rows_n=R, parts=parts, near=near, shared=shared),
        grid=(parts,),
        in_specs=[anywhere] * len(operands),
        out_specs=[by_tile] * 3
        + [pl.BlockSpec((tile, span), lambda i: (i, 0))] * R
        + [anywhere] * 2,
        out_shape=[jax.ShapeDtypeStruct((total, hidden_n), BF)] * 3
        + [jax.ShapeDtypeStruct((total, span), BF)] * R
        + [jax.ShapeDtypeStruct((total, R * span), BF)] * 2,
        scratch_shapes=[
            pltpu.VMEM((parts, tile, R * span), BF),
            pltpu.VMEM((parts, tile, R * span), BF),
            pltpu.VMEM((R, hidden_n, span), BF),
            pltpu.VMEM((R, hidden_n, span), BF),
            pltpu.VMEM((R, hidden_n, span), BF),
            pltpu.SemaphoreType.DMA((parts, R)),
            pltpu.SemaphoreType.DMA((parts, R)),
            pltpu.SemaphoreType.DMA((3, R, slots)),
            pltpu.SemaphoreType.DMA((2, parts)),
        ],
        compiler_params=pltpu.CompilerParams(vmem_limit_bytes=56 << 20),
        cost_estimate=pl.CostEstimate(
            flops=10 * total * R * span * hidden_n,
            transcendentals=total * hidden_n,
            bytes_accessed=10 * total * R * span + 6 * R * span * hidden_n,
        ),
        name="feed",
    )(*operands)


def feed_weight_body(x0, x1, g0, g1, out_ref):
    total = (dot_tn(g0[...], x0[...]) + dot_tn(g1[...], x1[...])).astype(BF)
    share = out_ref.shape[3]
    for q in range(out_ref.shape[0]):
        out_ref[q, 0] = total[:, q * share : (q + 1) * share]


def feed_weight_grad(x, grads, rows_n, dp_n):
    tokens, features = x[0].shape
    span = features // rows_n
    hidden_n = grads[0].shape[1]
    return pl.pallas_call(
        feed_weight_body,
        grid=(rows_n,),
        in_specs=[pl.BlockSpec((tokens, span), lambda k: (0, k))] * 2
        + [pl.BlockSpec((tokens, hidden_n), lambda k: (0, 0))] * 2,
        out_specs=pl.BlockSpec((dp_n, 1, hidden_n, span // dp_n), lambda k: (0, k, 0, 0)),
        out_shape=jax.ShapeDtypeStruct((dp_n, rows_n, hidden_n, span // dp_n), BF),
        compiler_params=pltpu.CompilerParams(vmem_limit_bytes=48 << 20),
        cost_estimate=pl.CostEstimate(
            flops=4 * tokens * features * hidden_n,
            transcendentals=0,
            bytes_accessed=4 * tokens * (features + hidden_n) + 2 * features * hidden_n,
        ),
        name="feed_weights",
    )(*x, *grads)


def down_weight_body(a0, a1, g0, g1, *outs):
    total = (dot_tn(a0[...], g0[...]) + dot_tn(a1[...], g1[...])).astype(BF)
    for k, out in enumerate(outs):

        @pl.when(pl.program_id(0) == k)
        def _(out=out):
            out[...] = total


def down_weight_grad(acts, grads, rows_n):
    tokens, features = grads[0].shape
    span = features // rows_n
    hidden_n = acts[0].shape[1]
    return pl.pallas_call(
        down_weight_body,
        grid=(rows_n,),
        in_specs=[pl.BlockSpec((tokens, hidden_n), lambda k: (0, 0))] * 2
        + [pl.BlockSpec((tokens, span), lambda k: (0, k))] * 2,
        out_specs=[pl.BlockSpec((hidden_n, span), lambda k: (0, 0))] * rows_n,
        out_shape=[jax.ShapeDtypeStruct((hidden_n, span), BF)] * rows_n,
        compiler_params=pltpu.CompilerParams(vmem_limit_bytes=48 << 20),
        cost_estimate=pl.CostEstimate(
            flops=4 * tokens * features * hidden_n,
            transcendentals=0,
            bytes_accessed=4 * tokens * (features + hidden_n) + 2 * features * hidden_n,
        ),
        name="down_weights",
    )(*acts, *grads)


def cut_body(where, *refs, ks, rows_n):
    gate, up = refs[:2]
    down_in = refs[2 : 2 + len(ks)]
    outs = refs[2 + len(ks) :]
    hidden_n = gate.shape[1] // rows_n
    for n, k in enumerate(ks):
        slot = where[0] ^ k
        for i in range(rows_n):

            @pl.when(slot == i)
            def _(n=n, i=i):
                here = slice(i * hidden_n, (i + 1) * hidden_n)
                outs[2 * n][0] = gate[:, here].T
                outs[2 * n][1] = up[:, here].T

        outs[2 * n + 1][...] = down_in[n][...]


def cut_weights(where, w_gate, w_up, w_down, ks, rows_n, rows_in, rows_down):
    hidden_n = w_gate.shape[1] // rows_n
    span = w_down.shape[1]
    per = hidden_n // rows_down
    ins = [pl.BlockSpec((rows_in, w_gate.shape[1]), lambda i, w: (w[1], 0))] * 2
    for k in ks:
        ins.append(pl.BlockSpec((rows_down, span), lambda i, w, k=k: ((w[0] ^ k) * per + w[2], 0)))
    out_specs, out_shape = [], []
    for _ in ks:
        out_specs += [
            pl.BlockSpec((2, hidden_n, rows_in), lambda i, w: (0, 0, 0)),
            pl.BlockSpec((rows_down, span), lambda i, w: (0, 0)),
        ]
        out_shape += [
            jax.ShapeDtypeStruct((2, hidden_n, rows_in), BF),
            jax.ShapeDtypeStruct((rows_down, span), BF),
        ]
    out = pl.pallas_call(
        functools.partial(cut_body, ks=ks, rows_n=rows_n),
        grid_spec=pltpu.PrefetchScalarGridSpec(
            num_scalar_prefetch=1, grid=(1,), in_specs=ins, out_specs=out_specs
        ),
        out_shape=out_shape,
        compiler_params=pltpu.CompilerParams(vmem_limit_bytes=40 << 20),
        name="cut_weights",
    )(where, w_gate, w_up, *([w_down] * len(ks)))
    return out[0::2], out[1::2]


def tie(value, *others):
    return lax.optimization_barrier((value, others))[0]


def per_device(
    rows_n,
    tokens,
    seq_ids,
    block_ids,
    positions,
    norm1_gain,
    norm2_gain,
    w_query,
    w_kv,
    w_out,
    w_gate,
    w_up,
    w_down,
    grad_output,
):
    R = rows_n
    bits = []
    while (1 << len(bits)) < R:
        bits.append(1 << len(bits))
    nbits = len(bits)

    def reverse(v):
        out = 0
        for b in range(nbits):
            out = out | (((v >> b) & 1) << (nbits - 1 - b))
        return out

    order = [reverse(v) for v in range(R)]
    row = lax.axis_index("row")
    col = lax.axis_index("col")
    half_rows, dslice = tokens.shape
    B = half_rows // R
    full_rows = 2 * half_rows
    width = w_kv.shape[1] // 2
    dp_n = lax.axis_size("dp")

    def swap_row(a, bit):
        return lax.ppermute(a, "row", [(i, i ^ bit) for i in range(R)])

    def swap_col(a):
        return lax.ppermute(a, "col", [(0, 1), (1, 0)])

    def psum_row(a):
        for bit in bits:
            a = a + swap_row(a, bit)
        return a

    def pick(a, index, size):
        return lax.dynamic_slice_in_dim(a, index * size, size, 0)

    def to_order(a):
        return jnp.concatenate([pick(a, row ^ order[p], B) for p in range(R)], axis=0)

    def from_order(a):
        return jnp.concatenate([pick(a, reverse(row ^ b), B) for b in range(R)], axis=0)

    def reduce_row(a, send_after=(), use_after=()):
        a = a.astype(BF)
        for bit in bits:
            half = a.shape[0] // 2
            keep, send = a[:half], a[half:]
            if bit == bits[-1]:
                send = tie(send, send_after)
            came = swap_row(send, bit)
            if bit == bits[-1]:
                came = tie(came, use_after)
            total = keep.astype(F32) + came.astype(F32)
            a = total.astype(BF)
        return total

    def gather_row(a):
        for bit in reversed(bits):
            a = jnp.concatenate([a, swap_row(a, bit)], axis=0)
        return a

    def spread(pieces, bit):
        out = dict(pieces)
        for (a, k), value in pieces.items():
            out[(a, k ^ bit)] = swap_row(value, bit)
        return out

    def spread_col(pieces):
        out = dict(pieces)
        for (a, k), value in pieces.items():
            out[(1 - a, k)] = swap_col(value)
        return out

    half = half_rows // 2

    def gather_plane(mine):
        first = came = spread_col({(0, 0): mine[:half]})
        for bit in reversed(bits[1:]):
            first = spread(first, bit)
        second = {(0, 0): mine[half:]}
        for bit in reversed(bits[1:]):
            second = spread(second, bit)
        second = spread_col(second)
        return (spread(first, 1), spread(second, 1)), came

    def add(a, b, wide=False):
        total = a.astype(F32) + b.astype(F32)
        return total if wide else total.astype(BF)

    def reduce_plane(blocks, after=()):
        moved = {(a, k): swap_row(blocks[(a, k ^ 1)], 1) for a in (1, 0) for k in range(0, R, 2)}
        outs = []
        for part in range(2):
            here = slice(part * half, (part + 1) * half)
            cur = {key: add(blocks[key][here], value[here]) for key, value in moved.items()}
            cur = tie(cur, after)

            def by_col(cur, last):
                return {
                    (0, k): add(cur[(0, k)], swap_col(cur[(1, k)]), last)
                    for (a, k) in cur
                    if a == 0
                }

            def by_rows(cur, last):
                for bit in bits[1:]:
                    cur = {
                        (a, k): add(v, swap_row(cur[(a, k ^ bit)], bit), last and bit == bits[-1])
                        for (a, k), v in cur.items()
                        if not k & bit
                    }
                return cur

            if part == 0:
                cur = by_rows(by_col(cur, False), True)
            else:
                cur = by_col(by_rows(cur, False), True)
            outs.append(cur[(0, 0)])
        return jnp.concatenate(outs, axis=0)

    residual = tokens.astype(F32)
    scale_one = lax.rsqrt(psum_row(jnp.sum(residual * residual, axis=1)) / D + EPS)
    weighted_in = (residual * norm1_gain[None, :]).astype(BF)
    ordered_in = to_order(weighted_in)
    w_query_far = swap_col(w_query)
    own = col * R + row
    own_scale = lax.dynamic_slice_in_dim(scale_one, row * B, B)[:, None]

    kv_pre = reduce_row(dot_nn(ordered_in, w_kv)) * own_scale
    query_near = reduce_row(dot_nn(ordered_in, w_query)) * own_scale

    z = lax.axis_index("dp")
    near = min(2, R)
    hidden_n = w_gate.shape[1] // R
    shared = (dslice % (128 * dp_n) == 0, hidden_n % (16 * dp_n) == 0)
    rows_in = dslice // dp_n if shared[0] else dslice
    rows_down = hidden_n // dp_n if shared[1] else hidden_n

    shares = jnp.stack([row, z if shared[0] else 0 * z, z if shared[1] else 0 * z])
    shares = tie(shares, kv_pre)
    far_ks = tuple(range(near, R))
    cut_in, cut_down = cut_weights(shares, w_gate, w_up, w_down, far_ks, R, rows_in, rows_down)
    far_in = [swap_row(a, k) for a, k in zip(cut_in, far_ks)]
    cut_down = tie(cut_down, query_near)
    far_down = [swap_row(a, k) for a, k in zip(cut_down, far_ks)]
    if shared[0]:
        far_in = [jnp.stack(far_in)]
    w_out_far = swap_col(tie(w_out, w_query_far))
    query_near = tie(query_near, far_in, w_out_far)
    if shared[0]:
        far_in = [lax.all_gather(far_in[0], "dp", axis=0)]

    half_width = width // 2
    frequency = ROPE_BASE ** (-2.0 * jnp.arange(half_width, dtype=F32) / width)
    own_positions = lax.dynamic_slice_in_dim(positions, own * B, B)
    angles = own_positions.astype(F32)[:, None] * frequency[None, :]
    cosine = jnp.concatenate([jnp.cos(angles)] * 2, axis=1)
    sine_half = jnp.sin(angles)
    sine = jnp.concatenate([-sine_half, sine_half], axis=1)

    key_pre = kv_pre[:, :width]
    key_turned = jnp.concatenate([key_pre[:, half_width:], key_pre[:, :half_width]], axis=1)
    key_own = key_pre * cosine + key_turned * sine
    kv_own = jnp.concatenate([key_own, kv_pre[:, width:]], axis=1).astype(BF)
    kv_pieces = spread_col({(0, 0): kv_own})
    for bit in reversed(bits):
        kv_pieces = spread(kv_pieces, bit)
    kv_all = jnp.stack([kv_pieces[(a, k)] for a in range(2) for k in range(R)])
    keys = kv_all[:, :, :width]
    values = kv_all[:, :, width:]
    keys_t = keys.transpose(0, 2, 1)
    values_t = values.transpose(0, 2, 1)

    meta = (jnp.stack([row, col]), seq_ids, block_ids)
    cut_in, cut_down = cut_weights(
        shares * jnp.array([1, 0, 0], jnp.int32), w_gate, w_up, w_down, tuple(range(near)), R, dslice, hidden_n
    )
    close_in = [swap_row(a, k) if k else a for k, a in enumerate(cut_in)]
    close_down = [swap_row(a, k) if k else a for k, a in enumerate(cut_down)]
    att_near, rot_near, lse_near = attend(meta, query_near, cosine, sine, keys, values_t, width, R)
    down_grad = grad_output.astype(BF)
    grad_pieces = {(0, 0): tie(down_grad, query_near)}
    for bit in reversed(bits[1:]):
        grad_pieces = spread(grad_pieces, bit)
    grad_rows = dict(grad_pieces)
    grad_pieces[(1, 0)] = swap_col(tie(down_grad, w_query_far))
    query_far = reduce_row(
        dot_nn(ordered_in, w_query_far), send_after=query_near, use_after=(att_near, close_in)
    )
    query_far = tie(query_far, dict(grad_pieces)) * own_scale
    for (a, k), value in grad_rows.items():
        if k:
            grad_pieces[(1, k)] = swap_col(value)
    att_far, rot_far, lse_far = attend(meta, query_far, cosine, sine, keys, values_t, width, R)

    far_down = tie(far_down, att_near)
    if shared[1]:
        far_down = [lax.all_gather(jnp.stack(far_down), "dp", axis=0)]
    all_near = gather_row(att_near)
    all_far = tie(gather_row(att_far), grad_pieces)
    hidden = residual + from_order(dot_nn(all_near, w_out) + dot_nn(all_far, w_out_far))

    def exchange(parts):
        return [parts[0]] + [swap_row(parts[k], k) for k in range(1, len(parts))]

    scale_two = lax.rsqrt(psum_row(jnp.sum(hidden * hidden, axis=1)) / D + EPS)[:, None]
    normed_two = (hidden * scale_two * norm2_gain[None, :]).astype(BF)
    normed_pieces, came = gather_plane(normed_two)
    grad_pieces = spread(tie(grad_pieces, came), 1)

    fed = {}
    backs = {}
    for a in (0, 1):
        fed[a] = feed(
            [[part[(a, k)] for k in range(R)] for part in normed_pieces],
            [grad_pieces[(a, k)] for k in range(R)],
            close_in,
            close_down,
            far_in,
            far_down,
            shared,
            dp_n,
        )
        for k in range(R):
            backs[(a, k)] = fed[a][3 + k]
    acts, gate_grads, up_grads = ([fed[a][j] for a in range(2)] for j in range(3))
    normed_halves, grad_halves = ([fed[a][3 + R + j] for a in range(2)] for j in range(2))
    normed2_grad = reduce_plane(backs)

    def rows_of_down(k):
        if k < near:
            return close_down[k]
        if shared[1]:
            return far_down[0][:, k - near].reshape(hidden_n, dslice)
        return far_down[k - near]

    def ff_input_place(piece):
        moved = jnp.stack(exchange([piece[k] for k in range(R)]))
        ordered = jnp.concatenate(
            [lax.dynamic_index_in_dim(moved, row ^ s, 0, keepdims=False) for s in range(R)], axis=0
        )
        return ordered.astype(F32).T[None]

    def over_dp(local):
        return lax.psum_scatter(local, "dp", scatter_dimension=0, tiled=True)

    gate_local = feed_weight_grad(normed_halves, gate_grads, R, dp_n)
    up_local = feed_weight_grad(normed_halves, up_grads, R, dp_n)
    gate_piece = over_dp(gate_local)
    up_piece = over_dp(up_local)
    down_local = down_weight_grad(acts, grad_halves, R)
    normed2_grad = tie(normed2_grad, gate_local, up_local, down_local)

    weighted = normed2_grad * norm2_gain[None, :]
    inner_two = psum_row(jnp.sum(weighted * hidden, axis=1))[:, None]
    hidden_grad = grad_output + (
        scale_two * weighted - hidden * (scale_two * scale_two * scale_two) * inner_two / D
    )
    gain_two = jnp.sum(normed2_grad * hidden * scale_two, axis=0)
    branch_ordered = to_order(hidden_grad.astype(BF))
    late_acts = tie(acts, hidden_grad)
    products = {
        (a, k): dot_nn(late_acts[a], rows_of_down(k)).astype(BF) for a in range(2) for k in range(R)
    }
    att_grad_far = reduce_row(dot_nt(branch_ordered, w_out_far), use_after=products).astype(BF)
    grad_out_far = dot_tn(all_far, branch_ordered).astype(BF)
    grad_out_came = swap_col(grad_out_far)
    att_grad_far = tie(att_grad_far, grad_out_far)

    qpg_far, dk, dv = attend_back(
        meta, rot_far, att_grad_far, att_far, lse_far, cosine, sine, keys, keys_t, values, width, R
    )
    att_grad_near = reduce_row(
        dot_nt(branch_ordered, w_out), send_after=att_grad_far, use_after=(qpg_far, grad_out_came)
    ).astype(BF)
    qpg_near, dk, dv = attend_back(
        meta, rot_near, att_grad_near, att_near, lse_near, cosine, sine, keys, keys_t, values, width, R,
        (dk, dv),
    )
    grad_out_local = add(dot_tn(all_near, branch_ordered), grad_out_came)
    grad_out = over_dp(tie(grad_out_local, gate_piece, up_piece))

    dkv = jnp.concatenate([dk * width**-0.5, dv], axis=2).astype(BF)
    cur = {(a, k): dkv[a * R + k] for a in range(2) for k in range(R)}
    for bit in bits:
        cur = {
            (a, k): add(v, swap_row(cur[(a, k ^ bit)], bit))
            for (a, k), v in cur.items()
            if not k & bit
        }
    dkv_own = cur[(0, 0)].astype(F32) + swap_col(cur[(1, 0)]).astype(F32)
    dk_own = dkv_own[:, :width]
    dk_turned = jnp.concatenate([dk_own[:, half_width:], dk_own[:, :half_width]], axis=1)
    kvg_own = jnp.concatenate(
        [dk_own * cosine - dk_turned * sine, dkv_own[:, width:]], axis=1
    ).astype(BF)

    down_sent = [down_local[0]]
    for k in range(1, R):
        down_sent.append(swap_row(tie(down_local[k], normed2_grad if k < 3 else att_grad_far), k))
    down_moved = jnp.stack(down_sent)
    down_ordered = jnp.concatenate(
        [lax.dynamic_index_in_dim(down_moved, row ^ s, 0, keepdims=False) for s in range(R)], axis=0
    )
    grad_down = over_dp(tie(down_ordered, grad_out))
    output = hidden + reduce_plane(products, after=qpg_near)

    scale_col = scale_one[:, None]
    normed_ordered = to_order((residual * scale_col * norm1_gain[None, :]).astype(BF))
    qpg_far_all = gather_row(qpg_far)
    grad_query_far = dot_tn(normed_ordered, qpg_far_all).astype(BF)
    grad_query_came = swap_col(grad_query_far)
    qpg_near_all = tie(gather_row(qpg_near), grad_query_far)
    kvg_all = gather_row(kvg_own)
    normed1_grad = from_order(
        dot_nt(qpg_far_all, w_query_far) + dot_nt(qpg_near_all, w_query) + dot_nt(kvg_all, w_kv)
    )
    weighted_one = normed1_grad * norm1_gain[None, :]
    inner_one = psum_row(jnp.sum(weighted_one * residual, axis=1))[:, None]
    input_grad = hidden_grad + (
        scale_col * weighted_one - residual * (scale_col * scale_col * scale_col) * inner_one / D
    )
    gain_one = jnp.sum(normed1_grad * residual * scale_col, axis=0)

    grad_query_local = add(dot_tn(normed_ordered, qpg_near_all), grad_query_came)
    grad_query = over_dp(tie(grad_query_local, grad_down, output))

    def small_over_dp_col(local):
        rest = local.shape[0] // (dp_n * 2)
        local = local.reshape(dp_n, 2, rest, local.shape[1])
        mine = lax.dynamic_index_in_dim(local, col, 1, keepdims=False)
        other = lax.dynamic_index_in_dim(local, 1 - col, 1, keepdims=False).astype(BF)
        both = mine + swap_col(other).astype(F32)
        total = lax.dynamic_index_in_dim(both, z, 0, keepdims=False)
        for j in range(1, dp_n):
            share = lax.dynamic_index_in_dim(both, z ^ j, 0, keepdims=False).astype(BF)
            share = lax.ppermute(share, "dp", [(i, i ^ j) for i in range(dp_n)])
            total = total + share.astype(F32)
        return total

    grad_kv = small_over_dp_col(dot_tn(normed_ordered, kvg_all))
    gains = small_over_dp_col(jnp.stack([gain_one, gain_two], axis=1))

    return (
        output,
        input_grad,
        grad_query.astype(F32)[None],
        grad_kv[None],
        grad_out.astype(F32)[None],
        ff_input_place(gate_piece[0]),
        ff_input_place(up_piece[0]),
        grad_down.astype(F32)[None],
        gains[:, 0][None, :],
        gains[:, 1][None, :],
    )


def solution(mesh):
    placed = (
        P(("dp", "col"), "row"),
        P("dp"),
        P("dp"),
        P("dp"),
        P("row"),
        P("row"),
        P("row", "col"),
        P("row", None),
        P("col", "row"),
        P("row", "col"),
        P("row", "col"),
        P("col", "row"),
        P(("dp", "col"), "row"),
    )
    return jax.shard_map(
        functools.partial(per_device, mesh.shape["row"]),
        mesh=mesh,
        in_specs=placed,
        out_specs=(
            P(("dp", "col"), "row"),
            P(("dp", "col"), "row"),
            P("row", "dp", "col"),
            P("row", ("dp", "col"), None),
            P("col", "dp", "row"),
            P("row", "dp", "col"),
            P("row", "dp", "col"),
            P("col", "dp", "row"),
            P("row", ("dp", "col")),
            P("row", ("dp", "col")),
        ),
        check_vma=False,
    )
```

```python
import functools

import jax
import jax.numpy as jnp
from jax import lax
from jax.experimental import pallas as pl
from jax.experimental.pallas import tpu as pltpu
from jax.sharding import PartitionSpec as P

D = 2048
EPS = 1e-05
ROPE_BASE = 500000.0
BLOCK = 256
LOG2E = 1.4426950408889634
BF = jnp.bfloat16
F32 = jnp.float32
HEADS_PER_STEP = 4
FL = {'f11': 0, 'f13': 1, 'f0': 1, 'f1': 1, 'f5': 2, 'f9': 1, 'f12': 2, 'f2': 1, 'f3': 1, 'f4': 0, 'f8': 0, 'f10': 3, 'f6': 1, 'f7': 1, 'f14': 1, 'f15': 0, 'f16': 0, 'f17': 0, 'b0': 1, 'b1': 1, 'b2': 1, 'b3': 0, 'b4': 0, 'b5': 3, 'b6': 0, 'b7': 1, 'b8': 1, 'b29': 1, 'b28': 0, 'b18': 2, 'b19': 1, 'b24': 2, 'b9': 3, 'b13': 5, 'b14': 3, 'b15': 0, 'b16': 0, 'b17': 2, 'b20': 0, 'b22': 0, 'b23': 0, 'b25': 1, 'b26': 0, 'b27': 0, 'b30': 0, 'b31': 0, 'b32': 1, 'b33': 0, 'b34': 0, 'b36': 0}


def dot_nn(a, b):
    return lax.dot_general(a, b, (((1,), (0,)), ((), ())), preferred_element_type=F32)


def dot_nt(a, b):
    return lax.dot_general(a, b, (((1,), (1,)), ((), ())), preferred_element_type=F32)


def dot_tn(a, b):
    return lax.dot_general(a, b, (((0,), (0,)), ((), ())), preferred_element_type=F32)


def list_visible(where, seq_ref, block_ref, list_ref, *, rows_n, rows):
    row, col = where[0], where[1]
    chunks = 2 * rows_n
    own = (col * rows_n + row) * rows
    count = jnp.int32(0)
    for j in range(chunks):
        seen = (seq_ref[j * rows] == seq_ref[own]) & (block_ref[j * rows] <= block_ref[own])

        @pl.when(seen)
        def _(j=j, count=count):
            list_ref[count] = ((j // rows_n) ^ col) * rows_n + ((j % rows_n) ^ row)

        count = count + seen.astype(jnp.int32)
    list_ref[chunks] = count


def attend_body(
    where, seq_ref, block_ref, q_ref, cos_ref, sin_ref, *refs, factor, width, rows_n,
):
    pieces = refs[:-6]
    att_ref, rot_ref, lse_ref, list_ref, k_ref, vt_ref = refs[-6:]

    @pl.when(pl.program_id(0) == 0)
    def _():
        list_visible(where, seq_ref, block_ref, list_ref, rows_n=rows_n, rows=q_ref.shape[0])
        for j, piece in enumerate(pieces):
            k_ref[j] = piece[:, :width]
            vt_ref[j] = piece[:, width:].T

    cosine = cos_ref[...]
    sine = sin_ref[...]
    rows = q_ref.shape[0]
    heads = [slice(h * width, (h + 1) * width) for h in range(HEADS_PER_STEP)]
    for cols in heads:
        pre = q_ref[:, cols]
        rot_ref[:, cols] = (pre * cosine + pltpu.roll(pre, width // 2, 1) * sine).astype(BF)

    def step(t, carry):
        chunk = list_ref[t]
        key = k_ref[chunk]
        value_t = vt_ref[chunk]
        all_scores = [dot_nt(key, rot_ref[:, cols]) * factor for cols in heads]
        out = []
        for (top, total, acc), scores in zip(carry, all_scores):
            new_top = jnp.maximum(top, jnp.max(scores, axis=0, keepdims=True))
            decay = jnp.exp2(top - new_top)
            weights = jnp.exp2(scores - new_top)
            total = total * decay + jnp.sum(weights, axis=0, keepdims=True)
            acc = acc * decay + dot_nn(value_t, weights.astype(BF))
            out.append((new_top, total, acc))
        return out

    start = (
        jnp.full((1, rows), -1e30, F32),
        jnp.zeros((1, rows), F32),
        jnp.zeros((width, rows), F32),
    )
    done = lax.fori_loop(0, list_ref[2 * rows_n], step, [start] * HEADS_PER_STEP)
    for head, (top, total, acc) in enumerate(done):
        att_ref[:, heads[head]] = (acc / total).T.astype(BF)
        lse_ref[head] = top + jnp.log2(total)


def attend(meta, q_pre, cosine, sine, kv, width, rows_n):
    where, seq_ids, block_ids = meta
    rows, columns = q_pre.shape
    heads = columns // width
    chunks = len(kv)
    span = HEADS_PER_STEP * width
    whole2 = lambda i, m: (0, 0)
    return pl.pallas_call(
        functools.partial(attend_body, factor=width**-0.5 * LOG2E, width=width, rows_n=rows_n),
        grid_spec=pltpu.PrefetchScalarGridSpec(
            num_scalar_prefetch=1,
            grid=(heads // HEADS_PER_STEP,),
            in_specs=[
                pl.BlockSpec(memory_space=pltpu.SMEM),
                pl.BlockSpec(memory_space=pltpu.SMEM),
                pl.BlockSpec((rows, span), lambda i, m: (0, i)),
                pl.BlockSpec((rows, width), whole2),
                pl.BlockSpec((rows, width), whole2),
            ]
            + [pl.BlockSpec((rows, 2 * width), whole2)] * chunks,
            out_specs=[
                pl.BlockSpec((rows, span), lambda i, m: (0, i)),
                pl.BlockSpec((rows, span), lambda i, m: (0, i)),
                pl.BlockSpec((HEADS_PER_STEP, 1, rows), lambda i, m: (i, 0, 0)),
            ],
            scratch_shapes=[
                pltpu.SMEM((chunks + 1,), jnp.int32),
                pltpu.VMEM((chunks, rows, width), BF),
                pltpu.VMEM((chunks, width, rows), BF),
            ],
        ),
        out_shape=[
            jax.ShapeDtypeStruct((rows, columns), BF),
            jax.ShapeDtypeStruct((rows, columns), BF),
            jax.ShapeDtypeStruct((heads, 1, rows), F32),
        ],
        cost_estimate=pl.CostEstimate(
            flops=4 * rows * columns * chunks * rows // 2,
            transcendentals=heads * rows * chunks * rows // 2,
            bytes_accessed=8 * rows * columns + 4 * chunks * rows * width,
        ),
        name="attend",
    )(where, seq_ids, block_ids, q_pre, cosine, sine, *kv)


def attend_back_body(
    where, seq_ref, block_ref, rot_ref, grad_ref, att_ref, lse_ref, cos_ref, sin_ref,
    *outs, factor, scale, width, rows_n,
):
    pieces, outs = outs[: 2 * rows_n], outs[2 * rows_n :]
    qpg_ref, dk_ref, dv_ref, list_ref, k_ref, kt_ref, v_ref = outs[-7:]

    @pl.when(pl.program_id(0) == 0)
    def _():
        list_visible(where, seq_ref, block_ref, list_ref, rows_n=rows_n, rows=rot_ref.shape[0])
        dk_ref[...] = jnp.zeros_like(dk_ref) if len(outs) == 7 else outs[0][...]
        dv_ref[...] = jnp.zeros_like(dv_ref) if len(outs) == 7 else outs[1][...]
        for j, piece in enumerate(pieces):
            k_ref[j] = piece[:, :width]
            kt_ref[j] = piece[:, :width].T
            v_ref[j] = piece[:, width:]

    cosine = cos_ref[...]
    sine = sin_ref[...]
    rows = rot_ref.shape[0]
    heads = [slice(h * width, (h + 1) * width) for h in range(HEADS_PER_STEP)]
    inners = []
    for cols in heads:
        inner = (grad_ref[:, cols].astype(F32) * att_ref[:, cols].astype(F32)).T
        inners.append(jnp.sum(inner, axis=0, keepdims=True))

    def step(t, dqs):
        chunk = list_ref[t]
        key = k_ref[chunk]
        key_t = kt_ref[chunk]
        value = v_ref[chunk]
        all_scores = [dot_nt(key, rot_ref[:, cols]) for cols in heads]
        backs = [dot_nt(value, grad_ref[:, cols]) for cols in heads]
        dv = dv_ref[chunk]
        dk = dk_ref[chunk]
        out = []
        for h, cols in enumerate(heads):
            probs = jnp.exp2(all_scores[h] * factor - lse_ref[h])
            score_grad = (probs * (backs[h] - inners[h])).astype(BF)
            dv = dv + dot_nn(probs.astype(BF), grad_ref[:, cols])
            dk = dk + dot_nn(score_grad, rot_ref[:, cols])
            out.append(dqs[h] + dot_nn(key_t, score_grad))
        dv_ref[chunk] = dv
        dk_ref[chunk] = dk
        return out

    dqs = lax.fori_loop(0, list_ref[2 * rows_n], step, [jnp.zeros((width, rows), F32)] * HEADS_PER_STEP)
    for h, cols in enumerate(heads):
        dq = dqs[h].T * scale
        qpg_ref[:, cols] = (dq * cosine - pltpu.roll(dq, width // 2, 1) * sine).astype(BF)


def attend_back(meta, rot, grad, att, lse, cosine, sine, kv, width, rows_n, running=()):
    where, seq_ids, block_ids = meta
    rows, columns = rot.shape
    heads = columns // width
    chunks = len(kv)
    span = HEADS_PER_STEP * width
    whole2 = lambda i, m: (0, 0)
    whole3 = lambda i, m: (0, 0, 0)
    by_head = lambda i, m: (0, i)
    return pl.pallas_call(
        functools.partial(
            attend_back_body,
            factor=width**-0.5 * LOG2E,
            scale=width**-0.5,
            width=width,
            rows_n=rows_n,
        ),
        grid_spec=pltpu.PrefetchScalarGridSpec(
            num_scalar_prefetch=1,
            grid=(heads // HEADS_PER_STEP,),
            in_specs=[
                pl.BlockSpec(memory_space=pltpu.SMEM),
                pl.BlockSpec(memory_space=pltpu.SMEM),
                pl.BlockSpec((rows, span), by_head),
                pl.BlockSpec((rows, span), by_head),
                pl.BlockSpec((rows, span), by_head),
                pl.BlockSpec((HEADS_PER_STEP, 1, rows), lambda i, m: (i, 0, 0)),
                pl.BlockSpec((rows, width), whole2),
                pl.BlockSpec((rows, width), whole2),
            ]
            + [pl.BlockSpec((rows, 2 * width), whole2)] * chunks
            + [pl.BlockSpec((chunks, rows, width), whole3)] * len(running),
            out_specs=[
                pl.BlockSpec((rows, span), by_head),
                pl.BlockSpec((chunks, rows, width), whole3),
                pl.BlockSpec((chunks, rows, width), whole3),
            ],
            scratch_shapes=[
                pltpu.SMEM((chunks + 1,), jnp.int32),
                pltpu.VMEM((chunks, rows, width), BF),
                pltpu.VMEM((chunks, width, rows), BF),
                pltpu.VMEM((chunks, rows, width), BF),
            ],
        ),
        out_shape=[
            jax.ShapeDtypeStruct((rows, columns), BF),
            jax.ShapeDtypeStruct((chunks, rows, width), F32),
            jax.ShapeDtypeStruct((chunks, rows, width), F32),
        ],
        cost_estimate=pl.CostEstimate(
            flops=10 * rows * columns * chunks * rows // 2,
            transcendentals=heads * rows * chunks * rows // 2,
            bytes_accessed=8 * rows * columns + 12 * chunks * rows * width,
        ),
        name="attend_back",
    )(where, seq_ids, block_ids, rot, grad, att, lse, cosine, sine, *kv, *running)


def feed_body(*refs, rows_n, parts, near, shared):
    R = rows_n
    refs = list(refs)
    take = lambda n: [refs.pop(0) for _ in range(n)]
    normed = take(parts * R)
    grads = take(R)
    close_in, close_down = take(near), take(near)
    far_in = take(1 if shared[0] else R - near)
    far_down = take(1 if shared[1] else R - near)
    act_ref, gate_grad_ref, up_grad_ref = take(3)
    back_refs = take(R)
    normed_out, grads_out = take(2)
    x_ref, g_ref, wg_ref, wu_ref, wd_ref, x_sem, g_sem, w_sem, o_sem = refs
    step = pl.program_id(0)
    tile, span = normed[0].shape

    def x_copy(p, k):
        return pltpu.make_async_copy(
            normed[p * R + k], x_ref.at[p, :, pl.ds(k * span, span)], x_sem.at[p, k]
        )

    def g_copy(p, k):
        return pltpu.make_async_copy(
            grads[k].at[pl.ds(p * tile, tile)], g_ref.at[p, :, pl.ds(k * span, span)], g_sem.at[p, k]
        )

    def w_copies(j, k):
        target = (wg_ref, wu_ref, wd_ref)[j]
        if k < near or not shared[j // 2]:
            whole = (close_in + far_in, close_down + far_down)[j // 2][k]
            whole = whole if j == 2 else whole.at[j]
            place = target.at[:, pl.ds(k * span, span)]
            return [pltpu.make_async_copy(whole, place, w_sem.at[j, k, 0])]
        source = far_down[0] if j == 2 else far_in[0]
        copies = []
        for z in range(source.shape[0]):
            if j == 2:
                size = source.shape[-2]
                share = source.at[z, k - near]
                place = target.at[pl.ds(z * size, size), pl.ds(k * span, span)]
            else:
                size = source.shape[-1]
                share = source.at[z, k - near, j]
                place = target.at[:, pl.ds(k * span + z * size, size)]
            copies.append(pltpu.make_async_copy(share, place, w_sem.at[j, k, z]))
        return copies

    def x_out(p):
        return pltpu.make_async_copy(
            x_ref.at[p], normed_out.at[pl.ds(p * tile, tile)], o_sem.at[0, p]
        )

    def g_out(p):
        return pltpu.make_async_copy(
            g_ref.at[p], grads_out.at[pl.ds(p * tile, tile)], o_sem.at[1, p]
        )

    @pl.when(step == 0)
    def _():
        weights = [w_copies(j, k) for j in range(3) for k in range(R)]
        for k in range(R):
            x_copy(0, k).start()
            g_copy(0, k).start()
        for group in weights:
            for copy in group:
                copy.start()
        for p in range(1, parts):
            for k in range(R):
                x_copy(p, k).start()
                g_copy(p, k).start()
        for k in range(R):
            x_copy(0, k).wait()
            g_copy(0, k).wait()
        for group in weights:
            for copy in group:
                copy.wait()
        x_out(0).start()
        g_out(0).start()

    for p in range(1, parts):

        @pl.when(step == p)
        def _(p=p):
            for k in range(R):
                x_copy(p, k).wait()
                g_copy(p, k).wait()
            x_out(p).start()
            g_out(p).start()

    gate = dot_nt(x_ref[step], wg_ref[...])
    up = dot_nt(x_ref[step], wu_ref[...])
    mixed_grad = dot_nt(g_ref[step], wd_ref[...])
    sig = 1.0 / (1.0 + jnp.exp(-gate))
    silu = gate * sig
    act_ref[...] = (silu * up).astype(BF)
    gate_grad = (mixed_grad * up * sig * (1.0 + gate * (1.0 - sig))).astype(BF)
    up_grad = (mixed_grad * silu).astype(BF)
    gate_grad_ref[...] = gate_grad
    up_grad_ref[...] = up_grad
    for k in range(R):
        here = slice(k * span, (k + 1) * span)
        back = dot_nn(gate_grad, wg_ref[:, here]) + dot_nn(up_grad, wu_ref[:, here])
        back_refs[k][...] = back.astype(BF)

    @pl.when(step == parts - 1)
    def _():
        for p in range(parts):
            x_out(p).wait()
            g_out(p).wait()


def feed(normed, grads, close_in, close_down, far_in, far_down, shared, slots):
    parts = len(normed)
    R = len(grads)
    near = len(close_in)
    tile, span = normed[0][0].shape
    hidden_n = close_in[0].shape[1]
    total = parts * tile
    operands = [a for p in normed for a in p] + list(grads)
    operands += [*close_in, *close_down, *far_in, *far_down]
    by_tile = pl.BlockSpec((tile, hidden_n), lambda i: (i, 0))
    anywhere = pl.BlockSpec(memory_space=pl.ANY)
    return pl.pallas_call(
        functools.partial(feed_body, rows_n=R, parts=parts, near=near, shared=shared),
        grid=(parts,),
        in_specs=[anywhere] * len(operands),
        out_specs=[by_tile] * 3
        + [pl.BlockSpec((tile, span), lambda i: (i, 0))] * R
        + [anywhere] * 2,
        out_shape=[jax.ShapeDtypeStruct((total, hidden_n), BF)] * 3
        + [jax.ShapeDtypeStruct((total, span), BF)] * R
        + [jax.ShapeDtypeStruct((total, R * span), BF)] * 2,
        scratch_shapes=[
            pltpu.VMEM((parts, tile, R * span), BF),
            pltpu.VMEM((parts, tile, R * span), BF),
            pltpu.VMEM((hidden_n, R * span), BF),
            pltpu.VMEM((hidden_n, R * span), BF),
            pltpu.VMEM((hidden_n, R * span), BF),
            pltpu.SemaphoreType.DMA((parts, R)),
            pltpu.SemaphoreType.DMA((parts, R)),
            pltpu.SemaphoreType.DMA((3, R, slots)),
            pltpu.SemaphoreType.DMA((2, parts)),
        ],
        compiler_params=pltpu.CompilerParams(vmem_limit_bytes=56 << 20),
        cost_estimate=pl.CostEstimate(
            flops=10 * total * R * span * hidden_n,
            transcendentals=total * hidden_n,
            bytes_accessed=10 * total * R * span + 6 * R * span * hidden_n,
        ),
        name="feed",
    )(*operands)


def feed_weight_body(x0, x1, g0, g1, out_ref):
    total = (dot_tn(g0[...], x0[...]) + dot_tn(g1[...], x1[...])).astype(BF)
    share = out_ref.shape[3]
    for q in range(out_ref.shape[0]):
        out_ref[q, 0] = total[:, q * share : (q + 1) * share]


def feed_weight_grad(x, grads, rows_n, dp_n):
    tokens, features = x[0].shape
    span = features // rows_n
    hidden_n = grads[0].shape[1]
    return pl.pallas_call(
        feed_weight_body,
        grid=(rows_n,),
        in_specs=[pl.BlockSpec((tokens, span), lambda k: (0, k))] * 2
        + [pl.BlockSpec((tokens, hidden_n), lambda k: (0, 0))] * 2,
        out_specs=pl.BlockSpec((dp_n, 1, hidden_n, span // dp_n), lambda k: (0, k, 0, 0)),
        out_shape=jax.ShapeDtypeStruct((dp_n, rows_n, hidden_n, span // dp_n), BF),
        compiler_params=pltpu.CompilerParams(vmem_limit_bytes=48 << 20),
        cost_estimate=pl.CostEstimate(
            flops=4 * tokens * features * hidden_n,
            transcendentals=0,
            bytes_accessed=4 * tokens * (features + hidden_n) + 2 * features * hidden_n,
        ),
        name="feed_weights",
    )(*x, *grads)


def down_weight_body(a0, a1, g0, g1, out_ref):
    total = (dot_tn(a0[...], g0[...]) + dot_tn(a1[...], g1[...])).astype(BF)
    part = out_ref.shape[2]
    for q in range(out_ref.shape[0]):
        out_ref[q, 0] = total[q * part : (q + 1) * part]


def down_weight_grad(acts, grads, rows_n, dp_n):
    tokens, features = grads[0].shape
    span = features // rows_n
    hidden_n = acts[0].shape[1]
    part = hidden_n // dp_n
    return pl.pallas_call(
        down_weight_body,
        grid=(rows_n,),
        in_specs=[pl.BlockSpec((tokens, hidden_n), lambda k: (0, 0))] * 2
        + [pl.BlockSpec((tokens, span), lambda k: (0, k))] * 2,
        out_specs=pl.BlockSpec((dp_n, 1, part, span), lambda k: (0, k, 0, 0)),
        out_shape=jax.ShapeDtypeStruct((dp_n, rows_n, part, span), BF),
        compiler_params=pltpu.CompilerParams(vmem_limit_bytes=48 << 20),
        cost_estimate=pl.CostEstimate(
            flops=4 * tokens * features * hidden_n,
            transcendentals=0,
            bytes_accessed=4 * tokens * (features + hidden_n) + 2 * features * hidden_n,
        ),
        name="down_weights",
    )(*acts, *grads)


def late_weight_body(x0, x1, u0, u1, g0, g1, a0, a1, out_ref, *, rows_n):
    planes, _, _, rows, share = out_ref.shape

    @pl.when(pl.program_id(0) < rows_n)
    def _():
        total = (dot_tn(u0[...], x0[...]) + dot_tn(u1[...], x1[...])).astype(BF)
        for q in range(planes):
            out_ref[q, 0, 0] = total[:, q * share : (q + 1) * share]

    @pl.when(pl.program_id(0) >= rows_n)
    def _():
        total = (dot_tn(a0[...], g0[...]) + dot_tn(a1[...], g1[...])).astype(BF)
        part = rows // planes
        for q in range(planes):
            for j in range(planes):
                out_ref[q, 0, 0, j * part : (j + 1) * part] = total[
                    q * part : (q + 1) * part, j * share : (j + 1) * share
                ]


def late_weight_grads(x, ups, grads, acts, rows_n, dp_n):
    tokens, features = x[0].shape
    span = features // rows_n
    hidden_n = ups[0].shape[1]
    share = span // dp_n
    whole = pl.BlockSpec((tokens, hidden_n), lambda i: (0, 0))
    first = pl.BlockSpec((tokens, span), lambda i: (0, jnp.minimum(i, rows_n - 1)))
    second = pl.BlockSpec((tokens, span), lambda i: (0, jnp.maximum(i - rows_n, 0)))
    return pl.pallas_call(
        functools.partial(late_weight_body, rows_n=rows_n),
        grid=(2 * rows_n,),
        in_specs=[first] * 2 + [whole] * 2 + [second] * 2 + [whole] * 2,
        out_specs=pl.BlockSpec(
            (dp_n, 1, 1, hidden_n, share), lambda i: (0, i // rows_n, i % rows_n, 0, 0)
        ),
        out_shape=jax.ShapeDtypeStruct((dp_n, 2, rows_n, hidden_n, share), BF),
        compiler_params=pltpu.CompilerParams(vmem_limit_bytes=56 << 20),
        cost_estimate=pl.CostEstimate(
            flops=8 * tokens * features * hidden_n,
            transcendentals=0,
            bytes_accessed=8 * tokens * (features + hidden_n) + 4 * features * hidden_n,
        ),
        name="late_weights",
    )(*x, *ups, *grads, *acts)


def product_body(a0, a1, *refs, near):
    half = len(refs) // 3
    outs = refs[half:]
    for k in range(half):

        @pl.when(pl.program_id(0) == k)
        def _(k=k):
            weight = refs[k][...].reshape(a0.shape[1], outs[0].shape[1])
            outs[2 * k][...] = dot_nn(a0[...], weight).astype(BF)
            outs[2 * k + 1][...] = dot_nn(a1[...], weight).astype(BF)


def down_products(acts, close_down, far_down, rows_n):
    tokens, hidden_n = acts[0].shape
    span = close_down[0].shape[1]
    near = len(close_down)
    act = pl.BlockSpec((tokens, hidden_n), lambda i: (0, 0))
    ins, operands = [act] * 2, list(acts)
    for k in range(rows_n):
        if k < near or len(far_down) > 1:
            ins.append(pl.BlockSpec((hidden_n, span), lambda i: (0, 0)))
            operands.append(close_down[k] if k < near else far_down[k - near])
        else:
            planes, _, rows, _ = far_down[0].shape
            ins.append(
                pl.BlockSpec((planes, 1, rows, span), lambda i, k=k: (0, k - near, 0, 0))
            )
            operands.append(far_down[0])
    out = pl.pallas_call(
        functools.partial(product_body, near=near),
        grid=(rows_n,),
        in_specs=ins,
        out_specs=[pl.BlockSpec((tokens, span), lambda i: (0, 0))] * (2 * rows_n),
        out_shape=[jax.ShapeDtypeStruct((tokens, span), BF)] * (2 * rows_n),
        compiler_params=pltpu.CompilerParams(vmem_limit_bytes=56 << 20),
        name="down_products",
    )(*operands)
    return {(a, k): out[2 * k + a] for k in range(rows_n) for a in range(2)}


def finish_body(where, *refs, rows_n, dp_n):
    pieces = refs[:rows_n]
    gate_ref, up_ref, down_ref = refs[rows_n:]
    part = pieces[0].shape[1] // dp_n
    share = pieces[0].shape[2]
    for k in range(rows_n):
        sender = where[0] ^ k
        for i in range(rows_n):

            @pl.when(sender == i)
            def _(k=k, i=i):
                for q in range(dp_n):
                    rows = slice(q * part, (q + 1) * part)
                    here = slice((q * rows_n + i) * part, (q * rows_n + i + 1) * part)
                    gate_ref[:, here] = pieces[k][0, rows].astype(F32).T
                    up_ref[:, here] = pieces[k][1, rows].astype(F32).T
                    down_ref[i * part : (i + 1) * part, q * share : (q + 1) * share] = pieces[k][
                        2, rows
                    ].astype(F32)


def finish_weight_grads(where, pieces, rows_n, dp_n):
    _, hidden_n, share = pieces[0].shape
    spec = pl.BlockSpec((3, hidden_n, share), lambda i, w: (0, 0, 0))
    shapes = [(share, rows_n * hidden_n)] * 2 + [(hidden_n, dp_n * share)]
    return pl.pallas_call(
        functools.partial(finish_body, rows_n=rows_n, dp_n=dp_n),
        grid_spec=pltpu.PrefetchScalarGridSpec(
            num_scalar_prefetch=1,
            grid=(1,),
            in_specs=[spec] * rows_n,
            out_specs=[pl.BlockSpec(shape, lambda i, w: (0, 0)) for shape in shapes],
        ),
        out_shape=[jax.ShapeDtypeStruct(shape, F32) for shape in shapes],
        compiler_params=pltpu.CompilerParams(vmem_limit_bytes=40 << 20),
        name="finish_weights",
    )(where, *pieces)


def cut_body(where, *refs, ks, rows_n, dp_n):
    gate, up = refs[:2]
    outs = refs[len(refs) - 2 * len(ks) :]
    down_in = refs[2 : len(refs) - 2 * len(ks)]
    part = gate.shape[1] // (dp_n * rows_n)
    for n, k in enumerate(ks):
        slot = where[0] ^ k
        for i in range(rows_n):

            @pl.when(slot == i)
            def _(n=n, i=i):
                for q in range(dp_n):
                    here = slice((q * rows_n + i) * part, (q * rows_n + i + 1) * part)
                    there = slice(q * part, (q + 1) * part)
                    outs[2 * n][0, there] = gate[:, here].T
                    outs[2 * n][1, there] = up[:, here].T
                    if len(down_in) < len(ks):
                        outs[2 * n + 1][there] = down_in[0][here]

        if len(down_in) == len(ks):
            outs[2 * n + 1][...] = down_in[n][...]


def cut_weights(where, w_gate, w_up, w_down, ks, rows_n, dp_n, rows_in, rows_down):
    hidden_n = w_gate.shape[1] // rows_n
    part = hidden_n // dp_n
    span = w_down.shape[1]
    ins = [pl.BlockSpec((rows_in, w_gate.shape[1]), lambda i, w: (w[1], 0))] * 2
    if rows_down == part:
        for k in ks:
            ins.append(pl.BlockSpec((part, span), lambda i, w, k=k: (w[2] * rows_n + (w[0] ^ k), 0)))
    else:
        ins.append(pl.BlockSpec(w_down.shape, lambda i, w: (0, 0)))
    out_specs, out_shape = [], []
    for _ in ks:
        out_specs += [
            pl.BlockSpec((2, hidden_n, rows_in), lambda i, w: (0, 0, 0)),
            pl.BlockSpec((rows_down, span), lambda i, w: (0, 0)),
        ]
        out_shape += [
            jax.ShapeDtypeStruct((2, hidden_n, rows_in), BF),
            jax.ShapeDtypeStruct((rows_down, span), BF),
        ]
    out = pl.pallas_call(
        functools.partial(cut_body, ks=ks, rows_n=rows_n, dp_n=dp_n),
        grid_spec=pltpu.PrefetchScalarGridSpec(
            num_scalar_prefetch=1, grid=(1,), in_specs=ins, out_specs=out_specs
        ),
        out_shape=out_shape,
        compiler_params=pltpu.CompilerParams(vmem_limit_bytes=40 << 20),
        name="cut_weights",
    )(where, w_gate, w_up, *([w_down] * (len(ins) - 2)))
    return out[0::2], out[1::2]


def cut_plain(row, w_gate, w_up, w_down, ks, rows_n, dp_n):
    part = w_gate.shape[1] // (dp_n * rows_n)
    cut_in, cut_down = [], []
    for k in ks:
        starts = [(q * rows_n + (row ^ k)) * part for q in range(dp_n)]
        both = []
        for w in (w_gate.T, w_up.T):
            both.append(jnp.concatenate([lax.dynamic_slice_in_dim(w, at, part, 0) for at in starts]))
        cut_in.append(jnp.stack(both))
        cut_down.append(
            jnp.concatenate([lax.dynamic_slice_in_dim(w_down, at, part, 0) for at in starts])
        )
    return cut_in, cut_down


def tie(value, *others):
    return lax.optimization_barrier((value, others))[0]


def per_device(
    rows_n,
    tokens,
    seq_ids,
    block_ids,
    positions,
    norm1_gain,
    norm2_gain,
    w_query,
    w_kv,
    w_out,
    w_gate,
    w_up,
    w_down,
    grad_output,
):
    R = rows_n
    bits = []
    while (1 << len(bits)) < R:
        bits.append(1 << len(bits))
    nbits = len(bits)

    def reverse(v):
        out = 0
        for b in range(nbits):
            out = out | (((v >> b) & 1) << (nbits - 1 - b))
        return out

    order = [reverse(v) for v in range(R)]
    row = lax.axis_index("row")
    col = lax.axis_index("col")
    half_rows, dslice = tokens.shape
    B = half_rows // R
    full_rows = 2 * half_rows
    width = w_kv.shape[1] // 2
    dp_n = lax.axis_size("dp")

    def tf(flag, value, *others):
        return tie(value, *others) if FL.get(flag, 0) else value

    def tc(flag, value, *options):
        k = FL.get(flag, 0)
        return tie(value, options[k - 1]) if k else value

    def swap_row(a, bit):
        return lax.ppermute(a, "row", [(i, i ^ bit) for i in range(R)])

    def swap_col(a):
        return lax.ppermute(a, "col", [(0, 1), (1, 0)])

    def psum_row(a):
        for bit in bits:
            a = a + swap_row(a, bit)
        return a

    def pick(a, index, size):
        return lax.dynamic_slice_in_dim(a, index * size, size, 0)

    def to_order(a):
        return jnp.concatenate([pick(a, row ^ order[p], B) for p in range(R)], axis=0)

    def from_order(a):
        return jnp.concatenate([pick(a, reverse(row ^ b), B) for b in range(R)], axis=0)

    def reduce_row(a, send_after=(), use_after=()):
        a = a.astype(BF)
        for bit in bits:
            half = a.shape[0] // 2
            keep, send = a[:half], a[half:]
            if bit == bits[-1]:
                send = tie(send, send_after)
            came = swap_row(send, bit)
            if bit == bits[-1]:
                came = tie(came, use_after)
            total = keep.astype(F32) + came.astype(F32)
            a = total.astype(BF)
        return total

    def gather_outer(a):
        for bit in reversed(bits[1:]):
            a = jnp.concatenate([a, swap_row(a, bit)], axis=0)
        return a

    def gather_core(a):
        return jnp.concatenate([a, swap_row(a, 1)], axis=0)

    def gather_row(a):
        return gather_core(gather_outer(a))

    def spread(pieces, bit):
        out = dict(pieces)
        for (a, k), value in pieces.items():
            out[(a, k ^ bit)] = swap_row(value, bit)
        return out

    def spread_col(pieces):
        out = dict(pieces)
        for (a, k), value in pieces.items():
            out[(1 - a, k)] = swap_col(value)
        return out

    half = half_rows // 2

    def gather_plane(mine):
        first = came = spread_col({(0, 0): mine[:half]})
        for bit in reversed(bits[1:]):
            first = spread(first, bit)
        second = {(0, 0): mine[half:]}
        for bit in reversed(bits[1:]):
            second = spread(second, bit)
        second = spread_col(second)
        return (spread(first, 1), spread(second, 1)), came

    def add(a, b, wide=False):
        total = a.astype(F32) + b.astype(F32)
        return total if wide else total.astype(BF)

    def reduce_plane(blocks, after=((), ()), then=()):
        moved = {(a, k): swap_row(blocks[(a, k ^ 1)], 1) for a in (1, 0) for k in range(0, R, 2)}
        outs, firsts, seconds = [], [], []
        for part in range(2):
            here = slice(part * half, (part + 1) * half)
            cur = {key: add(blocks[key][here], value[here]) for key, value in moved.items()}
            firsts.append(list(cur.values()))
            cur = tie(cur, after[part])

            def by_col(cur, last):
                return {
                    (0, k): add(cur[(0, k)], swap_col(cur[(1, k)]), last)
                    for (a, k) in cur
                    if a == 0
                }

            def by_rows(cur, last):
                for bit in bits[1:]:
                    cur = {
                        (a, k): add(v, swap_row(cur[(a, k ^ bit)], bit), last and bit == bits[-1])
                        for (a, k), v in cur.items()
                        if not k & bit
                    }
                return cur

            if part == 0:
                cur = by_col(cur, False)
                seconds.append(list(cur.values()))
                cur = by_rows(tie(cur, then), True)
            else:
                cur = by_rows(cur, False)
                seconds.append(list(cur.values()))
                cur = by_col(tie(cur, then), True)
            outs.append(cur[(0, 0)])
        return jnp.concatenate(outs, axis=0), firsts, seconds

    residual = tokens.astype(F32)
    scale_one = lax.rsqrt(psum_row(jnp.sum(residual * residual, axis=1)) / D + EPS)
    weighted_in = (residual * norm1_gain[None, :]).astype(BF)
    ordered_in = to_order(weighted_in)
    w_query_far = swap_col(w_query)
    own = col * R + row
    own_scale = lax.dynamic_slice_in_dim(scale_one, row * B, B)[:, None]

    kv_pre = reduce_row(dot_nn(ordered_in, w_kv)) * own_scale
    query_near = reduce_row(dot_nn(ordered_in, w_query)) * own_scale

    z = lax.axis_index("dp")
    near = min(2, R)
    hidden_n = w_gate.shape[1] // R
    shared = (dslice % (128 * dp_n) == 0, hidden_n % (16 * dp_n) == 0)
    shared = (all(shared), all(shared))
    rows_in = dslice // dp_n if shared[0] else dslice
    rows_down = hidden_n // dp_n if shared[1] else hidden_n

    shares = jnp.stack([row, z if shared[0] else 0 * z, z if shared[1] else 0 * z])
    shares = tie(shares, kv_pre)
    far_ks = tuple(range(near, R))
    part = hidden_n // dp_n
    if part % 16 == 0:
        cut_in, cut_down = cut_weights(shares, w_gate, w_up, w_down, far_ks, R, dp_n, rows_in, rows_down)
    else:
        cut_in, cut_down = cut_plain(row, w_gate, w_up, w_down, far_ks, R, dp_n)
    half_width = width // 2
    frequency = ROPE_BASE ** (-2.0 * jnp.arange(half_width, dtype=F32) / width)
    own_positions = lax.dynamic_slice_in_dim(positions, own * B, B)
    angles = own_positions.astype(F32)[:, None] * frequency[None, :]
    cosine = jnp.concatenate([jnp.cos(angles)] * 2, axis=1)
    sine_half = jnp.sin(angles)
    sine = jnp.concatenate([-sine_half, sine_half], axis=1)

    key_pre = kv_pre[:, :width]
    key_turned = jnp.concatenate([key_pre[:, half_width:], key_pre[:, :half_width]], axis=1)
    key_own = key_pre * cosine + key_turned * sine
    kv_own = jnp.concatenate([key_own, kv_pre[:, width:]], axis=1).astype(BF)
    kv_pieces = spread_col({(0, 0): kv_own})
    for bit in reversed(bits):
        kv_pieces = spread(kv_pieces, bit)
    kv_all = [kv_pieces[(a, k)] for a in range(2) for k in range(R)]
    meta = (jnp.stack([row, col]), seq_ids, block_ids)
    far_in = [swap_row(a, k) for a, k in zip(tf("f11", cut_in, kv_all), far_ks)]
    far_cut_down = cut_down
    if shared[0]:
        far_in = [jnp.stack(far_in)]
    w_out_far = swap_col(tc("f13", w_out, w_query_far, query_near, kv_pre))
    query_near = tf("f0", query_near, w_out_far)
    query_near = tf("f1", query_near, far_in)
    close_ks = tuple(range(near))
    if part % 16 == 0:
        shares = shares * jnp.array([1, 0, 0], jnp.int32)
        cut_in, cut_down = cut_weights(shares, w_gate, w_up, w_down, close_ks, R, dp_n, dslice, hidden_n)
    else:
        cut_in, cut_down = cut_plain(row, w_gate, w_up, w_down, close_ks, R, dp_n)
    close_in = [swap_row(a, k) if k else a for k, a in enumerate(cut_in)]
    close_down = [swap_row(a, k) if k else a for k, a in enumerate(cut_down)]
    query_near_raw = query_near
    down_grad = grad_output.astype(BF)
    part_qfar = dot_nn(ordered_in, w_query_far).astype(BF)
    if FL.get("f5", 0) < 3:
        grad_pieces = {(0, 0): tc("f5", down_grad, kv_pre, query_near)}
        for bit in reversed(bits[1:]):
            grad_pieces = spread(grad_pieces, bit)
        query_near = tf("f15", query_near, grad_pieces[(0, bits[-1])])
    att_near, rot_near, lse_near = attend(meta, query_near, cosine, sine, kv_all, width, R)
    if FL.get("f5", 0) >= 3:
        grad_pieces = {(0, 0): tie(down_grad, att_near)}
        for bit in reversed(bits[1:]):
            grad_pieces = spread(grad_pieces, bit)
    grad_rows = dict(grad_pieces)
    for (a, k), value in grad_rows.items():
        if k:
            grad_pieces[(1, k)] = swap_col(value)
        else:
            grad_pieces[(1, k)] = swap_col(tc("f12", down_grad, w_query_far, query_near_raw, w_out_far, att_near))
    query_far = reduce_row(
        part_qfar,
        send_after=query_near_raw if FL.get("f9", 0) else (),
        use_after=(att_near, close_in),
    )
    query_far = tf("f2", query_far, grad_pieces[(1, 0)])
    query_far = tf("f3", query_far, far_in)
    query_far = tf("f4", query_far, w_out_far)
    query_far = tf("f8", query_far, grad_rows) * own_scale
    if shared[0]:
        far_in = [lax.all_gather(far_in[0], "dp", axis=0)]
    near_outer = gather_outer(att_near)
    query_far = tf("f16", query_far, near_outer)
    att_far, rot_far, lse_far = attend(meta, query_far, cosine, sine, kv_all, width, R)
    far_cut_down = tc("f10", far_cut_down, query_near_raw, att_near, att_far, near_outer)
    far_down = [swap_row(a, k) for a, k in zip(far_cut_down, far_ks)]
    if shared[1]:
        far_down = [lax.all_gather(jnp.stack(far_down), "dp", axis=0)]

    all_near = gather_core(near_outer)
    far_outer = gather_outer(att_far)
    far_outer = tf("f6", far_outer, grad_rows)
    far_outer = tf("f17", far_outer, grad_pieces)
    all_far = gather_core(far_outer)
    hidden = residual + from_order(dot_nn(all_near, w_out) + dot_nn(all_far, w_out_far))

    def exchange(parts):
        return [parts[0]] + [swap_row(parts[k], k) for k in range(1, len(parts))]

    scale_two = lax.rsqrt(psum_row(jnp.sum(hidden * hidden, axis=1)) / D + EPS)[:, None]
    normed_two = (hidden * scale_two * norm2_gain[None, :]).astype(BF)
    normed_pieces, came = gather_plane(tf("f7", normed_two, grad_pieces))
    grad_pieces = spread(tf("f14", grad_pieces, came), 1)

    fed = {}
    backs = {}
    for a in (0, 1):
        fed[a] = feed(
            [[part[(a, k)] for k in range(R)] for part in normed_pieces],
            [grad_pieces[(a, k)] for k in range(R)],
            close_in,
            close_down,
            far_in,
            far_down,
            shared,
            dp_n,
        )
        for k in range(R):
            backs[(a, k)] = fed[a][3 + k]
    acts, gate_grads, up_grads = ([fed[a][j] for a in range(2)] for j in range(3))
    normed_halves, grad_halves = ([fed[a][3 + R + j] for a in range(2)] for j in range(2))
    normed2_grad, firsts, seconds = reduce_plane(backs)

    def place(pieces):
        moved = jnp.stack(exchange([jnp.stack([p[k] for p in pieces]) for k in range(R)]))
        ordered = [lax.dynamic_index_in_dim(moved, row ^ s, 0, keepdims=False) for s in range(R)]
        return [jnp.stack([o[n] for o in ordered]) for n in range(len(pieces))]

    def ff_input_place(rows):
        rows = rows.reshape(R, dp_n, part, -1).transpose(1, 0, 2, 3)
        return rows.reshape(R * hidden_n, -1).astype(F32).T

    def over_dp(local):
        return lax.psum_scatter(local, "dp", scatter_dimension=0, tiled=True)

    gate_local = feed_weight_grad(normed_halves, gate_grads, R, dp_n)
    gate_piece = over_dp(gate_local)
    if shared[1]:
        late = late_weight_grads(
            normed_halves, tf("b1", tf("b0", tie(up_grads, gate_local), firsts), seconds), grad_halves, acts, R, dp_n
        )
        late_piece = over_dp(tie(late, gate_local))
        up_piece, down_piece = late_piece[0, 0], late_piece[0, 1]
        normed2_grad = tie(normed2_grad, gate_local, late)
    else:
        late_piece = gate_piece
        up_piece = over_dp(feed_weight_grad(normed_halves, up_grads, R, dp_n))[0]
        down_piece = over_dp(down_weight_grad(acts, grad_halves, R, dp_n))[0]

    weighted = normed2_grad * norm2_gain[None, :]
    inner_two = psum_row(jnp.sum(weighted * hidden, axis=1))[:, None]
    hidden_grad = grad_output + (
        scale_two * weighted - hidden * (scale_two * scale_two * scale_two) * inner_two / D
    )
    gain_two = jnp.sum(normed2_grad * hidden * scale_two, axis=0)
    branch_ordered = to_order(hidden_grad.astype(BF))
    part_far = dot_nt(branch_ordered, w_out_far).astype(BF)
    part_near = dot_nt(branch_ordered, w_out).astype(BF)
    prod_dep = FL.get("b5", 0)
    branch_late, late_acts = branch_ordered, acts

    def make_products():
        return down_products(late_acts, close_down, far_down, R)

    if prod_dep < 2:
        late_acts = tie(acts, hidden_grad) if prod_dep == 0 else tie(acts, part_far, part_near)
        products = make_products()
    b6 = FL.get("b6", 0) if prod_dep < 2 else 0
    att_grad_far = reduce_row(part_far, use_after=products if b6 == 1 else ()).astype(BF)
    att_grad_near = reduce_row(
        part_near, send_after=att_grad_far if FL.get("b25", 0) else (), use_after=products if b6 == 2 else ()
    ).astype(BF)
    gout_early = FL.get("b26", 0)
    if gout_early:
        grad_out_far = dot_tn(all_far, branch_late).astype(BF)
        grad_out_came = swap_col(grad_out_far)
        grad_out_near = dot_tn(all_near, branch_late)
        att_grad_far = tf("b27", att_grad_far, grad_out_far, grad_out_near)
        att_grad_far = tf("b4", att_grad_far, grad_out_came)
    att_grad_far = tf("b2", att_grad_far, gate_piece)
    att_grad_far = tf("b3", att_grad_far, att_grad_near)

    qpg_far, dk, dv = attend_back(
        meta, rot_far, att_grad_far, att_far, lse_far, cosine, sine, kv_all, width, R
    )
    if not gout_early:
        branch_late = tie(branch_ordered, qpg_far)
        grad_out_far = dot_tn(all_far, branch_late).astype(BF)
        grad_out_came = swap_col(grad_out_far)
        grad_out_near = dot_tn(all_near, branch_late)
    if prod_dep == 2:
        late_acts = tie(acts, qpg_far)
        products = make_products()
    scale_col = scale_one[:, None]
    normed_ordered = to_order((residual * scale_col * norm1_gain[None, :]).astype(BF))
    qpg_far_outer = gather_outer(tf("b28", qpg_far, grad_out_far))
    qpg_far_all = gather_core(qpg_far_outer)
    qpg_far_used = tf("b8", qpg_far_all, grad_out_near)
    if prod_dep < 3:
        qpg_far_used = tf("b29", qpg_far_used, products)
    grad_query_far = dot_tn(normed_ordered, qpg_far_used).astype(BF)
    grad_query_came = swap_col(grad_query_far)
    att_grad_near = tf("b30", att_grad_near, qpg_far_outer)
    att_grad_near = tf("b7", att_grad_near, grad_query_far)
    att_grad_near = tf("b31", att_grad_near, grad_out_came)
    qpg_near, dk, dv = attend_back(
        meta, rot_near, att_grad_near, att_near, lse_near, cosine, sine, kv_all, width, R,
        (dk, dv),
    )
    if prod_dep == 3:
        late_acts = tie(acts, qpg_near)
        products = make_products()
    grad_out_local = add(grad_out_near, tc("b24", grad_out_came, qpg_far, qpg_near))
    grad_out = over_dp(tc("b18", grad_out_local, gate_piece, late_piece))
    qpg_near_outer = gather_outer(tf("b32", qpg_near, grad_out_local))
    qpg_near_all = gather_core(qpg_near_outer)
    qpg_near_used = tf("b19", tie(qpg_near_all, grad_query_came), late_piece)
    grad_query_near = dot_tn(normed_ordered, qpg_near_used)
    grad_query_local = add(grad_query_near, grad_query_came)
    opts = (qpg_far, qpg_near, qpg_near_outer, grad_query_came, grad_query_local)
    pick_opt = lambda k: () if not k else opts[k - 1]
    down_sum, _, seconds_out = reduce_plane(
        products,
        after=(pick_opt(FL.get("b13", 0)), pick_opt(FL.get("b14", 0))),
        then=pick_opt(FL.get("b15", 0)),
    )
    output = hidden + down_sum
    dk, dv = tc("b9", (dk, dv), qpg_near_outer, grad_out_local, grad_query_came, grad_query_local)

    dkv = jnp.concatenate([dk * width**-0.5, dv], axis=2).astype(BF)
    cur = {(a, k): dkv[a * R + k] for a in range(2) for k in range(R)}
    for bit in bits:
        cur = {
            (a, k): add(v, swap_row(cur[(a, k ^ bit)], bit))
            for (a, k), v in cur.items()
            if not k & bit
        }
    dkv_own = cur[(0, 0)].astype(F32) + swap_col(cur[(1, 0)]).astype(F32)
    dk_own = dkv_own[:, :width]
    dk_turned = jnp.concatenate([dk_own[:, half_width:], dk_own[:, :half_width]], axis=1)
    kvg_own = jnp.concatenate(
        [dk_own * cosine - dk_turned * sine, dkv_own[:, width:]], axis=1
    ).astype(BF)


    pieces = tc("b17", (gate_piece[0], up_piece, down_piece), qpg_near, grad_query_local, qpg_near_outer)
    moved = exchange([jnp.stack([p[k] for p in pieces]) for k in range(R)]) if shared[1] else ()
    kvg_own = tf("b36", kvg_own, moved)
    kvg_own = tc("b16", kvg_own, qpg_near_outer, grad_query_came, grad_query_local)
    kvg_all = gather_row(kvg_own)
    normed1_grad = from_order(
        dot_nt(qpg_far_all, w_query_far) + dot_nt(qpg_near_all, w_query) + dot_nt(kvg_all, w_kv)
    )
    normed1_grad = tf("b22", normed1_grad, grad_out)
    normed1_grad = tf("b33", normed1_grad, moved)
    normed1_grad = tf("b34", normed1_grad, grad_query_local)
    normed1_grad = tf("b23", normed1_grad, output)
    weighted_one = normed1_grad * norm1_gain[None, :]
    inner_one = psum_row(jnp.sum(weighted_one * residual, axis=1))[:, None]
    input_grad = hidden_grad + (
        scale_col * weighted_one - residual * (scale_col * scale_col * scale_col) * inner_one / D
    )
    gain_one = jnp.sum(normed1_grad * residual * scale_col, axis=0)

    grad_query = over_dp(tf("b20", grad_query_local, grad_out))
    if shared[1]:
        grad_gate, grad_up, grad_down = finish_weight_grads(meta[0], moved, R, dp_n)
    else:
        gate_rows, up_rows = place(pieces[:2])
        grad_gate, grad_up = ff_input_place(gate_rows), ff_input_place(up_rows)
        grad_down = place(pieces[2:])[0].reshape(hidden_n, dslice).astype(F32)

    rest = dslice // (2 * dp_n)
    gains = jnp.concatenate(
        [g.reshape(dp_n, 2, 1, rest) for g in (gain_one, gain_two)]
        + [jnp.zeros((dp_n, 2, 1, 2 * width - 2 * rest), F32)],
        axis=3,
    )
    local = dot_tn(normed_ordered, kvg_all).reshape(dp_n, 2, rest, 2 * width)
    local = jnp.concatenate([local, gains], axis=2)
    mine = lax.dynamic_index_in_dim(local, col, 1, keepdims=False)
    other = lax.dynamic_index_in_dim(local, 1 - col, 1, keepdims=False).astype(BF)
    both = mine + swap_col(other).astype(F32)
    small = lax.dynamic_index_in_dim(both, z, 0, keepdims=False)
    for j in range(1, dp_n):
        share = lax.dynamic_index_in_dim(both, z ^ j, 0, keepdims=False).astype(BF)
        share = lax.ppermute(share, "dp", [(i, i ^ j) for i in range(dp_n)])
        small = small + share.astype(F32)

    return (
        output,
        input_grad,
        grad_query.astype(F32)[None],
        small[None, :rest],
        grad_out.astype(F32)[None],
        grad_gate[None],
        grad_up[None],
        grad_down[None],
        small[rest:, :rest],
        small[rest:, rest : 2 * rest],
    )


def solution(mesh):
    placed = (
        P(("dp", "col"), "row"),
        P("dp"),
        P("dp"),
        P("dp"),
        P("row"),
        P("row"),
        P("row", "col"),
        P("row", None),
        P("col", "row"),
        P("row", "col"),
        P("row", "col"),
        P("col", "row"),
        P(("dp", "col"), "row"),
    )
    return jax.shard_map(
        functools.partial(per_device, mesh.shape["row"]),
        mesh=mesh,
        in_specs=placed,
        out_specs=(
            P(("dp", "col"), "row"),
            P(("dp", "col"), "row"),
            P("row", "dp", "col"),
            P("row", ("dp", "col"), None),
            P("col", "dp", "row"),
            P("row", "dp", "col"),
            P("row", "dp", "col"),
            P("col", "dp", "row"),
            P("row", ("dp", "col")),
            P("row", ("dp", "col")),
        ),
        check_vma=False,
    )
```

```python
import functools

import jax
import jax.numpy as jnp
from jax import lax
from jax.experimental import pallas as pl
from jax.experimental.pallas import tpu as pltpu
from jax.sharding import PartitionSpec as P

D = 2048
EPS = 1e-05
ROPE_BASE = 500000.0
BLOCK = 256
LOG2E = 1.4426950408889634
BF = jnp.bfloat16
F32 = jnp.float32
HEADS_PER_STEP = 4
FL = {'f11': 0, 'f13': 1, 'f0': 1, 'f1': 1, 'f5': 2, 'f9': 1, 'f12': 2, 'f2': 1, 'f3': 1, 'f4': 0, 'f8': 1, 'f10': 3, 'f6': 1, 'f7': 1, 'f14': 1, 'f15': 0, 'f16': 0, 'f17': 0, 'b0': 1, 'b1': 0, 'b2': 1, 'b3': 0, 'b4': 0, 'b5': 2, 'b6': 0, 'b7': 1, 'b8': 1, 'b29': 0, 'b28': 0, 'b18': 2, 'b19': 1, 'b24': 2, 'b9': 3, 'b13': 5, 'b14': 1, 'b15': 0, 'b16': 0, 'b17': 2, 'b20': 0, 'b22': 0, 'b23': 0, 'b25': 1, 'b26': 1, 'b27': 0, 'b30': 0, 'b31': 0, 'b32': 0, 'b33': 0, 'b34': 0, 'b36': 0, 'b37': 1}


def dot_nn(a, b):
    return lax.dot_general(a, b, (((1,), (0,)), ((), ())), preferred_element_type=F32)


def dot_nt(a, b):
    return lax.dot_general(a, b, (((1,), (1,)), ((), ())), preferred_element_type=F32)


def dot_tn(a, b):
    return lax.dot_general(a, b, (((0,), (0,)), ((), ())), preferred_element_type=F32)


def list_visible(where, seq_ref, block_ref, list_ref, *, rows_n, rows):
    row, col = where[0], where[1]
    chunks = 2 * rows_n
    own = (col * rows_n + row) * rows
    count = jnp.int32(0)
    for j in range(chunks):
        seen = (seq_ref[j * rows] == seq_ref[own]) & (block_ref[j * rows] <= block_ref[own])

        @pl.when(seen)
        def _(j=j, count=count):
            list_ref[count] = ((j // rows_n) ^ col) * rows_n + ((j % rows_n) ^ row)

        count = count + seen.astype(jnp.int32)
    list_ref[chunks] = count


def attend_body(
    where, seq_ref, block_ref, q_ref, cos_ref, sin_ref, *refs, factor, width, rows_n,
):
    pieces = refs[:-6]
    att_ref, rot_ref, lse_ref, list_ref, k_ref, vt_ref = refs[-6:]

    @pl.when(pl.program_id(0) == 0)
    def _():
        list_visible(where, seq_ref, block_ref, list_ref, rows_n=rows_n, rows=q_ref.shape[0])
        for j, piece in enumerate(pieces):
            k_ref[j] = piece[:, :width]
            vt_ref[j] = piece[:, width:].T

    cosine = cos_ref[...]
    sine = sin_ref[...]
    rows = q_ref.shape[0]
    heads = [slice(h * width, (h + 1) * width) for h in range(HEADS_PER_STEP)]
    for cols in heads:
        pre = q_ref[:, cols]
        rot_ref[:, cols] = (pre * cosine + pltpu.roll(pre, width // 2, 1) * sine).astype(BF)

    def step(t, carry):
        chunk = list_ref[t]
        key = k_ref[chunk]
        value_t = vt_ref[chunk]
        all_scores = [dot_nt(key, rot_ref[:, cols]) * factor for cols in heads]
        out = []
        for (top, total, acc), scores in zip(carry, all_scores):
            new_top = jnp.maximum(top, jnp.max(scores, axis=0, keepdims=True))
            decay = jnp.exp2(top - new_top)
            weights = jnp.exp2(scores - new_top)
            total = total * decay + jnp.sum(weights, axis=0, keepdims=True)
            acc = acc * decay + dot_nn(value_t, weights.astype(BF))
            out.append((new_top, total, acc))
        return out

    start = (
        jnp.full((1, rows), -1e30, F32),
        jnp.zeros((1, rows), F32),
        jnp.zeros((width, rows), F32),
    )
    done = lax.fori_loop(0, list_ref[2 * rows_n], step, [start] * HEADS_PER_STEP)
    for head, (top, total, acc) in enumerate(done):
        att_ref[:, heads[head]] = (acc / total).T.astype(BF)
        lse_ref[head] = top + jnp.log2(total)


def attend(meta, q_pre, cosine, sine, kv, width, rows_n):
    where, seq_ids, block_ids = meta
    rows, columns = q_pre.shape
    heads = columns // width
    chunks = len(kv)
    span = HEADS_PER_STEP * width
    whole2 = lambda i, m: (0, 0)
    return pl.pallas_call(
        functools.partial(attend_body, factor=width**-0.5 * LOG2E, width=width, rows_n=rows_n),
        grid_spec=pltpu.PrefetchScalarGridSpec(
            num_scalar_prefetch=1,
            grid=(heads // HEADS_PER_STEP,),
            in_specs=[
                pl.BlockSpec(memory_space=pltpu.SMEM),
                pl.BlockSpec(memory_space=pltpu.SMEM),
                pl.BlockSpec((rows, span), lambda i, m: (0, i)),
                pl.BlockSpec((rows, width), whole2),
                pl.BlockSpec((rows, width), whole2),
            ]
            + [pl.BlockSpec((rows, 2 * width), whole2)] * chunks,
            out_specs=[
                pl.BlockSpec((rows, span), lambda i, m: (0, i)),
                pl.BlockSpec((rows, span), lambda i, m: (0, i)),
                pl.BlockSpec((HEADS_PER_STEP, 1, rows), lambda i, m: (i, 0, 0)),
            ],
            scratch_shapes=[
                pltpu.SMEM((chunks + 1,), jnp.int32),
                pltpu.VMEM((chunks, rows, width), BF),
                pltpu.VMEM((chunks, width, rows), BF),
            ],
        ),
        out_shape=[
            jax.ShapeDtypeStruct((rows, columns), BF),
            jax.ShapeDtypeStruct((rows, columns), BF),
            jax.ShapeDtypeStruct((heads, 1, rows), F32),
        ],
        cost_estimate=pl.CostEstimate(
            flops=4 * rows * columns * chunks * rows // 2,
            transcendentals=heads * rows * chunks * rows // 2,
            bytes_accessed=8 * rows * columns + 4 * chunks * rows * width,
        ),
        name="attend",
    )(where, seq_ids, block_ids, q_pre, cosine, sine, *kv)


def attend_back_body(
    where, seq_ref, block_ref, rot_ref, grad_ref, att_ref, lse_ref, cos_ref, sin_ref,
    *outs, factor, scale, width, rows_n,
):
    pieces, outs = outs[: 2 * rows_n], outs[2 * rows_n :]
    qpg_ref, dk_ref, dv_ref, list_ref, k_ref, kt_ref, v_ref = outs[-7:]

    @pl.when(pl.program_id(0) == 0)
    def _():
        list_visible(where, seq_ref, block_ref, list_ref, rows_n=rows_n, rows=rot_ref.shape[0])
        dk_ref[...] = jnp.zeros_like(dk_ref) if len(outs) == 7 else outs[0][...]
        dv_ref[...] = jnp.zeros_like(dv_ref) if len(outs) == 7 else outs[1][...]
        for j, piece in enumerate(pieces):
            k_ref[j] = piece[:, :width]
            kt_ref[j] = piece[:, :width].T
            v_ref[j] = piece[:, width:]

    cosine = cos_ref[...]
    sine = sin_ref[...]
    rows = rot_ref.shape[0]
    heads = [slice(h * width, (h + 1) * width) for h in range(HEADS_PER_STEP)]
    inners = []
    for cols in heads:
        inner = (grad_ref[:, cols].astype(F32) * att_ref[:, cols].astype(F32)).T
        inners.append(jnp.sum(inner, axis=0, keepdims=True))

    def step(t, dqs):
        chunk = list_ref[t]
        key = k_ref[chunk]
        key_t = kt_ref[chunk]
        value = v_ref[chunk]
        all_scores = [dot_nt(key, rot_ref[:, cols]) for cols in heads]
        backs = [dot_nt(value, grad_ref[:, cols]) for cols in heads]
        dv = dv_ref[chunk]
        dk = dk_ref[chunk]
        out = []
        for h, cols in enumerate(heads):
            probs = jnp.exp2(all_scores[h] * factor - lse_ref[h])
            score_grad = (probs * (backs[h] - inners[h])).astype(BF)
            dv = dv + dot_nn(probs.astype(BF), grad_ref[:, cols])
            dk = dk + dot_nn(score_grad, rot_ref[:, cols])
            out.append(dqs[h] + dot_nn(key_t, score_grad))
        dv_ref[chunk] = dv
        dk_ref[chunk] = dk
        return out

    dqs = lax.fori_loop(0, list_ref[2 * rows_n], step, [jnp.zeros((width, rows), F32)] * HEADS_PER_STEP)
    for h, cols in enumerate(heads):
        dq = dqs[h].T * scale
        qpg_ref[:, cols] = (dq * cosine - pltpu.roll(dq, width // 2, 1) * sine).astype(BF)


def attend_back(meta, rot, grad, att, lse, cosine, sine, kv, width, rows_n, running=()):
    where, seq_ids, block_ids = meta
    rows, columns = rot.shape
    heads = columns // width
    chunks = len(kv)
    span = HEADS_PER_STEP * width
    whole2 = lambda i, m: (0, 0)
    whole3 = lambda i, m: (0, 0, 0)
    by_head = lambda i, m: (0, i)
    return pl.pallas_call(
        functools.partial(
            attend_back_body,
            factor=width**-0.5 * LOG2E,
            scale=width**-0.5,
            width=width,
            rows_n=rows_n,
        ),
        grid_spec=pltpu.PrefetchScalarGridSpec(
            num_scalar_prefetch=1,
            grid=(heads // HEADS_PER_STEP,),
            in_specs=[
                pl.BlockSpec(memory_space=pltpu.SMEM),
                pl.BlockSpec(memory_space=pltpu.SMEM),
                pl.BlockSpec((rows, span), by_head),
                pl.BlockSpec((rows, span), by_head),
                pl.BlockSpec((rows, span), by_head),
                pl.BlockSpec((HEADS_PER_STEP, 1, rows), lambda i, m: (i, 0, 0)),
                pl.BlockSpec((rows, width), whole2),
                pl.BlockSpec((rows, width), whole2),
            ]
            + [pl.BlockSpec((rows, 2 * width), whole2)] * chunks
            + [pl.BlockSpec((chunks, rows, width), whole3)] * len(running),
            out_specs=[
                pl.BlockSpec((rows, span), by_head),
                pl.BlockSpec((chunks, rows, width), whole3),
                pl.BlockSpec((chunks, rows, width), whole3),
            ],
            scratch_shapes=[
                pltpu.SMEM((chunks + 1,), jnp.int32),
                pltpu.VMEM((chunks, rows, width), BF),
                pltpu.VMEM((chunks, width, rows), BF),
                pltpu.VMEM((chunks, rows, width), BF),
            ],
        ),
        out_shape=[
            jax.ShapeDtypeStruct((rows, columns), BF),
            jax.ShapeDtypeStruct((chunks, rows, width), F32),
            jax.ShapeDtypeStruct((chunks, rows, width), F32),
        ],
        cost_estimate=pl.CostEstimate(
            flops=10 * rows * columns * chunks * rows // 2,
            transcendentals=heads * rows * chunks * rows // 2,
            bytes_accessed=8 * rows * columns + 12 * chunks * rows * width,
        ),
        name="attend_back",
    )(where, seq_ids, block_ids, rot, grad, att, lse, cosine, sine, *kv, *running)


def feed_body(*refs, rows_n, parts, near, shared):
    R = rows_n
    refs = list(refs)
    take = lambda n: [refs.pop(0) for _ in range(n)]
    normed = take(parts * R)
    grads = take(R)
    close_in, close_down = take(near), take(near)
    far_in = take(1 if shared[0] else R - near)
    far_down = take(1 if shared[1] else R - near)
    act_ref, gate_grad_ref, up_grad_ref = take(3)
    back_refs = take(R)
    normed_out, grads_out = take(2)
    x_ref, g_ref, wg_ref, wu_ref, wd_ref, x_sem, g_sem, w_sem, o_sem = refs
    step = pl.program_id(0)
    tile, span = normed[0].shape

    def x_copy(p, k):
        return pltpu.make_async_copy(
            normed[p * R + k], x_ref.at[p, :, pl.ds(k * span, span)], x_sem.at[p, k]
        )

    def g_copy(p, k):
        return pltpu.make_async_copy(
            grads[k].at[pl.ds(p * tile, tile)], g_ref.at[p, :, pl.ds(k * span, span)], g_sem.at[p, k]
        )

    def w_copies(j, k):
        target = (wg_ref, wu_ref, wd_ref)[j]
        if k < near or not shared[j // 2]:
            whole = (close_in + far_in, close_down + far_down)[j // 2][k]
            whole = whole if j == 2 else whole.at[j]
            place = target.at[:, pl.ds(k * span, span)]
            return [pltpu.make_async_copy(whole, place, w_sem.at[j, k, 0])]
        source = far_down[0] if j == 2 else far_in[0]
        copies = []
        for z in range(source.shape[0]):
            if j == 2:
                size = source.shape[-2]
                share = source.at[z, k - near]
                place = target.at[pl.ds(z * size, size), pl.ds(k * span, span)]
            else:
                size = source.shape[-1]
                share = source.at[z, k - near, j]
                place = target.at[:, pl.ds(k * span + z * size, size)]
            copies.append(pltpu.make_async_copy(share, place, w_sem.at[j, k, z]))
        return copies

    def x_out(p):
        return pltpu.make_async_copy(
            x_ref.at[p], normed_out.at[pl.ds(p * tile, tile)], o_sem.at[0, p]
        )

    def g_out(p):
        return pltpu.make_async_copy(
            g_ref.at[p], grads_out.at[pl.ds(p * tile, tile)], o_sem.at[1, p]
        )

    @pl.when(step == 0)
    def _():
        weights = [w_copies(j, k) for j in range(3) for k in range(R)]
        for k in range(R):
            x_copy(0, k).start()
            g_copy(0, k).start()
        for group in weights:
            for copy in group:
                copy.start()
        for p in range(1, parts):
            for k in range(R):
                x_copy(p, k).start()
                g_copy(p, k).start()
        for k in range(R):
            x_copy(0, k).wait()
            g_copy(0, k).wait()
        for group in weights:
            for copy in group:
                copy.wait()
        x_out(0).start()
        g_out(0).start()

    for p in range(1, parts):

        @pl.when(step == p)
        def _(p=p):
            for k in range(R):
                x_copy(p, k).wait()
                g_copy(p, k).wait()
            x_out(p).start()
            g_out(p).start()

    gate = dot_nt(x_ref[step], wg_ref[...])
    up = dot_nt(x_ref[step], wu_ref[...])
    mixed_grad = dot_nt(g_ref[step], wd_ref[...])
    sig = 1.0 / (1.0 + jnp.exp(-gate))
    silu = gate * sig
    act_ref[...] = (silu * up).astype(BF)
    gate_grad = (mixed_grad * up * sig * (1.0 + gate * (1.0 - sig))).astype(BF)
    up_grad = (mixed_grad * silu).astype(BF)
    gate_grad_ref[...] = gate_grad
    up_grad_ref[...] = up_grad
    for k in range(R):
        here = slice(k * span, (k + 1) * span)
        back = dot_nn(gate_grad, wg_ref[:, here]) + dot_nn(up_grad, wu_ref[:, here])
        back_refs[k][...] = back.astype(BF)

    @pl.when(step == parts - 1)
    def _():
        for p in range(parts):
            x_out(p).wait()
            g_out(p).wait()


def feed(normed, grads, close_in, close_down, far_in, far_down, shared, slots):
    parts = len(normed)
    R = len(grads)
    near = len(close_in)
    tile, span = normed[0][0].shape
    hidden_n = close_in[0].shape[1]
    total = parts * tile
    operands = [a for p in normed for a in p] + list(grads)
    operands += [*close_in, *close_down, *far_in, *far_down]
    by_tile = pl.BlockSpec((tile, hidden_n), lambda i: (i, 0))
    anywhere = pl.BlockSpec(memory_space=pl.ANY)
    return pl.pallas_call(
        functools.partial(feed_body, rows_n=R, parts=parts, near=near, shared=shared),
        grid=(parts,),
        in_specs=[anywhere] * len(operands),
        out_specs=[by_tile] * 3
        + [pl.BlockSpec((tile, span), lambda i: (i, 0))] * R
        + [anywhere] * 2,
        out_shape=[jax.ShapeDtypeStruct((total, hidden_n), BF)] * 3
        + [jax.ShapeDtypeStruct((total, span), BF)] * R
        + [jax.ShapeDtypeStruct((total, R * span), BF)] * 2,
        scratch_shapes=[
            pltpu.VMEM((parts, tile, R * span), BF),
            pltpu.VMEM((parts, tile, R * span), BF),
            pltpu.VMEM((hidden_n, R * span), BF),
            pltpu.VMEM((hidden_n, R * span), BF),
            pltpu.VMEM((hidden_n, R * span), BF),
            pltpu.SemaphoreType.DMA((parts, R)),
            pltpu.SemaphoreType.DMA((parts, R)),
            pltpu.SemaphoreType.DMA((3, R, slots)),
            pltpu.SemaphoreType.DMA((2, parts)),
        ],
        compiler_params=pltpu.CompilerParams(vmem_limit_bytes=56 << 20),
        cost_estimate=pl.CostEstimate(
            flops=10 * total * R * span * hidden_n,
            transcendentals=total * hidden_n,
            bytes_accessed=10 * total * R * span + 6 * R * span * hidden_n,
        ),
        name="feed",
    )(*operands)


def feed_weight_body(x0, x1, g0, g1, out_ref):
    total = (dot_tn(g0[...], x0[...]) + dot_tn(g1[...], x1[...])).astype(BF)
    share = out_ref.shape[3]
    for q in range(out_ref.shape[0]):
        out_ref[q, 0] = total[:, q * share : (q + 1) * share]


def feed_weight_grad(x, grads, rows_n, dp_n):
    tokens, features = x[0].shape
    span = features // rows_n
    hidden_n = grads[0].shape[1]
    return pl.pallas_call(
        feed_weight_body,
        grid=(rows_n,),
        in_specs=[pl.BlockSpec((tokens, span), lambda k: (0, k))] * 2
        + [pl.BlockSpec((tokens, hidden_n), lambda k: (0, 0))] * 2,
        out_specs=pl.BlockSpec((dp_n, 1, hidden_n, span // dp_n), lambda k: (0, k, 0, 0)),
        out_shape=jax.ShapeDtypeStruct((dp_n, rows_n, hidden_n, span // dp_n), BF),
        compiler_params=pltpu.CompilerParams(vmem_limit_bytes=48 << 20),
        cost_estimate=pl.CostEstimate(
            flops=4 * tokens * features * hidden_n,
            transcendentals=0,
            bytes_accessed=4 * tokens * (features + hidden_n) + 2 * features * hidden_n,
        ),
        name="feed_weights",
    )(*x, *grads)


def down_weight_body(a0, a1, g0, g1, out_ref):
    total = (dot_tn(a0[...], g0[...]) + dot_tn(a1[...], g1[...])).astype(BF)
    part = out_ref.shape[2]
    for q in range(out_ref.shape[0]):
        out_ref[q, 0] = total[q * part : (q + 1) * part]


def down_weight_grad(acts, grads, rows_n, dp_n):
    tokens, features = grads[0].shape
    span = features // rows_n
    hidden_n = acts[0].shape[1]
    part = hidden_n // dp_n
    return pl.pallas_call(
        down_weight_body,
        grid=(rows_n,),
        in_specs=[pl.BlockSpec((tokens, hidden_n), lambda k: (0, 0))] * 2
        + [pl.BlockSpec((tokens, span), lambda k: (0, k))] * 2,
        out_specs=pl.BlockSpec((dp_n, 1, part, span), lambda k: (0, k, 0, 0)),
        out_shape=jax.ShapeDtypeStruct((dp_n, rows_n, part, span), BF),
        compiler_params=pltpu.CompilerParams(vmem_limit_bytes=48 << 20),
        cost_estimate=pl.CostEstimate(
            flops=4 * tokens * features * hidden_n,
            transcendentals=0,
            bytes_accessed=4 * tokens * (features + hidden_n) + 2 * features * hidden_n,
        ),
        name="down_weights",
    )(*acts, *grads)


def late_weight_body(x0, x1, u0, u1, g0, g1, a0, a1, out_ref, *, rows_n):
    planes, _, _, rows, share = out_ref.shape

    @pl.when(pl.program_id(0) < rows_n)
    def _():
        total = (dot_tn(u0[...], x0[...]) + dot_tn(u1[...], x1[...])).astype(BF)
        for q in range(planes):
            out_ref[q, 0, 0] = total[:, q * share : (q + 1) * share]

    @pl.when(pl.program_id(0) >= rows_n)
    def _():
        total = (dot_tn(a0[...], g0[...]) + dot_tn(a1[...], g1[...])).astype(BF)
        part = rows // planes
        for q in range(planes):
            for j in range(planes):
                out_ref[q, 0, 0, j * part : (j + 1) * part] = total[
                    q * part : (q + 1) * part, j * share : (j + 1) * share
                ]


def late_weight_grads(x, ups, grads, acts, rows_n, dp_n):
    tokens, features = x[0].shape
    span = features // rows_n
    hidden_n = ups[0].shape[1]
    share = span // dp_n
    whole = pl.BlockSpec((tokens, hidden_n), lambda i: (0, 0))
    first = pl.BlockSpec((tokens, span), lambda i: (0, jnp.minimum(i, rows_n - 1)))
    second = pl.BlockSpec((tokens, span), lambda i: (0, jnp.maximum(i - rows_n, 0)))
    return pl.pallas_call(
        functools.partial(late_weight_body, rows_n=rows_n),
        grid=(2 * rows_n,),
        in_specs=[first] * 2 + [whole] * 2 + [second] * 2 + [whole] * 2,
        out_specs=pl.BlockSpec(
            (dp_n, 1, 1, hidden_n, share), lambda i: (0, i // rows_n, i % rows_n, 0, 0)
        ),
        out_shape=jax.ShapeDtypeStruct((dp_n, 2, rows_n, hidden_n, share), BF),
        compiler_params=pltpu.CompilerParams(vmem_limit_bytes=56 << 20),
        cost_estimate=pl.CostEstimate(
            flops=8 * tokens * features * hidden_n,
            transcendentals=0,
            bytes_accessed=8 * tokens * (features + hidden_n) + 4 * features * hidden_n,
        ),
        name="late_weights",
    )(*x, *ups, *grads, *acts)


def product_body(a0, a1, *refs, near):
    half = len(refs) // 3
    outs = refs[half:]
    for k in range(half):

        @pl.when(pl.program_id(0) == k)
        def _(k=k):
            weight = refs[k][...].reshape(a0.shape[1], outs[0].shape[1])
            outs[2 * k][...] = dot_nn(a0[...], weight).astype(BF)
            outs[2 * k + 1][...] = dot_nn(a1[...], weight).astype(BF)


def down_products(acts, close_down, far_down, rows_n):
    tokens, hidden_n = acts[0].shape
    span = close_down[0].shape[1]
    near = len(close_down)
    act = pl.BlockSpec((tokens, hidden_n), lambda i: (0, 0))
    ins, operands = [act] * 2, list(acts)
    for k in range(rows_n):
        if k < near or len(far_down) > 1:
            ins.append(pl.BlockSpec((hidden_n, span), lambda i: (0, 0)))
            operands.append(close_down[k] if k < near else far_down[k - near])
        else:
            planes, _, rows, _ = far_down[0].shape
            ins.append(
                pl.BlockSpec((planes, 1, rows, span), lambda i, k=k: (0, k - near, 0, 0))
            )
            operands.append(far_down[0])
    out = pl.pallas_call(
        functools.partial(product_body, near=near),
        grid=(rows_n,),
        in_specs=ins,
        out_specs=[pl.BlockSpec((tokens, span), lambda i: (0, 0))] * (2 * rows_n),
        out_shape=[jax.ShapeDtypeStruct((tokens, span), BF)] * (2 * rows_n),
        compiler_params=pltpu.CompilerParams(vmem_limit_bytes=56 << 20),
        name="down_products",
    )(*operands)
    return {(a, k): out[2 * k + a] for k in range(rows_n) for a in range(2)}


def finish_body(where, *refs, rows_n, dp_n):
    pieces = refs[:rows_n]
    gate_ref, up_ref, down_ref = refs[rows_n:]
    part = pieces[0].shape[1] // dp_n
    share = pieces[0].shape[2]
    for k in range(rows_n):
        sender = where[0] ^ k
        for i in range(rows_n):

            @pl.when(sender == i)
            def _(k=k, i=i):
                for q in range(dp_n):
                    rows = slice(q * part, (q + 1) * part)
                    here = slice((q * rows_n + i) * part, (q * rows_n + i + 1) * part)
                    gate_ref[:, here] = pieces[k][0, rows].astype(F32).T
                    up_ref[:, here] = pieces[k][1, rows].astype(F32).T
                    down_ref[i * part : (i + 1) * part, q * share : (q + 1) * share] = pieces[k][
                        2, rows
                    ].astype(F32)


def finish_weight_grads(where, pieces, rows_n, dp_n):
    _, hidden_n, share = pieces[0].shape
    spec = pl.BlockSpec((3, hidden_n, share), lambda i, w: (0, 0, 0))
    shapes = [(share, rows_n * hidden_n)] * 2 + [(hidden_n, dp_n * share)]
    return pl.pallas_call(
        functools.partial(finish_body, rows_n=rows_n, dp_n=dp_n),
        grid_spec=pltpu.PrefetchScalarGridSpec(
            num_scalar_prefetch=1,
            grid=(1,),
            in_specs=[spec] * rows_n,
            out_specs=[pl.BlockSpec(shape, lambda i, w: (0, 0)) for shape in shapes],
        ),
        out_shape=[jax.ShapeDtypeStruct(shape, F32) for shape in shapes],
        compiler_params=pltpu.CompilerParams(vmem_limit_bytes=40 << 20),
        name="finish_weights",
    )(where, *pieces)


def cut_body(where, *refs, ks, rows_n, dp_n):
    gate, up = refs[:2]
    outs = refs[len(refs) - 2 * len(ks) :]
    down_in = refs[2 : len(refs) - 2 * len(ks)]
    part = gate.shape[1] // (dp_n * rows_n)
    for n, k in enumerate(ks):
        slot = where[0] ^ k
        for i in range(rows_n):

            @pl.when(slot == i)
            def _(n=n, i=i):
                for q in range(dp_n):
                    here = slice((q * rows_n + i) * part, (q * rows_n + i + 1) * part)
                    there = slice(q * part, (q + 1) * part)
                    outs[2 * n][0, there] = gate[:, here].T
                    outs[2 * n][1, there] = up[:, here].T
                    if len(down_in) < len(ks):
                        outs[2 * n + 1][there] = down_in[0][here]

        if len(down_in) == len(ks):
            outs[2 * n + 1][...] = down_in[n][...]


def cut_weights(where, w_gate, w_up, w_down, ks, rows_n, dp_n, rows_in, rows_down):
    hidden_n = w_gate.shape[1] // rows_n
    part = hidden_n // dp_n
    span = w_down.shape[1]
    ins = [pl.BlockSpec((rows_in, w_gate.shape[1]), lambda i, w: (w[1], 0))] * 2
    if rows_down == part:
        for k in ks:
            ins.append(pl.BlockSpec((part, span), lambda i, w, k=k: (w[2] * rows_n + (w[0] ^ k), 0)))
    else:
        ins.append(pl.BlockSpec(w_down.shape, lambda i, w: (0, 0)))
    out_specs, out_shape = [], []
    for _ in ks:
        out_specs += [
            pl.BlockSpec((2, hidden_n, rows_in), lambda i, w: (0, 0, 0)),
            pl.BlockSpec((rows_down, span), lambda i, w: (0, 0)),
        ]
        out_shape += [
            jax.ShapeDtypeStruct((2, hidden_n, rows_in), BF),
            jax.ShapeDtypeStruct((rows_down, span), BF),
        ]
    out = pl.pallas_call(
        functools.partial(cut_body, ks=ks, rows_n=rows_n, dp_n=dp_n),
        grid_spec=pltpu.PrefetchScalarGridSpec(
            num_scalar_prefetch=1, grid=(1,), in_specs=ins, out_specs=out_specs
        ),
        out_shape=out_shape,
        compiler_params=pltpu.CompilerParams(vmem_limit_bytes=40 << 20),
        name="cut_weights",
    )(where, w_gate, w_up, *([w_down] * (len(ins) - 2)))
    return out[0::2], out[1::2]


def cut_plain(row, w_gate, w_up, w_down, ks, rows_n, dp_n):
    part = w_gate.shape[1] // (dp_n * rows_n)
    cut_in, cut_down = [], []
    for k in ks:
        starts = [(q * rows_n + (row ^ k)) * part for q in range(dp_n)]
        both = []
        for w in (w_gate.T, w_up.T):
            both.append(jnp.concatenate([lax.dynamic_slice_in_dim(w, at, part, 0) for at in starts]))
        cut_in.append(jnp.stack(both))
        cut_down.append(
            jnp.concatenate([lax.dynamic_slice_in_dim(w_down, at, part, 0) for at in starts])
        )
    return cut_in, cut_down


def tie(value, *others):
    return lax.optimization_barrier((value, others))[0]


def per_device(
    rows_n,
    tokens,
    seq_ids,
    block_ids,
    positions,
    norm1_gain,
    norm2_gain,
    w_query,
    w_kv,
    w_out,
    w_gate,
    w_up,
    w_down,
    grad_output,
):
    R = rows_n
    bits = []
    while (1 << len(bits)) < R:
        bits.append(1 << len(bits))
    nbits = len(bits)

    def reverse(v):
        out = 0
        for b in range(nbits):
            out = out | (((v >> b) & 1) << (nbits - 1 - b))
        return out

    order = [reverse(v) for v in range(R)]
    row = lax.axis_index("row")
    col = lax.axis_index("col")
    half_rows, dslice = tokens.shape
    B = half_rows // R
    full_rows = 2 * half_rows
    width = w_kv.shape[1] // 2
    dp_n = lax.axis_size("dp")

    def tf(flag, value, *others):
        return tie(value, *others) if FL.get(flag, 0) else value

    def tc(flag, value, *options):
        k = FL.get(flag, 0)
        return tie(value, options[k - 1]) if k else value

    def swap_row(a, bit):
        return lax.ppermute(a, "row", [(i, i ^ bit) for i in range(R)])

    def swap_col(a):
        return lax.ppermute(a, "col", [(0, 1), (1, 0)])

    def psum_row(a):
        for bit in bits:
            a = a + swap_row(a, bit)
        return a

    def pick(a, index, size):
        return lax.dynamic_slice_in_dim(a, index * size, size, 0)

    def to_order(a):
        return jnp.concatenate([pick(a, row ^ order[p], B) for p in range(R)], axis=0)

    def from_order(a):
        return jnp.concatenate([pick(a, reverse(row ^ b), B) for b in range(R)], axis=0)

    def reduce_row(a, send_after=(), use_after=()):
        a = a.astype(BF)
        for bit in bits:
            half = a.shape[0] // 2
            keep, send = a[:half], a[half:]
            if bit == bits[-1]:
                send = tie(send, send_after)
            came = swap_row(send, bit)
            if bit == bits[-1]:
                came = tie(came, use_after)
            total = keep.astype(F32) + came.astype(F32)
            a = total.astype(BF)
        return total

    def gather_outer(a):
        for bit in reversed(bits[1:]):
            a = jnp.concatenate([a, swap_row(a, bit)], axis=0)
        return a

    def gather_core(a):
        return jnp.concatenate([a, swap_row(a, 1)], axis=0)

    def gather_row(a):
        return gather_core(gather_outer(a))

    def spread(pieces, bit):
        out = dict(pieces)
        for (a, k), value in pieces.items():
            out[(a, k ^ bit)] = swap_row(value, bit)
        return out

    def spread_col(pieces):
        out = dict(pieces)
        for (a, k), value in pieces.items():
            out[(1 - a, k)] = swap_col(value)
        return out

    half = half_rows // 2

    def gather_plane(mine):
        first = came = spread_col({(0, 0): mine[:half]})
        for bit in reversed(bits[1:]):
            first = spread(first, bit)
        second = {(0, 0): mine[half:]}
        for bit in reversed(bits[1:]):
            second = spread(second, bit)
        second = spread_col(second)
        return (spread(first, 1), spread(second, 1)), came

    def add(a, b, wide=False):
        total = a.astype(F32) + b.astype(F32)
        return total if wide else total.astype(BF)

    def plane_core(blocks):
        moved = {(a, k): swap_row(blocks[(a, k ^ 1)], 1) for a in (1, 0) for k in range(0, R, 2)}
        halves = (slice(0, half), slice(half, 2 * half))
        return [{key: add(blocks[key][h], value[h]) for key, value in moved.items()} for h in halves]

    def plane_rest(parts, after=((), ()), then=(), use_after=()):
        def by_col(cur, last, use_after=()):
            return {
                (0, k): add(v, tie(swap_col(cur[(1, k)]), use_after), last)
                for (a, k), v in cur.items()
                if a == 0
            }

        def by_rows(cur, last, use_after=()):
            for bit in bits[1:]:
                cur = {
                    (a, k): add(
                        v, tie(swap_row(cur[(a, k ^ bit)], bit), use_after), last and bit == bits[-1]
                    )
                    for (a, k), v in cur.items()
                    if not k & bit
                }
            return cur

        first = by_col(tie(parts[0], after[0]), False, use_after)
        second = by_rows(tie(parts[1], after[1]), False, use_after)
        outs = [by_rows(tie(first, then), True), by_col(tie(second, then), True)]
        return jnp.concatenate([o[(0, 0)] for o in outs], axis=0)

    residual = tokens.astype(F32)
    scale_one = lax.rsqrt(psum_row(jnp.sum(residual * residual, axis=1)) / D + EPS)
    weighted_in = (residual * norm1_gain[None, :]).astype(BF)
    ordered_in = to_order(weighted_in)
    w_query_far = swap_col(w_query)
    own = col * R + row
    own_scale = lax.dynamic_slice_in_dim(scale_one, row * B, B)[:, None]

    kv_pre = reduce_row(dot_nn(ordered_in, w_kv)) * own_scale
    query_near = reduce_row(dot_nn(ordered_in, w_query)) * own_scale

    z = lax.axis_index("dp")
    near = min(2, R)
    hidden_n = w_gate.shape[1] // R
    shared = (dslice % (128 * dp_n) == 0, hidden_n % (16 * dp_n) == 0)
    shared = (all(shared), all(shared))
    rows_in = dslice // dp_n if shared[0] else dslice
    rows_down = hidden_n // dp_n if shared[1] else hidden_n

    shares = jnp.stack([row, z if shared[0] else 0 * z, z if shared[1] else 0 * z])
    shares = tie(shares, kv_pre)
    far_ks = tuple(range(near, R))
    part = hidden_n // dp_n
    if part % 16 == 0:
        cut_in, cut_down = cut_weights(shares, w_gate, w_up, w_down, far_ks, R, dp_n, rows_in, rows_down)
    else:
        cut_in, cut_down = cut_plain(row, w_gate, w_up, w_down, far_ks, R, dp_n)
    half_width = width // 2
    frequency = ROPE_BASE ** (-2.0 * jnp.arange(half_width, dtype=F32) / width)
    own_positions = lax.dynamic_slice_in_dim(positions, own * B, B)
    angles = own_positions.astype(F32)[:, None] * frequency[None, :]
    cosine = jnp.concatenate([jnp.cos(angles)] * 2, axis=1)
    sine_half = jnp.sin(angles)
    sine = jnp.concatenate([-sine_half, sine_half], axis=1)

    key_pre = kv_pre[:, :width]
    key_turned = jnp.concatenate([key_pre[:, half_width:], key_pre[:, :half_width]], axis=1)
    key_own = key_pre * cosine + key_turned * sine
    kv_own = jnp.concatenate([key_own, kv_pre[:, width:]], axis=1).astype(BF)
    kv_pieces = spread_col({(0, 0): kv_own})
    for bit in reversed(bits):
        kv_pieces = spread(kv_pieces, bit)
    kv_all = [kv_pieces[(a, k)] for a in range(2) for k in range(R)]
    meta = (jnp.stack([row, col]), seq_ids, block_ids)
    far_in = [swap_row(a, k) for a, k in zip(tf("f11", cut_in, kv_all), far_ks)]
    far_cut_down = cut_down
    if shared[0]:
        far_in = [jnp.stack(far_in)]
    w_out_far = swap_col(tc("f13", w_out, w_query_far, query_near, kv_pre))
    query_near = tf("f0", query_near, w_out_far)
    query_near = tf("f1", query_near, far_in)
    close_ks = tuple(range(near))
    if part % 16 == 0:
        shares = shares * jnp.array([1, 0, 0], jnp.int32)
        cut_in, cut_down = cut_weights(shares, w_gate, w_up, w_down, close_ks, R, dp_n, dslice, hidden_n)
    else:
        cut_in, cut_down = cut_plain(row, w_gate, w_up, w_down, close_ks, R, dp_n)
    close_in = [swap_row(a, k) if k else a for k, a in enumerate(cut_in)]
    close_down = [swap_row(a, k) if k else a for k, a in enumerate(cut_down)]
    query_near_raw = query_near
    down_grad = grad_output.astype(BF)
    part_qfar = dot_nn(ordered_in, w_query_far).astype(BF)
    if FL.get("f5", 0) < 3:
        grad_pieces = {(0, 0): tc("f5", down_grad, kv_pre, query_near)}
        for bit in reversed(bits[1:]):
            grad_pieces = spread(grad_pieces, bit)
        query_near = tf("f15", query_near, grad_pieces[(0, bits[-1])])
    att_near, rot_near, lse_near = attend(meta, query_near, cosine, sine, kv_all, width, R)
    if FL.get("f5", 0) >= 3:
        grad_pieces = {(0, 0): tie(down_grad, att_near)}
        for bit in reversed(bits[1:]):
            grad_pieces = spread(grad_pieces, bit)
    grad_rows = dict(grad_pieces)
    for (a, k), value in grad_rows.items():
        if k:
            grad_pieces[(1, k)] = swap_col(value)
        else:
            grad_pieces[(1, k)] = swap_col(tc("f12", down_grad, w_query_far, query_near_raw, w_out_far, att_near))
    query_far = reduce_row(
        part_qfar,
        send_after=query_near_raw if FL.get("f9", 0) else (),
        use_after=(att_near, close_in),
    )
    query_far = tf("f2", query_far, grad_pieces[(1, 0)])
    query_far = tf("f3", query_far, far_in)
    query_far = tf("f4", query_far, w_out_far)
    query_far = tf("f8", query_far, grad_rows) * own_scale
    if shared[0]:
        far_in = [lax.all_gather(far_in[0], "dp", axis=0)]
    near_outer = gather_outer(att_near)
    query_far = tf("f16", query_far, near_outer)
    att_far, rot_far, lse_far = attend(meta, query_far, cosine, sine, kv_all, width, R)
    far_cut_down = tc("f10", far_cut_down, query_near_raw, att_near, att_far, near_outer)
    far_down = [swap_row(a, k) for a, k in zip(far_cut_down, far_ks)]
    if shared[1]:
        far_down = [lax.all_gather(jnp.stack(far_down), "dp", axis=0)]

    all_near = gather_core(near_outer)
    far_outer = gather_outer(att_far)
    far_outer = tf("f6", far_outer, grad_rows)
    far_outer = tf("f17", far_outer, grad_pieces)
    all_far = gather_core(far_outer)
    hidden = residual + from_order(dot_nn(all_near, w_out) + dot_nn(all_far, w_out_far))

    def exchange(parts):
        return [parts[0]] + [swap_row(parts[k], k) for k in range(1, len(parts))]

    scale_two = lax.rsqrt(psum_row(jnp.sum(hidden * hidden, axis=1)) / D + EPS)[:, None]
    normed_two = (hidden * scale_two * norm2_gain[None, :]).astype(BF)
    normed_pieces, came = gather_plane(tf("f7", normed_two, grad_pieces))
    grad_pieces = spread(tf("f14", grad_pieces, came), 1)

    fed = {}
    backs = {}
    for a in (0, 1):
        fed[a] = feed(
            [[part[(a, k)] for k in range(R)] for part in normed_pieces],
            [grad_pieces[(a, k)] for k in range(R)],
            close_in,
            close_down,
            far_in,
            far_down,
            shared,
            dp_n,
        )
        for k in range(R):
            backs[(a, k)] = fed[a][3 + k]
    acts, gate_grads, up_grads = ([fed[a][j] for a in range(2)] for j in range(3))
    normed_halves, grad_halves = ([fed[a][3 + R + j] for a in range(2)] for j in range(2))
    core_sums = plane_core(backs)
    normed2_grad = None if FL.get("b37", 0) else plane_rest(core_sums)

    def place(pieces):
        moved = jnp.stack(exchange([jnp.stack([p[k] for p in pieces]) for k in range(R)]))
        ordered = [lax.dynamic_index_in_dim(moved, row ^ s, 0, keepdims=False) for s in range(R)]
        return [jnp.stack([o[n] for o in ordered]) for n in range(len(pieces))]

    def ff_input_place(rows):
        rows = rows.reshape(R, dp_n, part, -1).transpose(1, 0, 2, 3)
        return rows.reshape(R * hidden_n, -1).astype(F32).T

    def over_dp(local):
        return lax.psum_scatter(local, "dp", scatter_dimension=0, tiled=True)

    gate_local = feed_weight_grad(normed_halves, gate_grads, R, dp_n)
    gate_piece = over_dp(gate_local)
    if shared[1]:
        late = late_weight_grads(
            normed_halves, tf("b0", tie(up_grads, gate_local), core_sums), grad_halves, acts, R, dp_n
        )
        late_piece = over_dp(tie(late, gate_local))
        if FL.get("b37", 0):
            normed2_grad = plane_rest(core_sums, use_after=late)
        up_piece, down_piece = late_piece[0, 0], late_piece[0, 1]
        normed2_grad = tie(normed2_grad, gate_local, late)
    else:
        late_piece = gate_piece
        normed2_grad = plane_rest(core_sums)
        up_piece = over_dp(feed_weight_grad(normed_halves, up_grads, R, dp_n))[0]
        down_piece = over_dp(down_weight_grad(acts, grad_halves, R, dp_n))[0]

    weighted = normed2_grad * norm2_gain[None, :]
    inner_two = psum_row(jnp.sum(weighted * hidden, axis=1))[:, None]
    hidden_grad = grad_output + (
        scale_two * weighted - hidden * (scale_two * scale_two * scale_two) * inner_two / D
    )
    gain_two = jnp.sum(normed2_grad * hidden * scale_two, axis=0)
    branch_ordered = to_order(hidden_grad.astype(BF))
    part_far = dot_nt(branch_ordered, w_out_far).astype(BF)
    part_near = dot_nt(branch_ordered, w_out).astype(BF)
    prod_dep = FL.get("b5", 0)
    branch_late, late_acts = branch_ordered, acts

    def make_products():
        return down_products(late_acts, close_down, far_down, R)

    if prod_dep < 2:
        late_acts = tie(acts, hidden_grad) if prod_dep == 0 else tie(acts, part_far, part_near)
        products = make_products()
    b6 = FL.get("b6", 0) if prod_dep < 2 else 0
    att_grad_far = reduce_row(part_far, use_after=products if b6 == 1 else ()).astype(BF)
    att_grad_near = reduce_row(
        part_near, send_after=att_grad_far if FL.get("b25", 0) else (), use_after=products if b6 == 2 else ()
    ).astype(BF)
    gout_early = FL.get("b26", 0)
    if gout_early:
        grad_out_far = dot_tn(all_far, branch_late).astype(BF)
        grad_out_came = swap_col(grad_out_far)
        grad_out_near = dot_tn(all_near, branch_late)
        att_grad_far = tf("b27", att_grad_far, grad_out_far, grad_out_near)
        att_grad_far = tf("b4", att_grad_far, grad_out_came)
    att_grad_far = tf("b2", att_grad_far, gate_piece)
    att_grad_far = tf("b3", att_grad_far, att_grad_near)

    qpg_far, dk, dv = attend_back(
        meta, rot_far, att_grad_far, att_far, lse_far, cosine, sine, kv_all, width, R
    )
    if not gout_early:
        branch_late = tie(branch_ordered, qpg_far)
        grad_out_far = dot_tn(all_far, branch_late).astype(BF)
        grad_out_came = swap_col(grad_out_far)
        grad_out_near = dot_tn(all_near, branch_late)
    if prod_dep == 2:
        late_acts = tie(acts, qpg_far)
        products = make_products()
    scale_col = scale_one[:, None]
    normed_ordered = to_order((residual * scale_col * norm1_gain[None, :]).astype(BF))
    qpg_far_outer = gather_outer(tf("b28", qpg_far, grad_out_far))
    qpg_far_all = gather_core(qpg_far_outer)
    qpg_far_used = tf("b8", qpg_far_all, grad_out_near)
    if prod_dep < 3:
        qpg_far_used = tf("b29", qpg_far_used, products)
    grad_query_far = dot_tn(normed_ordered, qpg_far_used).astype(BF)
    grad_query_came = swap_col(grad_query_far)
    att_grad_near = tf("b30", att_grad_near, qpg_far_outer)
    att_grad_near = tf("b7", att_grad_near, grad_query_far)
    att_grad_near = tf("b31", att_grad_near, grad_out_came)
    qpg_near, dk, dv = attend_back(
        meta, rot_near, att_grad_near, att_near, lse_near, cosine, sine, kv_all, width, R,
        (dk, dv),
    )
    if prod_dep == 3:
        late_acts = tie(acts, qpg_near)
        products = make_products()
    grad_out_local = add(grad_out_near, tc("b24", grad_out_came, qpg_far, qpg_near))
    grad_out = over_dp(tc("b18", grad_out_local, gate_piece, late_piece))
    qpg_near_outer = gather_outer(tf("b32", qpg_near, grad_out_local))
    qpg_near_all = gather_core(qpg_near_outer)
    qpg_near_used = tf("b19", tie(qpg_near_all, grad_query_came), late_piece)
    grad_query_near = dot_tn(normed_ordered, qpg_near_used)
    grad_query_local = add(grad_query_near, grad_query_came)
    opts = (qpg_far, qpg_near, qpg_near_outer, grad_query_came, grad_query_local)
    pick_opt = lambda k: () if not k else opts[k - 1]
    down_sum = plane_rest(
        plane_core(products),
        after=(pick_opt(FL.get("b13", 0)), pick_opt(FL.get("b14", 0))),
        then=pick_opt(FL.get("b15", 0)),
    )
    output = hidden + down_sum
    dk, dv = tc("b9", (dk, dv), qpg_near_outer, grad_out_local, grad_query_came, grad_query_local)

    dkv = jnp.concatenate([dk * width**-0.5, dv], axis=2).astype(BF)
    cur = {(a, k): dkv[a * R + k] for a in range(2) for k in range(R)}
    for bit in bits:
        cur = {
            (a, k): add(v, swap_row(cur[(a, k ^ bit)], bit))
            for (a, k), v in cur.items()
            if not k & bit
        }
    dkv_own = cur[(0, 0)].astype(F32) + swap_col(cur[(1, 0)]).astype(F32)
    dk_own = dkv_own[:, :width]
    dk_turned = jnp.concatenate([dk_own[:, half_width:], dk_own[:, :half_width]], axis=1)
    kvg_own = jnp.concatenate(
        [dk_own * cosine - dk_turned * sine, dkv_own[:, width:]], axis=1
    ).astype(BF)


    pieces = tc("b17", (gate_piece[0], up_piece, down_piece), qpg_near, grad_query_local, qpg_near_outer)
    moved = exchange([jnp.stack([p[k] for p in pieces]) for k in range(R)]) if shared[1] else ()
    kvg_own = tf("b36", kvg_own, moved)
    kvg_own = tc("b16", kvg_own, qpg_near_outer, grad_query_came, grad_query_local)
    kvg_all = gather_row(kvg_own)
    normed1_grad = from_order(
        dot_nt(qpg_far_all, w_query_far) + dot_nt(qpg_near_all, w_query) + dot_nt(kvg_all, w_kv)
    )
    normed1_grad = tf("b22", normed1_grad, grad_out)
    normed1_grad = tf("b33", normed1_grad, moved)
    normed1_grad = tf("b34", normed1_grad, grad_query_local)
    normed1_grad = tf("b23", normed1_grad, output)
    weighted_one = normed1_grad * norm1_gain[None, :]
    inner_one = psum_row(jnp.sum(weighted_one * residual, axis=1))[:, None]
    input_grad = hidden_grad + (
        scale_col * weighted_one - residual * (scale_col * scale_col * scale_col) * inner_one / D
    )
    gain_one = jnp.sum(normed1_grad * residual * scale_col, axis=0)

    grad_query = over_dp(tf("b20", grad_query_local, grad_out))
    if shared[1]:
        grad_gate, grad_up, grad_down = finish_weight_grads(meta[0], moved, R, dp_n)
    else:
        gate_rows, up_rows = place(pieces[:2])
        grad_gate, grad_up = ff_input_place(gate_rows), ff_input_place(up_rows)
        grad_down = place(pieces[2:])[0].reshape(hidden_n, dslice).astype(F32)

    rest = dslice // (2 * dp_n)
    gains = jnp.concatenate(
        [g.reshape(dp_n, 2, 1, rest) for g in (gain_one, gain_two)]
        + [jnp.zeros((dp_n, 2, 1, 2 * width - 2 * rest), F32)],
        axis=3,
    )
    local = dot_tn(normed_ordered, kvg_all).reshape(dp_n, 2, rest, 2 * width)
    local = jnp.concatenate([local, gains], axis=2)
    mine = lax.dynamic_index_in_dim(local, col, 1, keepdims=False)
    other = lax.dynamic_index_in_dim(local, 1 - col, 1, keepdims=False).astype(BF)
    both = mine + swap_col(other).astype(F32)
    small = lax.dynamic_index_in_dim(both, z, 0, keepdims=False)
    for j in range(1, dp_n):
        share = lax.dynamic_index_in_dim(both, z ^ j, 0, keepdims=False).astype(BF)
        share = lax.ppermute(share, "dp", [(i, i ^ j) for i in range(dp_n)])
        small = small + share.astype(F32)

    return (
        output,
        input_grad,
        grad_query.astype(F32)[None],
        small[None, :rest],
        grad_out.astype(F32)[None],
        grad_gate[None],
        grad_up[None],
        grad_down[None],
        small[rest:, :rest],
        small[rest:, rest : 2 * rest],
    )


def solution(mesh):
    placed = (
        P(("dp", "col"), "row"),
        P("dp"),
        P("dp"),
        P("dp"),
        P("row"),
        P("row"),
        P("row", "col"),
        P("row", None),
        P("col", "row"),
        P("row", "col"),
        P("row", "col"),
        P("col", "row"),
        P(("dp", "col"), "row"),
    )
    return jax.shard_map(
        functools.partial(per_device, mesh.shape["row"]),
        mesh=mesh,
        in_specs=placed,
        out_specs=(
            P(("dp", "col"), "row"),
            P(("dp", "col"), "row"),
            P("row", "dp", "col"),
            P("row", ("dp", "col"), None),
            P("col", "dp", "row"),
            P("row", "dp", "col"),
            P("row", "dp", "col"),
            P("col", "dp", "row"),
            P("row", ("dp", "col")),
            P("row", ("dp", "col")),
        ),
        check_vma=False,
    )
```

```python
import functools

import jax
import jax.numpy as jnp
from jax import lax
from jax.experimental import pallas as pl
from jax.experimental.pallas import tpu as pltpu
from jax.sharding import PartitionSpec as P

D = 2048
EPS = 1e-05
ROPE_BASE = 500000.0
BLOCK = 256
LOG2E = 1.4426950408889634
BF = jnp.bfloat16
F32 = jnp.float32
HEADS_PER_STEP = 4
FL = {'f11': 0, 'f13': 1, 'f0': 1, 'f1': 1, 'f5': 2, 'f9': 1, 'f12': 2, 'f2': 1, 'f3': 1, 'f4': 0, 'f8': 1, 'f10': 3, 'f6': 1, 'f7': 1, 'f14': 1, 'f15': 0, 'f16': 0, 'f17': 0, 'b0': 1, 'b1': 0, 'b2': 1, 'b3': 0, 'b4': 0, 'b5': 2, 'b6': 0, 'b7': 1, 'b8': 1, 'b29': 0, 'b28': 0, 'b18': 2, 'b19': 1, 'b24': 2, 'b9': 3, 'b13': 5, 'b14': 1, 'b15': 0, 'b16': 3, 'b17': 2, 'b20': 0, 'b22': 0, 'b23': 0, 'b25': 1, 'b26': 1, 'b27': 0, 'b30': 0, 'b31': 0, 'b32': 0, 'b33': 0, 'b34': 0, 'b36': 0, 'b37': 1}


def dot_nn(a, b):
    return lax.dot_general(a, b, (((1,), (0,)), ((), ())), preferred_element_type=F32)


def dot_nt(a, b):
    return lax.dot_general(a, b, (((1,), (1,)), ((), ())), preferred_element_type=F32)


def dot_tn(a, b):
    return lax.dot_general(a, b, (((0,), (0,)), ((), ())), preferred_element_type=F32)


def list_visible(where, seq_ref, block_ref, list_ref, *, rows_n, rows):
    row, col = where[0], where[1]
    chunks = 2 * rows_n
    own = (col * rows_n + row) * rows
    count = jnp.int32(0)
    for j in range(chunks):
        seen = (seq_ref[j * rows] == seq_ref[own]) & (block_ref[j * rows] <= block_ref[own])

        @pl.when(seen)
        def _(j=j, count=count):
            list_ref[count] = ((j // rows_n) ^ col) * rows_n + ((j % rows_n) ^ row)

        count = count + seen.astype(jnp.int32)
    list_ref[chunks] = count


def attend_body(
    where, seq_ref, block_ref, q_ref, cos_ref, sin_ref, *refs, factor, width, rows_n,
):
    pieces = refs[:-6]
    att_ref, rot_ref, lse_ref, list_ref, k_ref, vt_ref = refs[-6:]

    @pl.when(pl.program_id(0) == 0)
    def _():
        list_visible(where, seq_ref, block_ref, list_ref, rows_n=rows_n, rows=q_ref.shape[0])
        for j, piece in enumerate(pieces):
            k_ref[j] = piece[:, :width]
            vt_ref[j] = piece[:, width:].T

    cosine = cos_ref[...]
    sine = sin_ref[...]
    rows = q_ref.shape[0]
    heads = [slice(h * width, (h + 1) * width) for h in range(HEADS_PER_STEP)]
    for cols in heads:
        pre = q_ref[:, cols]
        rot_ref[:, cols] = (pre * cosine + pltpu.roll(pre, width // 2, 1) * sine).astype(BF)

    def step(t, carry):
        chunk = list_ref[t]
        key = k_ref[chunk]
        value_t = vt_ref[chunk]
        all_scores = [dot_nt(key, rot_ref[:, cols]) * factor for cols in heads]
        out = []
        for (top, total, acc), scores in zip(carry, all_scores):
            new_top = jnp.maximum(top, jnp.max(scores, axis=0, keepdims=True))
            decay = jnp.exp2(top - new_top)
            weights = jnp.exp2(scores - new_top)
            total = total * decay + jnp.sum(weights, axis=0, keepdims=True)
            acc = acc * decay + dot_nn(value_t, weights.astype(BF))
            out.append((new_top, total, acc))
        return out

    start = (
        jnp.full((1, rows), -1e30, F32),
        jnp.zeros((1, rows), F32),
        jnp.zeros((width, rows), F32),
    )
    done = lax.fori_loop(0, list_ref[2 * rows_n], step, [start] * HEADS_PER_STEP)
    for head, (top, total, acc) in enumerate(done):
        att_ref[:, heads[head]] = (acc / total).T.astype(BF)
        lse_ref[head] = top + jnp.log2(total)


def attend(meta, q_pre, cosine, sine, kv, width, rows_n):
    where, seq_ids, block_ids = meta
    rows, columns = q_pre.shape
    heads = columns // width
    chunks = len(kv)
    span = HEADS_PER_STEP * width
    whole2 = lambda i, m: (0, 0)
    return pl.pallas_call(
        functools.partial(attend_body, factor=width**-0.5 * LOG2E, width=width, rows_n=rows_n),
        grid_spec=pltpu.PrefetchScalarGridSpec(
            num_scalar_prefetch=1,
            grid=(heads // HEADS_PER_STEP,),
            in_specs=[
                pl.BlockSpec(memory_space=pltpu.SMEM),
                pl.BlockSpec(memory_space=pltpu.SMEM),
                pl.BlockSpec((rows, span), lambda i, m: (0, i)),
                pl.BlockSpec((rows, width), whole2),
                pl.BlockSpec((rows, width), whole2),
            ]
            + [pl.BlockSpec((rows, 2 * width), whole2)] * chunks,
            out_specs=[
                pl.BlockSpec((rows, span), lambda i, m: (0, i)),
                pl.BlockSpec((rows, span), lambda i, m: (0, i)),
                pl.BlockSpec((HEADS_PER_STEP, 1, rows), lambda i, m: (i, 0, 0)),
            ],
            scratch_shapes=[
                pltpu.SMEM((chunks + 1,), jnp.int32),
                pltpu.VMEM((chunks, rows, width), BF),
                pltpu.VMEM((chunks, width, rows), BF),
            ],
        ),
        out_shape=[
            jax.ShapeDtypeStruct((rows, columns), BF),
            jax.ShapeDtypeStruct((rows, columns), BF),
            jax.ShapeDtypeStruct((heads, 1, rows), F32),
        ],
        cost_estimate=pl.CostEstimate(
            flops=4 * rows * columns * chunks * rows // 2,
            transcendentals=heads * rows * chunks * rows // 2,
            bytes_accessed=8 * rows * columns + 4 * chunks * rows * width,
        ),
        name="attend",
    )(where, seq_ids, block_ids, q_pre, cosine, sine, *kv)


def attend_back_body(
    where, seq_ref, block_ref, rot_ref, grad_ref, att_ref, lse_ref, cos_ref, sin_ref,
    *outs, factor, scale, width, rows_n,
):
    pieces, outs = outs[: 2 * rows_n], outs[2 * rows_n :]
    qpg_ref, dk_ref, dv_ref, list_ref, k_ref, kt_ref, v_ref = outs[-7:]

    @pl.when(pl.program_id(0) == 0)
    def _():
        list_visible(where, seq_ref, block_ref, list_ref, rows_n=rows_n, rows=rot_ref.shape[0])
        dk_ref[...] = jnp.zeros_like(dk_ref) if len(outs) == 7 else outs[0][...]
        dv_ref[...] = jnp.zeros_like(dv_ref) if len(outs) == 7 else outs[1][...]
        for j, piece in enumerate(pieces):
            k_ref[j] = piece[:, :width]
            kt_ref[j] = piece[:, :width].T
            v_ref[j] = piece[:, width:]

    cosine = cos_ref[...]
    sine = sin_ref[...]
    rows = rot_ref.shape[0]
    heads = [slice(h * width, (h + 1) * width) for h in range(HEADS_PER_STEP)]
    inners = []
    for cols in heads:
        inner = (grad_ref[:, cols].astype(F32) * att_ref[:, cols].astype(F32)).T
        inners.append(jnp.sum(inner, axis=0, keepdims=True))

    def step(t, dqs):
        chunk = list_ref[t]
        key = k_ref[chunk]
        key_t = kt_ref[chunk]
        value = v_ref[chunk]
        all_scores = [dot_nt(key, rot_ref[:, cols]) for cols in heads]
        backs = [dot_nt(value, grad_ref[:, cols]) for cols in heads]
        dv = dv_ref[chunk]
        dk = dk_ref[chunk]
        out = []
        for h, cols in enumerate(heads):
            probs = jnp.exp2(all_scores[h] * factor - lse_ref[h])
            score_grad = (probs * (backs[h] - inners[h])).astype(BF)
            dv = dv + dot_nn(probs.astype(BF), grad_ref[:, cols])
            dk = dk + dot_nn(score_grad, rot_ref[:, cols])
            out.append(dqs[h] + dot_nn(key_t, score_grad))
        dv_ref[chunk] = dv
        dk_ref[chunk] = dk
        return out

    dqs = lax.fori_loop(0, list_ref[2 * rows_n], step, [jnp.zeros((width, rows), F32)] * HEADS_PER_STEP)
    for h, cols in enumerate(heads):
        dq = dqs[h].T * scale
        qpg_ref[:, cols] = (dq * cosine - pltpu.roll(dq, width // 2, 1) * sine).astype(BF)


def attend_back(meta, rot, grad, att, lse, cosine, sine, kv, width, rows_n, running=()):
    where, seq_ids, block_ids = meta
    rows, columns = rot.shape
    heads = columns // width
    chunks = len(kv)
    span = HEADS_PER_STEP * width
    whole2 = lambda i, m: (0, 0)
    whole3 = lambda i, m: (0, 0, 0)
    by_head = lambda i, m: (0, i)
    return pl.pallas_call(
        functools.partial(
            attend_back_body,
            factor=width**-0.5 * LOG2E,
            scale=width**-0.5,
            width=width,
            rows_n=rows_n,
        ),
        grid_spec=pltpu.PrefetchScalarGridSpec(
            num_scalar_prefetch=1,
            grid=(heads // HEADS_PER_STEP,),
            in_specs=[
                pl.BlockSpec(memory_space=pltpu.SMEM),
                pl.BlockSpec(memory_space=pltpu.SMEM),
                pl.BlockSpec((rows, span), by_head),
                pl.BlockSpec((rows, span), by_head),
                pl.BlockSpec((rows, span), by_head),
                pl.BlockSpec((HEADS_PER_STEP, 1, rows), lambda i, m: (i, 0, 0)),
                pl.BlockSpec((rows, width), whole2),
                pl.BlockSpec((rows, width), whole2),
            ]
            + [pl.BlockSpec((rows, 2 * width), whole2)] * chunks
            + [pl.BlockSpec((chunks, rows, width), whole3)] * len(running),
            out_specs=[
                pl.BlockSpec((rows, span), by_head),
                pl.BlockSpec((chunks, rows, width), whole3),
                pl.BlockSpec((chunks, rows, width), whole3),
            ],
            scratch_shapes=[
                pltpu.SMEM((chunks + 1,), jnp.int32),
                pltpu.VMEM((chunks, rows, width), BF),
                pltpu.VMEM((chunks, width, rows), BF),
                pltpu.VMEM((chunks, rows, width), BF),
            ],
        ),
        out_shape=[
            jax.ShapeDtypeStruct((rows, columns), BF),
            jax.ShapeDtypeStruct((chunks, rows, width), F32),
            jax.ShapeDtypeStruct((chunks, rows, width), F32),
        ],
        cost_estimate=pl.CostEstimate(
            flops=10 * rows * columns * chunks * rows // 2,
            transcendentals=heads * rows * chunks * rows // 2,
            bytes_accessed=8 * rows * columns + 12 * chunks * rows * width,
        ),
        name="attend_back",
    )(where, seq_ids, block_ids, rot, grad, att, lse, cosine, sine, *kv, *running)


def feed_body(*refs, rows_n, parts, near, shared):
    R = rows_n
    refs = list(refs)
    take = lambda n: [refs.pop(0) for _ in range(n)]
    normed = take(parts * R)
    grads = take(R)
    close_in, close_down = take(near), take(near)
    far_in = take(1 if shared[0] else R - near)
    far_down = take(1 if shared[1] else R - near)
    act_ref, gate_grad_ref, up_grad_ref = take(3)
    back_refs = take(R)
    normed_out, grads_out = take(2)
    x_ref, g_ref, wg_ref, wu_ref, wd_ref, x_sem, g_sem, w_sem, o_sem = refs
    step = pl.program_id(0)
    tile, span = normed[0].shape

    def x_copy(p, k):
        return pltpu.make_async_copy(
            normed[p * R + k], x_ref.at[p, :, pl.ds(k * span, span)], x_sem.at[p, k]
        )

    def g_copy(p, k):
        return pltpu.make_async_copy(
            grads[k].at[pl.ds(p * tile, tile)], g_ref.at[p, :, pl.ds(k * span, span)], g_sem.at[p, k]
        )

    def w_copies(j, k):
        target = (wg_ref, wu_ref, wd_ref)[j]
        if k < near or not shared[j // 2]:
            whole = (close_in + far_in, close_down + far_down)[j // 2][k]
            whole = whole if j == 2 else whole.at[j]
            place = target.at[:, pl.ds(k * span, span)]
            return [pltpu.make_async_copy(whole, place, w_sem.at[j, k, 0])]
        source = far_down[0] if j == 2 else far_in[0]
        copies = []
        for z in range(source.shape[0]):
            if j == 2:
                size = source.shape[-2]
                share = source.at[z, k - near]
                place = target.at[pl.ds(z * size, size), pl.ds(k * span, span)]
            else:
                size = source.shape[-1]
                share = source.at[z, k - near, j]
                place = target.at[:, pl.ds(k * span + z * size, size)]
            copies.append(pltpu.make_async_copy(share, place, w_sem.at[j, k, z]))
        return copies

    def x_out(p):
        return pltpu.make_async_copy(
            x_ref.at[p], normed_out.at[pl.ds(p * tile, tile)], o_sem.at[0, p]
        )

    def g_out(p):
        return pltpu.make_async_copy(
            g_ref.at[p], grads_out.at[pl.ds(p * tile, tile)], o_sem.at[1, p]
        )

    @pl.when(step == 0)
    def _():
        weights = [w_copies(j, k) for j in range(3) for k in range(R)]
        for k in range(R):
            x_copy(0, k).start()
            g_copy(0, k).start()
        for group in weights:
            for copy in group:
                copy.start()
        for p in range(1, parts):
            for k in range(R):
                x_copy(p, k).start()
                g_copy(p, k).start()
        for k in range(R):
            x_copy(0, k).wait()
            g_copy(0, k).wait()
        for group in weights:
            for copy in group:
                copy.wait()
        x_out(0).start()
        g_out(0).start()

    for p in range(1, parts):

        @pl.when(step == p)
        def _(p=p):
            for k in range(R):
                x_copy(p, k).wait()
                g_copy(p, k).wait()
            x_out(p).start()
            g_out(p).start()

    gate = dot_nt(x_ref[step], wg_ref[...])
    up = dot_nt(x_ref[step], wu_ref[...])
    mixed_grad = dot_nt(g_ref[step], wd_ref[...])
    sig = 1.0 / (1.0 + jnp.exp(-gate))
    silu = gate * sig
    act_ref[...] = (silu * up).astype(BF)
    gate_grad = (mixed_grad * up * sig * (1.0 + gate * (1.0 - sig))).astype(BF)
    up_grad = (mixed_grad * silu).astype(BF)
    gate_grad_ref[...] = gate_grad
    up_grad_ref[...] = up_grad
    for k in range(R):
        here = slice(k * span, (k + 1) * span)
        back = dot_nn(gate_grad, wg_ref[:, here]) + dot_nn(up_grad, wu_ref[:, here])
        back_refs[k][...] = back.astype(BF)

    @pl.when(step == parts - 1)
    def _():
        for p in range(parts):
            x_out(p).wait()
            g_out(p).wait()


def feed(normed, grads, close_in, close_down, far_in, far_down, shared, slots):
    parts = len(normed)
    R = len(grads)
    near = len(close_in)
    tile, span = normed[0][0].shape
    hidden_n = close_in[0].shape[1]
    total = parts * tile
    operands = [a for p in normed for a in p] + list(grads)
    operands += [*close_in, *close_down, *far_in, *far_down]
    by_tile = pl.BlockSpec((tile, hidden_n), lambda i: (i, 0))
    anywhere = pl.BlockSpec(memory_space=pl.ANY)
    return pl.pallas_call(
        functools.partial(feed_body, rows_n=R, parts=parts, near=near, shared=shared),
        grid=(parts,),
        in_specs=[anywhere] * len(operands),
        out_specs=[by_tile] * 3
        + [pl.BlockSpec((tile, span), lambda i: (i, 0))] * R
        + [anywhere] * 2,
        out_shape=[jax.ShapeDtypeStruct((total, hidden_n), BF)] * 3
        + [jax.ShapeDtypeStruct((total, span), BF)] * R
        + [jax.ShapeDtypeStruct((total, R * span), BF)] * 2,
        scratch_shapes=[
            pltpu.VMEM((parts, tile, R * span), BF),
            pltpu.VMEM((parts, tile, R * span), BF),
            pltpu.VMEM((hidden_n, R * span), BF),
            pltpu.VMEM((hidden_n, R * span), BF),
            pltpu.VMEM((hidden_n, R * span), BF),
            pltpu.SemaphoreType.DMA((parts, R)),
            pltpu.SemaphoreType.DMA((parts, R)),
            pltpu.SemaphoreType.DMA((3, R, slots)),
            pltpu.SemaphoreType.DMA((2, parts)),
        ],
        compiler_params=pltpu.CompilerParams(vmem_limit_bytes=56 << 20),
        cost_estimate=pl.CostEstimate(
            flops=10 * total * R * span * hidden_n,
            transcendentals=total * hidden_n,
            bytes_accessed=10 * total * R * span + 6 * R * span * hidden_n,
        ),
        name="feed",
    )(*operands)


def feed_weight_body(x0, x1, g0, g1, out_ref):
    total = (dot_tn(g0[...], x0[...]) + dot_tn(g1[...], x1[...])).astype(BF)
    share = out_ref.shape[3]
    for q in range(out_ref.shape[0]):
        out_ref[q, 0] = total[:, q * share : (q + 1) * share]


def feed_weight_grad(x, grads, rows_n, dp_n):
    tokens, features = x[0].shape
    span = features // rows_n
    hidden_n = grads[0].shape[1]
    return pl.pallas_call(
        feed_weight_body,
        grid=(rows_n,),
        in_specs=[pl.BlockSpec((tokens, span), lambda k: (0, k))] * 2
        + [pl.BlockSpec((tokens, hidden_n), lambda k: (0, 0))] * 2,
        out_specs=pl.BlockSpec((dp_n, 1, hidden_n, span // dp_n), lambda k: (0, k, 0, 0)),
        out_shape=jax.ShapeDtypeStruct((dp_n, rows_n, hidden_n, span // dp_n), BF),
        compiler_params=pltpu.CompilerParams(vmem_limit_bytes=48 << 20),
        cost_estimate=pl.CostEstimate(
            flops=4 * tokens * features * hidden_n,
            transcendentals=0,
            bytes_accessed=4 * tokens * (features + hidden_n) + 2 * features * hidden_n,
        ),
        name="feed_weights",
    )(*x, *grads)


def down_weight_body(a0, a1, g0, g1, out_ref):
    total = (dot_tn(a0[...], g0[...]) + dot_tn(a1[...], g1[...])).astype(BF)
    part = out_ref.shape[2]
    for q in range(out_ref.shape[0]):
        out_ref[q, 0] = total[q * part : (q + 1) * part]


def down_weight_grad(acts, grads, rows_n, dp_n):
    tokens, features = grads[0].shape
    span = features // rows_n
    hidden_n = acts[0].shape[1]
    part = hidden_n // dp_n
    return pl.pallas_call(
        down_weight_body,
        grid=(rows_n,),
        in_specs=[pl.BlockSpec((tokens, hidden_n), lambda k: (0, 0))] * 2
        + [pl.BlockSpec((tokens, span), lambda k: (0, k))] * 2,
        out_specs=pl.BlockSpec((dp_n, 1, part, span), lambda k: (0, k, 0, 0)),
        out_shape=jax.ShapeDtypeStruct((dp_n, rows_n, part, span), BF),
        compiler_params=pltpu.CompilerParams(vmem_limit_bytes=48 << 20),
        cost_estimate=pl.CostEstimate(
            flops=4 * tokens * features * hidden_n,
            transcendentals=0,
            bytes_accessed=4 * tokens * (features + hidden_n) + 2 * features * hidden_n,
        ),
        name="down_weights",
    )(*acts, *grads)


def late_weight_body(x0, x1, u0, u1, g0, g1, a0, a1, out_ref, *, rows_n):
    planes, _, _, rows, share = out_ref.shape

    @pl.when(pl.program_id(0) < rows_n)
    def _():
        total = (dot_tn(u0[...], x0[...]) + dot_tn(u1[...], x1[...])).astype(BF)
        for q in range(planes):
            out_ref[q, 0, 0] = total[:, q * share : (q + 1) * share]

    @pl.when(pl.program_id(0) >= rows_n)
    def _():
        total = (dot_tn(a0[...], g0[...]) + dot_tn(a1[...], g1[...])).astype(BF)
        part = rows // planes
        for q in range(planes):
            for j in range(planes):
                out_ref[q, 0, 0, j * part : (j + 1) * part] = total[
                    q * part : (q + 1) * part, j * share : (j + 1) * share
                ]


def late_weight_grads(x, ups, grads, acts, rows_n, dp_n):
    tokens, features = x[0].shape
    span = features // rows_n
    hidden_n = ups[0].shape[1]
    share = span // dp_n
    whole = pl.BlockSpec((tokens, hidden_n), lambda i: (0, 0))
    first = pl.BlockSpec((tokens, span), lambda i: (0, jnp.minimum(i, rows_n - 1)))
    second = pl.BlockSpec((tokens, span), lambda i: (0, jnp.maximum(i - rows_n, 0)))
    return pl.pallas_call(
        functools.partial(late_weight_body, rows_n=rows_n),
        grid=(2 * rows_n,),
        in_specs=[first] * 2 + [whole] * 2 + [second] * 2 + [whole] * 2,
        out_specs=pl.BlockSpec(
            (dp_n, 1, 1, hidden_n, share), lambda i: (0, i // rows_n, i % rows_n, 0, 0)
        ),
        out_shape=jax.ShapeDtypeStruct((dp_n, 2, rows_n, hidden_n, share), BF),
        compiler_params=pltpu.CompilerParams(vmem_limit_bytes=56 << 20),
        cost_estimate=pl.CostEstimate(
            flops=8 * tokens * features * hidden_n,
            transcendentals=0,
            bytes_accessed=8 * tokens * (features + hidden_n) + 4 * features * hidden_n,
        ),
        name="late_weights",
    )(*x, *ups, *grads, *acts)


def product_body(a0, a1, *refs, near):
    half = len(refs) // 3
    outs = refs[half:]
    for k in range(half):

        @pl.when(pl.program_id(0) == k)
        def _(k=k):
            weight = refs[k][...].reshape(a0.shape[1], outs[0].shape[1])
            outs[2 * k][...] = dot_nn(a0[...], weight).astype(BF)
            outs[2 * k + 1][...] = dot_nn(a1[...], weight).astype(BF)


def down_products(acts, close_down, far_down, rows_n):
    tokens, hidden_n = acts[0].shape
    span = close_down[0].shape[1]
    near = len(close_down)
    act = pl.BlockSpec((tokens, hidden_n), lambda i: (0, 0))
    ins, operands = [act] * 2, list(acts)
    for k in range(rows_n):
        if k < near or len(far_down) > 1:
            ins.append(pl.BlockSpec((hidden_n, span), lambda i: (0, 0)))
            operands.append(close_down[k] if k < near else far_down[k - near])
        else:
            planes, _, rows, _ = far_down[0].shape
            ins.append(
                pl.BlockSpec((planes, 1, rows, span), lambda i, k=k: (0, k - near, 0, 0))
            )
            operands.append(far_down[0])
    out = pl.pallas_call(
        functools.partial(product_body, near=near),
        grid=(rows_n,),
        in_specs=ins,
        out_specs=[pl.BlockSpec((tokens, span), lambda i: (0, 0))] * (2 * rows_n),
        out_shape=[jax.ShapeDtypeStruct((tokens, span), BF)] * (2 * rows_n),
        compiler_params=pltpu.CompilerParams(vmem_limit_bytes=56 << 20),
        name="down_products",
    )(*operands)
    return {(a, k): out[2 * k + a] for k in range(rows_n) for a in range(2)}


def finish_body(where, *refs, rows_n, dp_n):
    pieces = refs[:rows_n]
    gate_ref, up_ref, down_ref = refs[rows_n:]
    part = pieces[0].shape[1] // dp_n
    share = pieces[0].shape[2]
    for k in range(rows_n):
        sender = where[0] ^ k
        for i in range(rows_n):

            @pl.when(sender == i)
            def _(k=k, i=i):
                for q in range(dp_n):
                    rows = slice(q * part, (q + 1) * part)
                    here = slice((q * rows_n + i) * part, (q * rows_n + i + 1) * part)
                    gate_ref[:, here] = pieces[k][0, rows].astype(F32).T
                    up_ref[:, here] = pieces[k][1, rows].astype(F32).T
                    down_ref[i * part : (i + 1) * part, q * share : (q + 1) * share] = pieces[k][
                        2, rows
                    ].astype(F32)


def finish_weight_grads(where, pieces, rows_n, dp_n):
    _, hidden_n, share = pieces[0].shape
    spec = pl.BlockSpec((3, hidden_n, share), lambda i, w: (0, 0, 0))
    shapes = [(share, rows_n * hidden_n)] * 2 + [(hidden_n, dp_n * share)]
    return pl.pallas_call(
        functools.partial(finish_body, rows_n=rows_n, dp_n=dp_n),
        grid_spec=pltpu.PrefetchScalarGridSpec(
            num_scalar_prefetch=1,
            grid=(1,),
            in_specs=[spec] * rows_n,
            out_specs=[pl.BlockSpec(shape, lambda i, w: (0, 0)) for shape in shapes],
        ),
        out_shape=[jax.ShapeDtypeStruct(shape, F32) for shape in shapes],
        compiler_params=pltpu.CompilerParams(vmem_limit_bytes=40 << 20),
        name="finish_weights",
    )(where, *pieces)


def cut_body(where, *refs, ks, rows_n, dp_n):
    gate, up = refs[:2]
    outs = refs[len(refs) - 2 * len(ks) :]
    down_in = refs[2 : len(refs) - 2 * len(ks)]
    part = gate.shape[1] // (dp_n * rows_n)
    for n, k in enumerate(ks):
        slot = where[0] ^ k
        for i in range(rows_n):

            @pl.when(slot == i)
            def _(n=n, i=i):
                for q in range(dp_n):
                    here = slice((q * rows_n + i) * part, (q * rows_n + i + 1) * part)
                    there = slice(q * part, (q + 1) * part)
                    outs[2 * n][0, there] = gate[:, here].T
                    outs[2 * n][1, there] = up[:, here].T
                    if len(down_in) < len(ks):
                        outs[2 * n + 1][there] = down_in[0][here]

        if len(down_in) == len(ks):
            outs[2 * n + 1][...] = down_in[n][...]


def cut_weights(where, w_gate, w_up, w_down, ks, rows_n, dp_n, rows_in, rows_down):
    hidden_n = w_gate.shape[1] // rows_n
    part = hidden_n // dp_n
    span = w_down.shape[1]
    ins = [pl.BlockSpec((rows_in, w_gate.shape[1]), lambda i, w: (w[1], 0))] * 2
    if rows_down == part:
        for k in ks:
            ins.append(pl.BlockSpec((part, span), lambda i, w, k=k: (w[2] * rows_n + (w[0] ^ k), 0)))
    else:
        ins.append(pl.BlockSpec(w_down.shape, lambda i, w: (0, 0)))
    out_specs, out_shape = [], []
    for _ in ks:
        out_specs += [
            pl.BlockSpec((2, hidden_n, rows_in), lambda i, w: (0, 0, 0)),
            pl.BlockSpec((rows_down, span), lambda i, w: (0, 0)),
        ]
        out_shape += [
            jax.ShapeDtypeStruct((2, hidden_n, rows_in), BF),
            jax.ShapeDtypeStruct((rows_down, span), BF),
        ]
    out = pl.pallas_call(
        functools.partial(cut_body, ks=ks, rows_n=rows_n, dp_n=dp_n),
        grid_spec=pltpu.PrefetchScalarGridSpec(
            num_scalar_prefetch=1, grid=(1,), in_specs=ins, out_specs=out_specs
        ),
        out_shape=out_shape,
        compiler_params=pltpu.CompilerParams(vmem_limit_bytes=40 << 20),
        name="cut_weights",
    )(where, w_gate, w_up, *([w_down] * (len(ins) - 2)))
    return out[0::2], out[1::2]


def cut_plain(row, w_gate, w_up, w_down, ks, rows_n, dp_n):
    part = w_gate.shape[1] // (dp_n * rows_n)
    cut_in, cut_down = [], []
    for k in ks:
        starts = [(q * rows_n + (row ^ k)) * part for q in range(dp_n)]
        both = []
        for w in (w_gate.T, w_up.T):
            both.append(jnp.concatenate([lax.dynamic_slice_in_dim(w, at, part, 0) for at in starts]))
        cut_in.append(jnp.stack(both))
        cut_down.append(
            jnp.concatenate([lax.dynamic_slice_in_dim(w_down, at, part, 0) for at in starts])
        )
    return cut_in, cut_down


def tie(value, *others):
    return lax.optimization_barrier((value, others))[0]


def per_device(
    rows_n,
    tokens,
    seq_ids,
    block_ids,
    positions,
    norm1_gain,
    norm2_gain,
    w_query,
    w_kv,
    w_out,
    w_gate,
    w_up,
    w_down,
    grad_output,
):
    R = rows_n
    bits = []
    while (1 << len(bits)) < R:
        bits.append(1 << len(bits))
    nbits = len(bits)

    def reverse(v):
        out = 0
        for b in range(nbits):
            out = out | (((v >> b) & 1) << (nbits - 1 - b))
        return out

    order = [reverse(v) for v in range(R)]
    row = lax.axis_index("row")
    col = lax.axis_index("col")
    half_rows, dslice = tokens.shape
    B = half_rows // R
    full_rows = 2 * half_rows
    width = w_kv.shape[1] // 2
    dp_n = lax.axis_size("dp")

    def tf(flag, value, *others):
        return tie(value, *others) if FL.get(flag, 0) else value

    def tc(flag, value, *options):
        k = FL.get(flag, 0)
        return tie(value, options[k - 1]) if k else value

    def swap_row(a, bit):
        return lax.ppermute(a, "row", [(i, i ^ bit) for i in range(R)])

    def swap_col(a):
        return lax.ppermute(a, "col", [(0, 1), (1, 0)])

    def psum_row(a):
        for bit in bits:
            a = a + swap_row(a, bit)
        return a

    def pick(a, index, size):
        return lax.dynamic_slice_in_dim(a, index * size, size, 0)

    def to_order(a):
        return jnp.concatenate([pick(a, row ^ order[p], B) for p in range(R)], axis=0)

    def from_order(a):
        return jnp.concatenate([pick(a, reverse(row ^ b), B) for b in range(R)], axis=0)

    def reduce_row(a, send_after=(), use_after=()):
        a = a.astype(BF)
        for bit in bits:
            half = a.shape[0] // 2
            keep, send = a[:half], a[half:]
            if bit == bits[-1]:
                send = tie(send, send_after)
            came = swap_row(send, bit)
            if bit == bits[-1]:
                came = tie(came, use_after)
            total = keep.astype(F32) + came.astype(F32)
            a = total.astype(BF)
        return total

    def gather_outer(a):
        for bit in reversed(bits[1:]):
            a = jnp.concatenate([a, swap_row(a, bit)], axis=0)
        return a

    def gather_core(a):
        return jnp.concatenate([a, swap_row(a, 1)], axis=0)

    def gather_row(a):
        return gather_core(gather_outer(a))

    def spread(pieces, bit):
        out = dict(pieces)
        for (a, k), value in pieces.items():
            out[(a, k ^ bit)] = swap_row(value, bit)
        return out

    def spread_col(pieces):
        out = dict(pieces)
        for (a, k), value in pieces.items():
            out[(1 - a, k)] = swap_col(value)
        return out

    half = half_rows // 2

    def gather_plane(mine):
        first = came = spread_col({(0, 0): mine[:half]})
        for bit in reversed(bits[1:]):
            first = spread(first, bit)
        second = {(0, 0): mine[half:]}
        for bit in reversed(bits[1:]):
            second = spread(second, bit)
        second = spread_col(second)
        return (spread(first, 1), spread(second, 1)), came

    def add(a, b, wide=False):
        total = a.astype(F32) + b.astype(F32)
        return total if wide else total.astype(BF)

    def plane_core(blocks):
        moved = {(a, k): swap_row(blocks[(a, k ^ 1)], 1) for a in (1, 0) for k in range(0, R, 2)}
        halves = (slice(0, half), slice(half, 2 * half))
        return [{key: add(blocks[key][h], value[h]) for key, value in moved.items()} for h in halves]

    def plane_rest(parts, after=((), ()), then=(), use_after=()):
        def by_col(cur, last, use_after=()):
            return {
                (0, k): add(v, tie(swap_col(cur[(1, k)]), use_after), last)
                for (a, k), v in cur.items()
                if a == 0
            }

        def by_rows(cur, last, use_after=()):
            for bit in bits[1:]:
                cur = {
                    (a, k): add(
                        v, tie(swap_row(cur[(a, k ^ bit)], bit), use_after), last and bit == bits[-1]
                    )
                    for (a, k), v in cur.items()
                    if not k & bit
                }
            return cur

        first = by_col(tie(parts[0], after[0]), False, use_after)
        second = by_rows(tie(parts[1], after[1]), False, use_after)
        outs = [by_rows(tie(first, then), True), by_col(tie(second, then), True)]
        return jnp.concatenate([o[(0, 0)] for o in outs], axis=0)

    residual = tokens.astype(F32)
    scale_one = lax.rsqrt(psum_row(jnp.sum(residual * residual, axis=1)) / D + EPS)
    weighted_in = (residual * norm1_gain[None, :]).astype(BF)
    ordered_in = to_order(weighted_in)
    w_query_far = swap_col(w_query)
    own = col * R + row
    own_scale = lax.dynamic_slice_in_dim(scale_one, row * B, B)[:, None]

    kv_pre = reduce_row(dot_nn(ordered_in, w_kv)) * own_scale
    query_near = reduce_row(dot_nn(ordered_in, w_query)) * own_scale

    z = lax.axis_index("dp")
    near = min(2, R)
    hidden_n = w_gate.shape[1] // R
    shared = (dslice % (128 * dp_n) == 0, hidden_n % (16 * dp_n) == 0)
    shared = (all(shared), all(shared))
    rows_in = dslice // dp_n if shared[0] else dslice
    rows_down = hidden_n // dp_n if shared[1] else hidden_n

    shares = jnp.stack([row, z if shared[0] else 0 * z, z if shared[1] else 0 * z])
    shares = tie(shares, kv_pre)
    far_ks = tuple(range(near, R))
    part = hidden_n // dp_n
    if part % 16 == 0:
        cut_in, cut_down = cut_weights(shares, w_gate, w_up, w_down, far_ks, R, dp_n, rows_in, rows_down)
    else:
        cut_in, cut_down = cut_plain(row, w_gate, w_up, w_down, far_ks, R, dp_n)
    half_width = width // 2
    frequency = ROPE_BASE ** (-2.0 * jnp.arange(half_width, dtype=F32) / width)
    own_positions = lax.dynamic_slice_in_dim(positions, own * B, B)
    angles = own_positions.astype(F32)[:, None] * frequency[None, :]
    cosine = jnp.concatenate([jnp.cos(angles)] * 2, axis=1)
    sine_half = jnp.sin(angles)
    sine = jnp.concatenate([-sine_half, sine_half], axis=1)

    key_pre = kv_pre[:, :width]
    key_turned = jnp.concatenate([key_pre[:, half_width:], key_pre[:, :half_width]], axis=1)
    key_own = key_pre * cosine + key_turned * sine
    kv_own = jnp.concatenate([key_own, kv_pre[:, width:]], axis=1).astype(BF)
    kv_pieces = spread_col({(0, 0): kv_own})
    for bit in reversed(bits):
        kv_pieces = spread(kv_pieces, bit)
    kv_all = [kv_pieces[(a, k)] for a in range(2) for k in range(R)]
    meta = (jnp.stack([row, col]), seq_ids, block_ids)
    far_in = [swap_row(a, k) for a, k in zip(tf("f11", cut_in, kv_all), far_ks)]
    far_cut_down = cut_down
    if shared[0]:
        far_in = [jnp.stack(far_in)]
    w_out_far = swap_col(tc("f13", w_out, w_query_far, query_near, kv_pre))
    query_near = tf("f0", query_near, w_out_far)
    query_near = tf("f1", query_near, far_in)
    close_ks = tuple(range(near))
    if part % 16 == 0:
        shares = shares * jnp.array([1, 0, 0], jnp.int32)
        cut_in, cut_down = cut_weights(shares, w_gate, w_up, w_down, close_ks, R, dp_n, dslice, hidden_n)
    else:
        cut_in, cut_down = cut_plain(row, w_gate, w_up, w_down, close_ks, R, dp_n)
    close_in = [swap_row(a, k) if k else a for k, a in enumerate(cut_in)]
    close_down = [swap_row(a, k) if k else a for k, a in enumerate(cut_down)]
    query_near_raw = query_near
    down_grad = grad_output.astype(BF)
    part_qfar = dot_nn(ordered_in, w_query_far).astype(BF)
    if FL.get("f5", 0) < 3:
        grad_pieces = {(0, 0): tc("f5", down_grad, kv_pre, query_near)}
        for bit in reversed(bits[1:]):
            grad_pieces = spread(grad_pieces, bit)
        query_near = tf("f15", query_near, grad_pieces[(0, bits[-1])])
    att_near, rot_near, lse_near = attend(meta, query_near, cosine, sine, kv_all, width, R)
    if FL.get("f5", 0) >= 3:
        grad_pieces = {(0, 0): tie(down_grad, att_near)}
        for bit in reversed(bits[1:]):
            grad_pieces = spread(grad_pieces, bit)
    grad_rows = dict(grad_pieces)
    for (a, k), value in grad_rows.items():
        if k:
            grad_pieces[(1, k)] = swap_col(value)
        else:
            grad_pieces[(1, k)] = swap_col(tc("f12", down_grad, w_query_far, query_near_raw, w_out_far, att_near))
    query_far = reduce_row(
        part_qfar,
        send_after=query_near_raw if FL.get("f9", 0) else (),
        use_after=(att_near, close_in),
    )
    query_far = tf("f2", query_far, grad_pieces[(1, 0)])
    query_far = tf("f3", query_far, far_in)
    query_far = tf("f4", query_far, w_out_far)
    query_far = tf("f8", query_far, grad_rows) * own_scale
    if shared[0]:
        far_in = [lax.all_gather(far_in[0], "dp", axis=0)]
    near_outer = gather_outer(att_near)
    query_far = tf("f16", query_far, near_outer)
    att_far, rot_far, lse_far = attend(meta, query_far, cosine, sine, kv_all, width, R)
    far_cut_down = tc("f10", far_cut_down, query_near_raw, att_near, att_far, near_outer)
    far_down = [swap_row(a, k) for a, k in zip(far_cut_down, far_ks)]
    if shared[1]:
        far_down = [lax.all_gather(jnp.stack(far_down), "dp", axis=0)]

    all_near = gather_core(near_outer)
    far_outer = gather_outer(att_far)
    far_outer = tf("f6", far_outer, grad_rows)
    far_outer = tf("f17", far_outer, grad_pieces)
    all_far = gather_core(far_outer)
    hidden = residual + from_order(dot_nn(all_near, w_out) + dot_nn(all_far, w_out_far))

    def exchange(parts):
        return [parts[0]] + [swap_row(parts[k], k) for k in range(1, len(parts))]

    scale_two = lax.rsqrt(psum_row(jnp.sum(hidden * hidden, axis=1)) / D + EPS)[:, None]
    normed_two = (hidden * scale_two * norm2_gain[None, :]).astype(BF)
    normed_pieces, came = gather_plane(tf("f7", normed_two, grad_pieces))
    grad_pieces = spread(tf("f14", grad_pieces, came), 1)

    fed = {}
    backs = {}
    for a in (0, 1):
        fed[a] = feed(
            [[part[(a, k)] for k in range(R)] for part in normed_pieces],
            [grad_pieces[(a, k)] for k in range(R)],
            close_in,
            close_down,
            far_in,
            far_down,
            shared,
            dp_n,
        )
        for k in range(R):
            backs[(a, k)] = fed[a][3 + k]
    acts, gate_grads, up_grads = ([fed[a][j] for a in range(2)] for j in range(3))
    normed_halves, grad_halves = ([fed[a][3 + R + j] for a in range(2)] for j in range(2))
    core_sums = plane_core(backs)
    normed2_grad = None if FL.get("b37", 0) else plane_rest(core_sums)

    def place(pieces):
        moved = jnp.stack(exchange([jnp.stack([p[k] for p in pieces]) for k in range(R)]))
        ordered = [lax.dynamic_index_in_dim(moved, row ^ s, 0, keepdims=False) for s in range(R)]
        return [jnp.stack([o[n] for o in ordered]) for n in range(len(pieces))]

    def ff_input_place(rows):
        rows = rows.reshape(R, dp_n, part, -1).transpose(1, 0, 2, 3)
        return rows.reshape(R * hidden_n, -1).astype(F32).T

    def over_dp(local):
        return lax.psum_scatter(local, "dp", scatter_dimension=0, tiled=True)

    gate_local = feed_weight_grad(normed_halves, gate_grads, R, dp_n)
    gate_piece = over_dp(gate_local)
    if shared[1]:
        late = late_weight_grads(
            normed_halves, tf("b0", tie(up_grads, gate_local), core_sums), grad_halves, acts, R, dp_n
        )
        late_piece = over_dp(tie(late, gate_local))
        if FL.get("b37", 0):
            normed2_grad = plane_rest(core_sums, use_after=late)
        up_piece, down_piece = late_piece[0, 0], late_piece[0, 1]
        normed2_grad = tie(normed2_grad, gate_local, late)
    else:
        late_piece = gate_piece
        normed2_grad = plane_rest(core_sums)
        up_piece = over_dp(feed_weight_grad(normed_halves, up_grads, R, dp_n))[0]
        down_piece = over_dp(down_weight_grad(acts, grad_halves, R, dp_n))[0]

    weighted = normed2_grad * norm2_gain[None, :]
    inner_two = psum_row(jnp.sum(weighted * hidden, axis=1))[:, None]
    hidden_grad = grad_output + (
        scale_two * weighted - hidden * (scale_two * scale_two * scale_two) * inner_two / D
    )
    gain_two = jnp.sum(normed2_grad * hidden * scale_two, axis=0)
    branch_ordered = to_order(hidden_grad.astype(BF))
    part_far = dot_nt(branch_ordered, w_out_far).astype(BF)
    part_near = dot_nt(branch_ordered, w_out).astype(BF)
    prod_dep = FL.get("b5", 0)
    branch_late, late_acts = branch_ordered, acts

    def make_products():
        return down_products(late_acts, close_down, far_down, R)

    if prod_dep < 2:
        late_acts = tie(acts, hidden_grad) if prod_dep == 0 else tie(acts, part_far, part_near)
        products = make_products()
    b6 = FL.get("b6", 0) if prod_dep < 2 else 0
    att_grad_far = reduce_row(part_far, use_after=products if b6 == 1 else ()).astype(BF)
    att_grad_near = reduce_row(
        part_near, send_after=att_grad_far if FL.get("b25", 0) else (), use_after=products if b6 == 2 else ()
    ).astype(BF)
    gout_early = FL.get("b26", 0)
    if gout_early:
        grad_out_far = dot_tn(all_far, branch_late).astype(BF)
        grad_out_came = swap_col(grad_out_far)
        grad_out_near = dot_tn(all_near, branch_late)
        att_grad_far = tf("b27", att_grad_far, grad_out_far, grad_out_near)
        att_grad_far = tf("b4", att_grad_far, grad_out_came)
    att_grad_far = tf("b2", att_grad_far, gate_piece)
    att_grad_far = tf("b3", att_grad_far, att_grad_near)

    qpg_far, dk, dv = attend_back(
        meta, rot_far, att_grad_far, att_far, lse_far, cosine, sine, kv_all, width, R
    )
    if not gout_early:
        branch_late = tie(branch_ordered, qpg_far)
        grad_out_far = dot_tn(all_far, branch_late).astype(BF)
        grad_out_came = swap_col(grad_out_far)
        grad_out_near = dot_tn(all_near, branch_late)
    if prod_dep == 2:
        late_acts = tie(acts, qpg_far)
        products = make_products()
    scale_col = scale_one[:, None]
    normed_ordered = to_order((residual * scale_col * norm1_gain[None, :]).astype(BF))
    qpg_far_outer = gather_outer(tf("b28", qpg_far, grad_out_far))
    qpg_far_all = gather_core(qpg_far_outer)
    qpg_far_used = tf("b8", qpg_far_all, grad_out_near)
    if prod_dep < 3:
        qpg_far_used = tf("b29", qpg_far_used, products)
    grad_query_far = dot_tn(normed_ordered, qpg_far_used).astype(BF)
    grad_query_came = swap_col(grad_query_far)
    att_grad_near = tf("b30", att_grad_near, qpg_far_outer)
    att_grad_near = tf("b7", att_grad_near, grad_query_far)
    att_grad_near = tf("b31", att_grad_near, grad_out_came)
    qpg_near, dk, dv = attend_back(
        meta, rot_near, att_grad_near, att_near, lse_near, cosine, sine, kv_all, width, R,
        (dk, dv),
    )
    if prod_dep == 3:
        late_acts = tie(acts, qpg_near)
        products = make_products()
    grad_out_local = add(grad_out_near, tc("b24", grad_out_came, qpg_far, qpg_near))
    grad_out = over_dp(tc("b18", grad_out_local, gate_piece, late_piece))
    qpg_near_outer = gather_outer(tf("b32", qpg_near, grad_out_local))
    qpg_near_all = gather_core(qpg_near_outer)
    qpg_near_used = tf("b19", tie(qpg_near_all, grad_query_came), late_piece)
    grad_query_near = dot_tn(normed_ordered, qpg_near_used)
    grad_query_local = add(grad_query_near, grad_query_came)
    opts = (qpg_far, qpg_near, qpg_near_outer, grad_query_came, grad_query_local)
    pick_opt = lambda k: () if not k else opts[k - 1]
    down_sum = plane_rest(
        plane_core(products),
        after=(pick_opt(FL.get("b13", 0)), pick_opt(FL.get("b14", 0))),
        then=pick_opt(FL.get("b15", 0)),
    )
    output = hidden + down_sum
    dk, dv = tc("b9", (dk, dv), qpg_near_outer, grad_out_local, grad_query_came, grad_query_local)

    dkv = jnp.concatenate([dk * width**-0.5, dv], axis=2).astype(BF)
    cur = {(a, k): dkv[a * R + k] for a in range(2) for k in range(R)}
    for bit in bits:
        cur = {
            (a, k): add(v, swap_row(cur[(a, k ^ bit)], bit))
            for (a, k), v in cur.items()
            if not k & bit
        }
    dkv_own = cur[(0, 0)].astype(F32) + swap_col(cur[(1, 0)]).astype(F32)
    dk_own = dkv_own[:, :width]
    dk_turned = jnp.concatenate([dk_own[:, half_width:], dk_own[:, :half_width]], axis=1)
    kvg_own = jnp.concatenate(
        [dk_own * cosine - dk_turned * sine, dkv_own[:, width:]], axis=1
    ).astype(BF)


    pieces = tc("b17", (gate_piece[0], up_piece, down_piece), qpg_near, grad_query_local, qpg_near_outer)
    moved = exchange([jnp.stack([p[k] for p in pieces]) for k in range(R)]) if shared[1] else ()
    kvg_own = tf("b36", kvg_own, moved)
    kvg_own = tc("b16", kvg_own, qpg_near_outer, grad_query_came, grad_query_local)
    kvg_all = gather_row(kvg_own)
    normed1_grad = from_order(
        dot_nt(qpg_far_all, w_query_far) + dot_nt(qpg_near_all, w_query) + dot_nt(kvg_all, w_kv)
    )
    normed1_grad = tf("b22", normed1_grad, grad_out)
    normed1_grad = tf("b33", normed1_grad, moved)
    normed1_grad = tf("b34", normed1_grad, grad_query_local)
    normed1_grad = tf("b23", normed1_grad, output)
    weighted_one = normed1_grad * norm1_gain[None, :]
    inner_one = psum_row(jnp.sum(weighted_one * residual, axis=1))[:, None]
    input_grad = hidden_grad + (
        scale_col * weighted_one - residual * (scale_col * scale_col * scale_col) * inner_one / D
    )
    gain_one = jnp.sum(normed1_grad * residual * scale_col, axis=0)

    grad_query = over_dp(tf("b20", grad_query_local, grad_out))
    if shared[1]:
        grad_gate, grad_up, grad_down = finish_weight_grads(meta[0], moved, R, dp_n)
    else:
        gate_rows, up_rows = place(pieces[:2])
        grad_gate, grad_up = ff_input_place(gate_rows), ff_input_place(up_rows)
        grad_down = place(pieces[2:])[0].reshape(hidden_n, dslice).astype(F32)

    rest = dslice // (2 * dp_n)
    gains = jnp.concatenate(
        [g.reshape(dp_n, 2, 1, rest) for g in (gain_one, gain_two)]
        + [jnp.zeros((dp_n, 2, 1, 2 * width - 2 * rest), F32)],
        axis=3,
    )
    local = dot_tn(normed_ordered, kvg_all).reshape(dp_n, 2, rest, 2 * width)
    local = jnp.concatenate([local, gains], axis=2)
    mine = lax.dynamic_index_in_dim(local, col, 1, keepdims=False)
    other = lax.dynamic_index_in_dim(local, 1 - col, 1, keepdims=False).astype(BF)
    both = mine + swap_col(other).astype(F32)
    small = lax.dynamic_index_in_dim(both, z, 0, keepdims=False)
    for j in range(1, dp_n):
        share = lax.dynamic_index_in_dim(both, z ^ j, 0, keepdims=False).astype(BF)
        share = lax.ppermute(share, "dp", [(i, i ^ j) for i in range(dp_n)])
        small = small + share.astype(F32)

    return (
        output,
        input_grad,
        grad_query.astype(F32)[None],
        small[None, :rest],
        grad_out.astype(F32)[None],
        grad_gate[None],
        grad_up[None],
        grad_down[None],
        small[rest:, :rest],
        small[rest:, rest : 2 * rest],
    )


def solution(mesh):
    placed = (
        P(("dp", "col"), "row"),
        P("dp"),
        P("dp"),
        P("dp"),
        P("row"),
        P("row"),
        P("row", "col"),
        P("row", None),
        P("col", "row"),
        P("row", "col"),
        P("row", "col"),
        P("col", "row"),
        P(("dp", "col"), "row"),
    )
    return jax.shard_map(
        functools.partial(per_device, mesh.shape["row"]),
        mesh=mesh,
        in_specs=placed,
        out_specs=(
            P(("dp", "col"), "row"),
            P(("dp", "col"), "row"),
            P("row", "dp", "col"),
            P("row", ("dp", "col"), None),
            P("col", "dp", "row"),
            P("row", "dp", "col"),
            P("row", "dp", "col"),
            P("col", "dp", "row"),
            P("row", ("dp", "col")),
            P("row", ("dp", "col")),
        ),
        check_vma=False,
    )
```

```python
import functools

import jax
import jax.numpy as jnp
from jax import lax
from jax.experimental import pallas as pl
from jax.experimental.pallas import tpu as pltpu
from jax.sharding import PartitionSpec as P

D = 2048
EPS = 1e-05
ROPE_BASE = 500000.0
BLOCK = 256
LOG2E = 1.4426950408889634
BF = jnp.bfloat16
F32 = jnp.float32
HEADS_PER_STEP = 4
FL = {'f11': 0, 'f13': 1, 'f0': 1, 'f1': 1, 'f5': 2, 'f9': 1, 'f12': 2, 'f2': 1, 'f3': 1, 'f4': 0, 'f8': 1, 'f10': 3, 'f6': 1, 'f7': 1, 'f14': 1, 'f15': 0, 'f16': 0, 'f17': 0, 'b0': 1, 'b1': 0, 'b2': 1, 'b3': 0, 'b4': 0, 'b5': 2, 'b6': 0, 'b7': 1, 'b8': 1, 'b29': 0, 'b28': 0, 'b18': 2, 'b19': 1, 'b24': 1, 'b9': 3, 'b13': 5, 'b14': 1, 'b15': 1, 'b16': 3, 'b17': 2, 'b20': 0, 'b22': 0, 'b23': 0, 'b25': 1, 'b26': 1, 'b27': 0, 'b30': 0, 'b31': 0, 'b32': 0, 'b33': 0, 'b34': 0, 'b36': 0, 'b37': 1}


def dot_nn(a, b):
    return lax.dot_general(a, b, (((1,), (0,)), ((), ())), preferred_element_type=F32)


def dot_nt(a, b):
    return lax.dot_general(a, b, (((1,), (1,)), ((), ())), preferred_element_type=F32)


def dot_tn(a, b):
    return lax.dot_general(a, b, (((0,), (0,)), ((), ())), preferred_element_type=F32)


def list_visible(where, seq_ref, block_ref, list_ref, *, rows_n, rows):
    row, col = where[0], where[1]
    chunks = 2 * rows_n
    own = (col * rows_n + row) * rows
    count = jnp.int32(0)
    for j in range(chunks):
        seen = (seq_ref[j * rows] == seq_ref[own]) & (block_ref[j * rows] <= block_ref[own])

        @pl.when(seen)
        def _(j=j, count=count):
            list_ref[count] = ((j // rows_n) ^ col) * rows_n + ((j % rows_n) ^ row)

        count = count + seen.astype(jnp.int32)
    list_ref[chunks] = count


def attend_body(
    where, seq_ref, block_ref, q_ref, cos_ref, sin_ref, *refs, factor, width, rows_n,
):
    pieces = refs[:-6]
    att_ref, rot_ref, lse_ref, list_ref, k_ref, vt_ref = refs[-6:]

    @pl.when(pl.program_id(0) == 0)
    def _():
        list_visible(where, seq_ref, block_ref, list_ref, rows_n=rows_n, rows=q_ref.shape[0])
        for j, piece in enumerate(pieces):
            k_ref[j] = piece[:, :width]
            vt_ref[j] = piece[:, width:].T

    cosine = cos_ref[...]
    sine = sin_ref[...]
    rows = q_ref.shape[0]
    heads = [slice(h * width, (h + 1) * width) for h in range(HEADS_PER_STEP)]
    for cols in heads:
        pre = q_ref[:, cols]
        rot_ref[:, cols] = (pre * cosine + pltpu.roll(pre, width // 2, 1) * sine).astype(BF)

    def step(t, carry):
        chunk = list_ref[t]
        key = k_ref[chunk]
        value_t = vt_ref[chunk]
        all_scores = [dot_nt(key, rot_ref[:, cols]) * factor for cols in heads]
        out = []
        for (top, total, acc), scores in zip(carry, all_scores):
            new_top = jnp.maximum(top, jnp.max(scores, axis=0, keepdims=True))
            decay = jnp.exp2(top - new_top)
            weights = jnp.exp2(scores - new_top)
            total = total * decay + jnp.sum(weights, axis=0, keepdims=True)
            acc = acc * decay + dot_nn(value_t, weights.astype(BF))
            out.append((new_top, total, acc))
        return out

    start = (
        jnp.full((1, rows), -1e30, F32),
        jnp.zeros((1, rows), F32),
        jnp.zeros((width, rows), F32),
    )
    done = lax.fori_loop(0, list_ref[2 * rows_n], step, [start] * HEADS_PER_STEP)
    for head, (top, total, acc) in enumerate(done):
        att_ref[:, heads[head]] = (acc / total).T.astype(BF)
        lse_ref[head] = top + jnp.log2(total)


def attend(meta, q_pre, cosine, sine, kv, width, rows_n):
    where, seq_ids, block_ids = meta
    rows, columns = q_pre.shape
    heads = columns // width
    chunks = len(kv)
    span = HEADS_PER_STEP * width
    whole2 = lambda i, m: (0, 0)
    return pl.pallas_call(
        functools.partial(attend_body, factor=width**-0.5 * LOG2E, width=width, rows_n=rows_n),
        grid_spec=pltpu.PrefetchScalarGridSpec(
            num_scalar_prefetch=1,
            grid=(heads // HEADS_PER_STEP,),
            in_specs=[
                pl.BlockSpec(memory_space=pltpu.SMEM),
                pl.BlockSpec(memory_space=pltpu.SMEM),
                pl.BlockSpec((rows, span), lambda i, m: (0, i)),
                pl.BlockSpec((rows, width), whole2),
                pl.BlockSpec((rows, width), whole2),
            ]
            + [pl.BlockSpec((rows, 2 * width), whole2)] * chunks,
            out_specs=[
                pl.BlockSpec((rows, span), lambda i, m: (0, i)),
                pl.BlockSpec((rows, span), lambda i, m: (0, i)),
                pl.BlockSpec((HEADS_PER_STEP, 1, rows), lambda i, m: (i, 0, 0)),
            ],
            scratch_shapes=[
                pltpu.SMEM((chunks + 1,), jnp.int32),
                pltpu.VMEM((chunks, rows, width), BF),
                pltpu.VMEM((chunks, width, rows), BF),
            ],
        ),
        out_shape=[
            jax.ShapeDtypeStruct((rows, columns), BF),
            jax.ShapeDtypeStruct((rows, columns), BF),
            jax.ShapeDtypeStruct((heads, 1, rows), F32),
        ],
        cost_estimate=pl.CostEstimate(
            flops=4 * rows * columns * chunks * rows // 2,
            transcendentals=heads * rows * chunks * rows // 2,
            bytes_accessed=8 * rows * columns + 4 * chunks * rows * width,
        ),
        name="attend",
    )(where, seq_ids, block_ids, q_pre, cosine, sine, *kv)


def attend_back_body(
    where, seq_ref, block_ref, rot_ref, grad_ref, att_ref, lse_ref, cos_ref, sin_ref,
    *outs, factor, scale, width, rows_n,
):
    pieces, outs = outs[: 2 * rows_n], outs[2 * rows_n :]
    qpg_ref, dk_ref, dv_ref, list_ref, k_ref, kt_ref, v_ref = outs[-7:]

    @pl.when(pl.program_id(0) == 0)
    def _():
        list_visible(where, seq_ref, block_ref, list_ref, rows_n=rows_n, rows=rot_ref.shape[0])
        dk_ref[...] = jnp.zeros_like(dk_ref) if len(outs) == 7 else outs[0][...]
        dv_ref[...] = jnp.zeros_like(dv_ref) if len(outs) == 7 else outs[1][...]
        for j, piece in enumerate(pieces):
            k_ref[j] = piece[:, :width]
            kt_ref[j] = piece[:, :width].T
            v_ref[j] = piece[:, width:]

    cosine = cos_ref[...]
    sine = sin_ref[...]
    rows = rot_ref.shape[0]
    heads = [slice(h * width, (h + 1) * width) for h in range(HEADS_PER_STEP)]
    inners = []
    for cols in heads:
        inner = (grad_ref[:, cols].astype(F32) * att_ref[:, cols].astype(F32)).T
        inners.append(jnp.sum(inner, axis=0, keepdims=True))

    def step(t, dqs):
        chunk = list_ref[t]
        key = k_ref[chunk]
        key_t = kt_ref[chunk]
        value = v_ref[chunk]
        all_scores = [dot_nt(key, rot_ref[:, cols]) for cols in heads]
        backs = [dot_nt(value, grad_ref[:, cols]) for cols in heads]
        dv = dv_ref[chunk]
        dk = dk_ref[chunk]
        out = []
        for h, cols in enumerate(heads):
            probs = jnp.exp2(all_scores[h] * factor - lse_ref[h])
            score_grad = (probs * (backs[h] - inners[h])).astype(BF)
            dv = dv + dot_nn(probs.astype(BF), grad_ref[:, cols])
            dk = dk + dot_nn(score_grad, rot_ref[:, cols])
            out.append(dqs[h] + dot_nn(key_t, score_grad))
        dv_ref[chunk] = dv
        dk_ref[chunk] = dk
        return out

    dqs = lax.fori_loop(0, list_ref[2 * rows_n], step, [jnp.zeros((width, rows), F32)] * HEADS_PER_STEP)
    for h, cols in enumerate(heads):
        dq = dqs[h].T * scale
        qpg_ref[:, cols] = (dq * cosine - pltpu.roll(dq, width // 2, 1) * sine).astype(BF)


def attend_back(meta, rot, grad, att, lse, cosine, sine, kv, width, rows_n, running=()):
    where, seq_ids, block_ids = meta
    rows, columns = rot.shape
    heads = columns // width
    chunks = len(kv)
    span = HEADS_PER_STEP * width
    whole2 = lambda i, m: (0, 0)
    whole3 = lambda i, m: (0, 0, 0)
    by_head = lambda i, m: (0, i)
    return pl.pallas_call(
        functools.partial(
            attend_back_body,
            factor=width**-0.5 * LOG2E,
            scale=width**-0.5,
            width=width,
            rows_n=rows_n,
        ),
        grid_spec=pltpu.PrefetchScalarGridSpec(
            num_scalar_prefetch=1,
            grid=(heads // HEADS_PER_STEP,),
            in_specs=[
                pl.BlockSpec(memory_space=pltpu.SMEM),
                pl.BlockSpec(memory_space=pltpu.SMEM),
                pl.BlockSpec((rows, span), by_head),
                pl.BlockSpec((rows, span), by_head),
                pl.BlockSpec((rows, span), by_head),
                pl.BlockSpec((HEADS_PER_STEP, 1, rows), lambda i, m: (i, 0, 0)),
                pl.BlockSpec((rows, width), whole2),
                pl.BlockSpec((rows, width), whole2),
            ]
            + [pl.BlockSpec((rows, 2 * width), whole2)] * chunks
            + [pl.BlockSpec((chunks, rows, width), whole3)] * len(running),
            out_specs=[
                pl.BlockSpec((rows, span), by_head),
                pl.BlockSpec((chunks, rows, width), whole3),
                pl.BlockSpec((chunks, rows, width), whole3),
            ],
            scratch_shapes=[
                pltpu.SMEM((chunks + 1,), jnp.int32),
                pltpu.VMEM((chunks, rows, width), BF),
                pltpu.VMEM((chunks, width, rows), BF),
                pltpu.VMEM((chunks, rows, width), BF),
            ],
        ),
        out_shape=[
            jax.ShapeDtypeStruct((rows, columns), BF),
            jax.ShapeDtypeStruct((chunks, rows, width), F32),
            jax.ShapeDtypeStruct((chunks, rows, width), F32),
        ],
        cost_estimate=pl.CostEstimate(
            flops=10 * rows * columns * chunks * rows // 2,
            transcendentals=heads * rows * chunks * rows // 2,
            bytes_accessed=8 * rows * columns + 12 * chunks * rows * width,
        ),
        name="attend_back",
    )(where, seq_ids, block_ids, rot, grad, att, lse, cosine, sine, *kv, *running)


def feed_body(*refs, rows_n, parts, near, shared):
    R = rows_n
    refs = list(refs)
    take = lambda n: [refs.pop(0) for _ in range(n)]
    normed = take(parts * R)
    grads = take(R)
    close_in, close_down = take(near), take(near)
    far_in = take(1 if shared[0] else R - near)
    far_down = take(1 if shared[1] else R - near)
    act_ref, gate_grad_ref, up_grad_ref = take(3)
    back_refs = take(R)
    normed_out, grads_out = take(2)
    x_ref, g_ref, wg_ref, wu_ref, wd_ref, x_sem, g_sem, w_sem, o_sem = refs
    step = pl.program_id(0)
    tile, span = normed[0].shape

    def x_copy(p, k):
        return pltpu.make_async_copy(
            normed[p * R + k], x_ref.at[p, :, pl.ds(k * span, span)], x_sem.at[p, k]
        )

    def g_copy(p, k):
        return pltpu.make_async_copy(
            grads[k].at[pl.ds(p * tile, tile)], g_ref.at[p, :, pl.ds(k * span, span)], g_sem.at[p, k]
        )

    def w_copies(j, k):
        target = (wg_ref, wu_ref, wd_ref)[j]
        if k < near or not shared[j // 2]:
            whole = (close_in + far_in, close_down + far_down)[j // 2][k]
            whole = whole if j == 2 else whole.at[j]
            place = target.at[:, pl.ds(k * span, span)]
            return [pltpu.make_async_copy(whole, place, w_sem.at[j, k, 0])]
        source = far_down[0] if j == 2 else far_in[0]
        copies = []
        for z in range(source.shape[0]):
            if j == 2:
                size = source.shape[-2]
                share = source.at[z, k - near]
                place = target.at[pl.ds(z * size, size), pl.ds(k * span, span)]
            else:
                size = source.shape[-1]
                share = source.at[z, k - near, j]
                place = target.at[:, pl.ds(k * span + z * size, size)]
            copies.append(pltpu.make_async_copy(share, place, w_sem.at[j, k, z]))
        return copies

    def x_out(p):
        return pltpu.make_async_copy(
            x_ref.at[p], normed_out.at[pl.ds(p * tile, tile)], o_sem.at[0, p]
        )

    def g_out(p):
        return pltpu.make_async_copy(
            g_ref.at[p], grads_out.at[pl.ds(p * tile, tile)], o_sem.at[1, p]
        )

    @pl.when(step == 0)
    def _():
        weights = [w_copies(j, k) for j in range(3) for k in range(R)]
        for k in range(R):
            x_copy(0, k).start()
            g_copy(0, k).start()
        for group in weights:
            for copy in group:
                copy.start()
        for p in range(1, parts):
            for k in range(R):
                x_copy(p, k).start()
                g_copy(p, k).start()
        for k in range(R):
            x_copy(0, k).wait()
            g_copy(0, k).wait()
        for group in weights:
            for copy in group:
                copy.wait()
        x_out(0).start()
        g_out(0).start()

    for p in range(1, parts):

        @pl.when(step == p)
        def _(p=p):
            for k in range(R):
                x_copy(p, k).wait()
                g_copy(p, k).wait()
            x_out(p).start()
            g_out(p).start()

    gate = dot_nt(x_ref[step], wg_ref[...])
    up = dot_nt(x_ref[step], wu_ref[...])
    mixed_grad = dot_nt(g_ref[step], wd_ref[...])
    sig = 1.0 / (1.0 + jnp.exp(-gate))
    silu = gate * sig
    act_ref[...] = (silu * up).astype(BF)
    gate_grad = (mixed_grad * up * sig * (1.0 + gate * (1.0 - sig))).astype(BF)
    up_grad = (mixed_grad * silu).astype(BF)
    gate_grad_ref[...] = gate_grad
    up_grad_ref[...] = up_grad
    for k in range(R):
        here = slice(k * span, (k + 1) * span)
        back = dot_nn(gate_grad, wg_ref[:, here]) + dot_nn(up_grad, wu_ref[:, here])
        back_refs[k][...] = back.astype(BF)

    @pl.when(step == parts - 1)
    def _():
        for p in range(parts):
            x_out(p).wait()
            g_out(p).wait()


def feed(normed, grads, close_in, close_down, far_in, far_down, shared, slots):
    parts = len(normed)
    R = len(grads)
    near = len(close_in)
    tile, span = normed[0][0].shape
    hidden_n = close_in[0].shape[1]
    total = parts * tile
    operands = [a for p in normed for a in p] + list(grads)
    operands += [*close_in, *close_down, *far_in, *far_down]
    by_tile = pl.BlockSpec((tile, hidden_n), lambda i: (i, 0))
    anywhere = pl.BlockSpec(memory_space=pl.ANY)
    return pl.pallas_call(
        functools.partial(feed_body, rows_n=R, parts=parts, near=near, shared=shared),
        grid=(parts,),
        in_specs=[anywhere] * len(operands),
        out_specs=[by_tile] * 3
        + [pl.BlockSpec((tile, span), lambda i: (i, 0))] * R
        + [anywhere] * 2,
        out_shape=[jax.ShapeDtypeStruct((total, hidden_n), BF)] * 3
        + [jax.ShapeDtypeStruct((total, span), BF)] * R
        + [jax.ShapeDtypeStruct((total, R * span), BF)] * 2,
        scratch_shapes=[
            pltpu.VMEM((parts, tile, R * span), BF),
            pltpu.VMEM((parts, tile, R * span), BF),
            pltpu.VMEM((hidden_n, R * span), BF),
            pltpu.VMEM((hidden_n, R * span), BF),
            pltpu.VMEM((hidden_n, R * span), BF),
            pltpu.SemaphoreType.DMA((parts, R)),
            pltpu.SemaphoreType.DMA((parts, R)),
            pltpu.SemaphoreType.DMA((3, R, slots)),
            pltpu.SemaphoreType.DMA((2, parts)),
        ],
        compiler_params=pltpu.CompilerParams(vmem_limit_bytes=56 << 20),
        cost_estimate=pl.CostEstimate(
            flops=10 * total * R * span * hidden_n,
            transcendentals=total * hidden_n,
            bytes_accessed=10 * total * R * span + 6 * R * span * hidden_n,
        ),
        name="feed",
    )(*operands)


def feed_weight_body(x0, x1, g0, g1, out_ref):
    total = (dot_tn(g0[...], x0[...]) + dot_tn(g1[...], x1[...])).astype(BF)
    share = out_ref.shape[3]
    for q in range(out_ref.shape[0]):
        out_ref[q, 0] = total[:, q * share : (q + 1) * share]


def feed_weight_grad(x, grads, rows_n, dp_n):
    tokens, features = x[0].shape
    span = features // rows_n
    hidden_n = grads[0].shape[1]
    return pl.pallas_call(
        feed_weight_body,
        grid=(rows_n,),
        in_specs=[pl.BlockSpec((tokens, span), lambda k: (0, k))] * 2
        + [pl.BlockSpec((tokens, hidden_n), lambda k: (0, 0))] * 2,
        out_specs=pl.BlockSpec((dp_n, 1, hidden_n, span // dp_n), lambda k: (0, k, 0, 0)),
        out_shape=jax.ShapeDtypeStruct((dp_n, rows_n, hidden_n, span // dp_n), BF),
        compiler_params=pltpu.CompilerParams(vmem_limit_bytes=48 << 20),
        cost_estimate=pl.CostEstimate(
            flops=4 * tokens * features * hidden_n,
            transcendentals=0,
            bytes_accessed=4 * tokens * (features + hidden_n) + 2 * features * hidden_n,
        ),
        name="feed_weights",
    )(*x, *grads)


def down_weight_body(a0, a1, g0, g1, out_ref):
    total = (dot_tn(a0[...], g0[...]) + dot_tn(a1[...], g1[...])).astype(BF)
    part = out_ref.shape[2]
    for q in range(out_ref.shape[0]):
        out_ref[q, 0] = total[q * part : (q + 1) * part]


def down_weight_grad(acts, grads, rows_n, dp_n):
    tokens, features = grads[0].shape
    span = features // rows_n
    hidden_n = acts[0].shape[1]
    part = hidden_n // dp_n
    return pl.pallas_call(
        down_weight_body,
        grid=(rows_n,),
        in_specs=[pl.BlockSpec((tokens, hidden_n), lambda k: (0, 0))] * 2
        + [pl.BlockSpec((tokens, span), lambda k: (0, k))] * 2,
        out_specs=pl.BlockSpec((dp_n, 1, part, span), lambda k: (0, k, 0, 0)),
        out_shape=jax.ShapeDtypeStruct((dp_n, rows_n, part, span), BF),
        compiler_params=pltpu.CompilerParams(vmem_limit_bytes=48 << 20),
        cost_estimate=pl.CostEstimate(
            flops=4 * tokens * features * hidden_n,
            transcendentals=0,
            bytes_accessed=4 * tokens * (features + hidden_n) + 2 * features * hidden_n,
        ),
        name="down_weights",
    )(*acts, *grads)


def late_weight_body(x0, x1, u0, u1, g0, g1, a0, a1, out_ref, *, rows_n):
    planes, _, _, rows, share = out_ref.shape

    @pl.when(pl.program_id(0) < rows_n)
    def _():
        total = (dot_tn(u0[...], x0[...]) + dot_tn(u1[...], x1[...])).astype(BF)
        for q in range(planes):
            out_ref[q, 0, 0] = total[:, q * share : (q + 1) * share]

    @pl.when(pl.program_id(0) >= rows_n)
    def _():
        total = (dot_tn(a0[...], g0[...]) + dot_tn(a1[...], g1[...])).astype(BF)
        part = rows // planes
        for q in range(planes):
            for j in range(planes):
                out_ref[q, 0, 0, j * part : (j + 1) * part] = total[
                    q * part : (q + 1) * part, j * share : (j + 1) * share
                ]


def late_weight_grads(x, ups, grads, acts, rows_n, dp_n):
    tokens, features = x[0].shape
    span = features // rows_n
    hidden_n = ups[0].shape[1]
    share = span // dp_n
    whole = pl.BlockSpec((tokens, hidden_n), lambda i: (0, 0))
    first = pl.BlockSpec((tokens, span), lambda i: (0, jnp.minimum(i, rows_n - 1)))
    second = pl.BlockSpec((tokens, span), lambda i: (0, jnp.maximum(i - rows_n, 0)))
    return pl.pallas_call(
        functools.partial(late_weight_body, rows_n=rows_n),
        grid=(2 * rows_n,),
        in_specs=[first] * 2 + [whole] * 2 + [second] * 2 + [whole] * 2,
        out_specs=pl.BlockSpec(
            (dp_n, 1, 1, hidden_n, share), lambda i: (0, i // rows_n, i % rows_n, 0, 0)
        ),
        out_shape=jax.ShapeDtypeStruct((dp_n, 2, rows_n, hidden_n, share), BF),
        compiler_params=pltpu.CompilerParams(vmem_limit_bytes=56 << 20),
        cost_estimate=pl.CostEstimate(
            flops=8 * tokens * features * hidden_n,
            transcendentals=0,
            bytes_accessed=8 * tokens * (features + hidden_n) + 4 * features * hidden_n,
        ),
        name="late_weights",
    )(*x, *ups, *grads, *acts)


def product_body(a0, a1, *refs, near):
    half = len(refs) // 3
    outs = refs[half:]
    for k in range(half):

        @pl.when(pl.program_id(0) == k)
        def _(k=k):
            weight = refs[k][...].reshape(a0.shape[1], outs[0].shape[1])
            outs[2 * k][...] = dot_nn(a0[...], weight).astype(BF)
            outs[2 * k + 1][...] = dot_nn(a1[...], weight).astype(BF)


def down_products(acts, close_down, far_down, rows_n):
    tokens, hidden_n = acts[0].shape
    span = close_down[0].shape[1]
    near = len(close_down)
    act = pl.BlockSpec((tokens, hidden_n), lambda i: (0, 0))
    ins, operands = [act] * 2, list(acts)
    for k in range(rows_n):
        if k < near or len(far_down) > 1:
            ins.append(pl.BlockSpec((hidden_n, span), lambda i: (0, 0)))
            operands.append(close_down[k] if k < near else far_down[k - near])
        else:
            planes, _, rows, _ = far_down[0].shape
            ins.append(
                pl.BlockSpec((planes, 1, rows, span), lambda i, k=k: (0, k - near, 0, 0))
            )
            operands.append(far_down[0])
    out = pl.pallas_call(
        functools.partial(product_body, near=near),
        grid=(rows_n,),
        in_specs=ins,
        out_specs=[pl.BlockSpec((tokens, span), lambda i: (0, 0))] * (2 * rows_n),
        out_shape=[jax.ShapeDtypeStruct((tokens, span), BF)] * (2 * rows_n),
        compiler_params=pltpu.CompilerParams(vmem_limit_bytes=56 << 20),
        name="down_products",
    )(*operands)
    return {(a, k): out[2 * k + a] for k in range(rows_n) for a in range(2)}


def finish_body(where, *refs, rows_n, dp_n):
    pieces = refs[:rows_n]
    gate_ref, up_ref, down_ref = refs[rows_n:]
    part = pieces[0].shape[1] // dp_n
    share = pieces[0].shape[2]
    for k in range(rows_n):
        sender = where[0] ^ k
        for i in range(rows_n):

            @pl.when(sender == i)
            def _(k=k, i=i):
                for q in range(dp_n):
                    rows = slice(q * part, (q + 1) * part)
                    here = slice((q * rows_n + i) * part, (q * rows_n + i + 1) * part)
                    gate_ref[:, here] = pieces[k][0, rows].astype(F32).T
                    up_ref[:, here] = pieces[k][1, rows].astype(F32).T
                    down_ref[i * part : (i + 1) * part, q * share : (q + 1) * share] = pieces[k][
                        2, rows
                    ].astype(F32)


def finish_weight_grads(where, pieces, rows_n, dp_n):
    _, hidden_n, share = pieces[0].shape
    spec = pl.BlockSpec((3, hidden_n, share), lambda i, w: (0, 0, 0))
    shapes = [(share, rows_n * hidden_n)] * 2 + [(hidden_n, dp_n * share)]
    return pl.pallas_call(
        functools.partial(finish_body, rows_n=rows_n, dp_n=dp_n),
        grid_spec=pltpu.PrefetchScalarGridSpec(
            num_scalar_prefetch=1,
            grid=(1,),
            in_specs=[spec] * rows_n,
            out_specs=[pl.BlockSpec(shape, lambda i, w: (0, 0)) for shape in shapes],
        ),
        out_shape=[jax.ShapeDtypeStruct(shape, F32) for shape in shapes],
        compiler_params=pltpu.CompilerParams(vmem_limit_bytes=40 << 20),
        name="finish_weights",
    )(where, *pieces)


def cut_body(where, *refs, ks, rows_n, dp_n):
    gate, up = refs[:2]
    outs = refs[len(refs) - 2 * len(ks) :]
    down_in = refs[2 : len(refs) - 2 * len(ks)]
    part = gate.shape[1] // (dp_n * rows_n)
    for n, k in enumerate(ks):
        slot = where[0] ^ k
        for i in range(rows_n):

            @pl.when(slot == i)
            def _(n=n, i=i):
                for q in range(dp_n):
                    here = slice((q * rows_n + i) * part, (q * rows_n + i + 1) * part)
                    there = slice(q * part, (q + 1) * part)
                    outs[2 * n][0, there] = gate[:, here].T
                    outs[2 * n][1, there] = up[:, here].T
                    if len(down_in) < len(ks):
                        outs[2 * n + 1][there] = down_in[0][here]

        if len(down_in) == len(ks):
            outs[2 * n + 1][...] = down_in[n][...]


def cut_weights(where, w_gate, w_up, w_down, ks, rows_n, dp_n, rows_in, rows_down):
    hidden_n = w_gate.shape[1] // rows_n
    part = hidden_n // dp_n
    span = w_down.shape[1]
    ins = [pl.BlockSpec((rows_in, w_gate.shape[1]), lambda i, w: (w[1], 0))] * 2
    if rows_down == part:
        for k in ks:
            ins.append(pl.BlockSpec((part, span), lambda i, w, k=k: (w[2] * rows_n + (w[0] ^ k), 0)))
    else:
        ins.append(pl.BlockSpec(w_down.shape, lambda i, w: (0, 0)))
    out_specs, out_shape = [], []
    for _ in ks:
        out_specs += [
            pl.BlockSpec((2, hidden_n, rows_in), lambda i, w: (0, 0, 0)),
            pl.BlockSpec((rows_down, span), lambda i, w: (0, 0)),
        ]
        out_shape += [
            jax.ShapeDtypeStruct((2, hidden_n, rows_in), BF),
            jax.ShapeDtypeStruct((rows_down, span), BF),
        ]
    out = pl.pallas_call(
        functools.partial(cut_body, ks=ks, rows_n=rows_n, dp_n=dp_n),
        grid_spec=pltpu.PrefetchScalarGridSpec(
            num_scalar_prefetch=1, grid=(1,), in_specs=ins, out_specs=out_specs
        ),
        out_shape=out_shape,
        compiler_params=pltpu.CompilerParams(vmem_limit_bytes=40 << 20),
        name="cut_weights",
    )(where, w_gate, w_up, *([w_down] * (len(ins) - 2)))
    return out[0::2], out[1::2]


def cut_plain(row, w_gate, w_up, w_down, ks, rows_n, dp_n):
    part = w_gate.shape[1] // (dp_n * rows_n)
    cut_in, cut_down = [], []
    for k in ks:
        starts = [(q * rows_n + (row ^ k)) * part for q in range(dp_n)]
        both = []
        for w in (w_gate.T, w_up.T):
            both.append(jnp.concatenate([lax.dynamic_slice_in_dim(w, at, part, 0) for at in starts]))
        cut_in.append(jnp.stack(both))
        cut_down.append(
            jnp.concatenate([lax.dynamic_slice_in_dim(w_down, at, part, 0) for at in starts])
        )
    return cut_in, cut_down


def tie(value, *others):
    return lax.optimization_barrier((value, others))[0]


def per_device(
    rows_n,
    tokens,
    seq_ids,
    block_ids,
    positions,
    norm1_gain,
    norm2_gain,
    w_query,
    w_kv,
    w_out,
    w_gate,
    w_up,
    w_down,
    grad_output,
):
    R = rows_n
    bits = []
    while (1 << len(bits)) < R:
        bits.append(1 << len(bits))
    nbits = len(bits)

    def reverse(v):
        out = 0
        for b in range(nbits):
            out = out | (((v >> b) & 1) << (nbits - 1 - b))
        return out

    order = [reverse(v) for v in range(R)]
    row = lax.axis_index("row")
    col = lax.axis_index("col")
    half_rows, dslice = tokens.shape
    B = half_rows // R
    full_rows = 2 * half_rows
    width = w_kv.shape[1] // 2
    dp_n = lax.axis_size("dp")

    def tf(flag, value, *others):
        return tie(value, *others) if FL.get(flag, 0) else value

    def tc(flag, value, *options):
        k = FL.get(flag, 0)
        return tie(value, options[k - 1]) if k else value

    def swap_row(a, bit):
        return lax.ppermute(a, "row", [(i, i ^ bit) for i in range(R)])

    def swap_col(a):
        return lax.ppermute(a, "col", [(0, 1), (1, 0)])

    def psum_row(a):
        for bit in bits:
            a = a + swap_row(a, bit)
        return a

    def pick(a, index, size):
        return lax.dynamic_slice_in_dim(a, index * size, size, 0)

    def to_order(a):
        return jnp.concatenate([pick(a, row ^ order[p], B) for p in range(R)], axis=0)

    def from_order(a):
        return jnp.concatenate([pick(a, reverse(row ^ b), B) for b in range(R)], axis=0)

    def reduce_row(a, send_after=(), use_after=()):
        a = a.astype(BF)
        for bit in bits:
            half = a.shape[0] // 2
            keep, send = a[:half], a[half:]
            if bit == bits[-1]:
                send = tie(send, send_after)
            came = swap_row(send, bit)
            if bit == bits[-1]:
                came = tie(came, use_after)
            total = keep.astype(F32) + came.astype(F32)
            a = total.astype(BF)
        return total

    def gather_outer(a):
        for bit in reversed(bits[1:]):
            a = jnp.concatenate([a, swap_row(a, bit)], axis=0)
        return a

    def gather_core(a):
        return jnp.concatenate([a, swap_row(a, 1)], axis=0)

    def gather_row(a):
        return gather_core(gather_outer(a))

    def spread(pieces, bit):
        out = dict(pieces)
        for (a, k), value in pieces.items():
            out[(a, k ^ bit)] = swap_row(value, bit)
        return out

    def spread_col(pieces):
        out = dict(pieces)
        for (a, k), value in pieces.items():
            out[(1 - a, k)] = swap_col(value)
        return out

    half = half_rows // 2

    def gather_plane(mine):
        first = came = spread_col({(0, 0): mine[:half]})
        for bit in reversed(bits[1:]):
            first = spread(first, bit)
        second = {(0, 0): mine[half:]}
        for bit in reversed(bits[1:]):
            second = spread(second, bit)
        second = spread_col(second)
        return (spread(first, 1), spread(second, 1)), came

    def add(a, b, wide=False):
        total = a.astype(F32) + b.astype(F32)
        return total if wide else total.astype(BF)

    def plane_core(blocks):
        moved = {(a, k): swap_row(blocks[(a, k ^ 1)], 1) for a in (1, 0) for k in range(0, R, 2)}
        halves = (slice(0, half), slice(half, 2 * half))
        return [{key: add(blocks[key][h], value[h]) for key, value in moved.items()} for h in halves]

    def plane_rest(parts, after=((), ()), then=(), use_after=()):
        def by_col(cur, last, use_after=()):
            return {
                (0, k): add(v, tie(swap_col(cur[(1, k)]), use_after), last)
                for (a, k), v in cur.items()
                if a == 0
            }

        def by_rows(cur, last, use_after=()):
            for bit in bits[1:]:
                cur = {
                    (a, k): add(
                        v, tie(swap_row(cur[(a, k ^ bit)], bit), use_after), last and bit == bits[-1]
                    )
                    for (a, k), v in cur.items()
                    if not k & bit
                }
            return cur

        first = by_col(tie(parts[0], after[0]), False, use_after)
        second = by_rows(tie(parts[1], after[1]), False, use_after)
        outs = [by_rows(tie(first, then), True), by_col(tie(second, then), True)]
        return jnp.concatenate([o[(0, 0)] for o in outs], axis=0)

    residual = tokens.astype(F32)
    scale_one = lax.rsqrt(psum_row(jnp.sum(residual * residual, axis=1)) / D + EPS)
    weighted_in = (residual * norm1_gain[None, :]).astype(BF)
    ordered_in = to_order(weighted_in)
    w_query_far = swap_col(w_query)
    own = col * R + row
    own_scale = lax.dynamic_slice_in_dim(scale_one, row * B, B)[:, None]

    kv_pre = reduce_row(dot_nn(ordered_in, w_kv)) * own_scale
    query_near = reduce_row(dot_nn(ordered_in, w_query)) * own_scale

    z = lax.axis_index("dp")
    near = min(2, R)
    hidden_n = w_gate.shape[1] // R
    shared = (dslice % (128 * dp_n) == 0, hidden_n % (16 * dp_n) == 0)
    shared = (all(shared), all(shared))
    rows_in = dslice // dp_n if shared[0] else dslice
    rows_down = hidden_n // dp_n if shared[1] else hidden_n

    shares = jnp.stack([row, z if shared[0] else 0 * z, z if shared[1] else 0 * z])
    shares = tie(shares, kv_pre)
    far_ks = tuple(range(near, R))
    part = hidden_n // dp_n
    if part % 16 == 0:
        cut_in, cut_down = cut_weights(shares, w_gate, w_up, w_down, far_ks, R, dp_n, rows_in, rows_down)
    else:
        cut_in, cut_down = cut_plain(row, w_gate, w_up, w_down, far_ks, R, dp_n)
    half_width = width // 2
    frequency = ROPE_BASE ** (-2.0 * jnp.arange(half_width, dtype=F32) / width)
    own_positions = lax.dynamic_slice_in_dim(positions, own * B, B)
    angles = own_positions.astype(F32)[:, None] * frequency[None, :]
    cosine = jnp.concatenate([jnp.cos(angles)] * 2, axis=1)
    sine_half = jnp.sin(angles)
    sine = jnp.concatenate([-sine_half, sine_half], axis=1)

    key_pre = kv_pre[:, :width]
    key_turned = jnp.concatenate([key_pre[:, half_width:], key_pre[:, :half_width]], axis=1)
    key_own = key_pre * cosine + key_turned * sine
    kv_own = jnp.concatenate([key_own, kv_pre[:, width:]], axis=1).astype(BF)
    kv_pieces = spread_col({(0, 0): kv_own})
    for bit in reversed(bits):
        kv_pieces = spread(kv_pieces, bit)
    kv_all = [kv_pieces[(a, k)] for a in range(2) for k in range(R)]
    meta = (jnp.stack([row, col]), seq_ids, block_ids)
    far_in = [swap_row(a, k) for a, k in zip(tf("f11", cut_in, kv_all), far_ks)]
    far_cut_down = cut_down
    if shared[0]:
        far_in = [jnp.stack(far_in)]
    w_out_far = swap_col(tc("f13", w_out, w_query_far, query_near, kv_pre))
    query_near = tf("f0", query_near, w_out_far)
    query_near = tf("f1", query_near, far_in)
    close_ks = tuple(range(near))
    if part % 16 == 0:
        shares = shares * jnp.array([1, 0, 0], jnp.int32)
        cut_in, cut_down = cut_weights(shares, w_gate, w_up, w_down, close_ks, R, dp_n, dslice, hidden_n)
    else:
        cut_in, cut_down = cut_plain(row, w_gate, w_up, w_down, close_ks, R, dp_n)
    close_in = [swap_row(a, k) if k else a for k, a in enumerate(cut_in)]
    close_down = [swap_row(a, k) if k else a for k, a in enumerate(cut_down)]
    query_near_raw = query_near
    down_grad = grad_output.astype(BF)
    part_qfar = dot_nn(ordered_in, w_query_far).astype(BF)
    if FL.get("f5", 0) < 3:
        grad_pieces = {(0, 0): tc("f5", down_grad, kv_pre, query_near)}
        for bit in reversed(bits[1:]):
            grad_pieces = spread(grad_pieces, bit)
        query_near = tf("f15", query_near, grad_pieces[(0, bits[-1])])
    att_near, rot_near, lse_near = attend(meta, query_near, cosine, sine, kv_all, width, R)
    if FL.get("f5", 0) >= 3:
        grad_pieces = {(0, 0): tie(down_grad, att_near)}
        for bit in reversed(bits[1:]):
            grad_pieces = spread(grad_pieces, bit)
    grad_rows = dict(grad_pieces)
    for (a, k), value in grad_rows.items():
        if k:
            grad_pieces[(1, k)] = swap_col(value)
        else:
            grad_pieces[(1, k)] = swap_col(tc("f12", down_grad, w_query_far, query_near_raw, w_out_far, att_near))
    query_far = reduce_row(
        part_qfar,
        send_after=query_near_raw if FL.get("f9", 0) else (),
        use_after=(att_near, close_in),
    )
    query_far = tf("f2", query_far, grad_pieces[(1, 0)])
    query_far = tf("f3", query_far, far_in)
    query_far = tf("f4", query_far, w_out_far)
    query_far = tf("f8", query_far, grad_rows) * own_scale
    if shared[0]:
        far_in = [lax.all_gather(far_in[0], "dp", axis=0)]
    near_outer = gather_outer(att_near)
    query_far = tf("f16", query_far, near_outer)
    att_far, rot_far, lse_far = attend(meta, query_far, cosine, sine, kv_all, width, R)
    far_cut_down = tc("f10", far_cut_down, query_near_raw, att_near, att_far, near_outer)
    far_down = [swap_row(a, k) for a, k in zip(far_cut_down, far_ks)]
    if shared[1]:
        far_down = [lax.all_gather(jnp.stack(far_down), "dp", axis=0)]

    all_near = gather_core(near_outer)
    far_outer = gather_outer(att_far)
    far_outer = tf("f6", far_outer, grad_rows)
    far_outer = tf("f17", far_outer, grad_pieces)
    all_far = gather_core(far_outer)
    hidden = residual + from_order(dot_nn(all_near, w_out) + dot_nn(all_far, w_out_far))

    def exchange(parts):
        return [parts[0]] + [swap_row(parts[k], k) for k in range(1, len(parts))]

    scale_two = lax.rsqrt(psum_row(jnp.sum(hidden * hidden, axis=1)) / D + EPS)[:, None]
    normed_two = (hidden * scale_two * norm2_gain[None, :]).astype(BF)
    normed_pieces, came = gather_plane(tf("f7", normed_two, grad_pieces))
    grad_pieces = spread(tf("f14", grad_pieces, came), 1)

    fed = {}
    backs = {}
    for a in (0, 1):
        fed[a] = feed(
            [[part[(a, k)] for k in range(R)] for part in normed_pieces],
            [grad_pieces[(a, k)] for k in range(R)],
            close_in,
            close_down,
            far_in,
            far_down,
            shared,
            dp_n,
        )
        for k in range(R):
            backs[(a, k)] = fed[a][3 + k]
    acts, gate_grads, up_grads = ([fed[a][j] for a in range(2)] for j in range(3))
    normed_halves, grad_halves = ([fed[a][3 + R + j] for a in range(2)] for j in range(2))
    core_sums = plane_core(backs)
    normed2_grad = None if FL.get("b37", 0) else plane_rest(core_sums)

    def place(pieces):
        moved = jnp.stack(exchange([jnp.stack([p[k] for p in pieces]) for k in range(R)]))
        ordered = [lax.dynamic_index_in_dim(moved, row ^ s, 0, keepdims=False) for s in range(R)]
        return [jnp.stack([o[n] for o in ordered]) for n in range(len(pieces))]

    def ff_input_place(rows):
        rows = rows.reshape(R, dp_n, part, -1).transpose(1, 0, 2, 3)
        return rows.reshape(R * hidden_n, -1).astype(F32).T

    def over_dp(local):
        return lax.psum_scatter(local, "dp", scatter_dimension=0, tiled=True)

    gate_local = feed_weight_grad(normed_halves, gate_grads, R, dp_n)
    gate_piece = over_dp(gate_local)
    if shared[1]:
        late = late_weight_grads(
            normed_halves, tf("b0", tie(up_grads, gate_local), core_sums), grad_halves, acts, R, dp_n
        )
        late_piece = over_dp(tie(late, gate_local))
        if FL.get("b37", 0):
            normed2_grad = plane_rest(core_sums, use_after=late)
        up_piece, down_piece = late_piece[0, 0], late_piece[0, 1]
        normed2_grad = tie(normed2_grad, gate_local, late)
    else:
        late_piece = gate_piece
        normed2_grad = plane_rest(core_sums)
        up_piece = over_dp(feed_weight_grad(normed_halves, up_grads, R, dp_n))[0]
        down_piece = over_dp(down_weight_grad(acts, grad_halves, R, dp_n))[0]

    weighted = normed2_grad * norm2_gain[None, :]
    inner_two = psum_row(jnp.sum(weighted * hidden, axis=1))[:, None]
    hidden_grad = grad_output + (
        scale_two * weighted - hidden * (scale_two * scale_two * scale_two) * inner_two / D
    )
    gain_two = jnp.sum(normed2_grad * hidden * scale_two, axis=0)
    branch_ordered = to_order(hidden_grad.astype(BF))
    part_far = dot_nt(branch_ordered, w_out_far).astype(BF)
    part_near = dot_nt(branch_ordered, w_out).astype(BF)
    prod_dep = FL.get("b5", 0)
    branch_late, late_acts = branch_ordered, acts

    def make_products():
        return down_products(late_acts, close_down, far_down, R)

    if prod_dep < 2:
        late_acts = tie(acts, hidden_grad) if prod_dep == 0 else tie(acts, part_far, part_near)
        products = make_products()
    b6 = FL.get("b6", 0) if prod_dep < 2 else 0
    att_grad_far = reduce_row(part_far, use_after=products if b6 == 1 else ()).astype(BF)
    att_grad_near = reduce_row(
        part_near, send_after=att_grad_far if FL.get("b25", 0) else (), use_after=products if b6 == 2 else ()
    ).astype(BF)
    gout_early = FL.get("b26", 0)
    if gout_early:
        grad_out_far = dot_tn(all_far, branch_late).astype(BF)
        grad_out_came = swap_col(grad_out_far)
        grad_out_near = dot_tn(all_near, branch_late)
        att_grad_far = tf("b27", att_grad_far, grad_out_far, grad_out_near)
        att_grad_far = tf("b4", att_grad_far, grad_out_came)
    att_grad_far = tf("b2", att_grad_far, gate_piece)
    att_grad_far = tf("b3", att_grad_far, att_grad_near)

    qpg_far, dk, dv = attend_back(
        meta, rot_far, att_grad_far, att_far, lse_far, cosine, sine, kv_all, width, R
    )
    if not gout_early:
        branch_late = tie(branch_ordered, qpg_far)
        grad_out_far = dot_tn(all_far, branch_late).astype(BF)
        grad_out_came = swap_col(grad_out_far)
        grad_out_near = dot_tn(all_near, branch_late)
    if prod_dep == 2:
        late_acts = tie(acts, qpg_far)
        products = make_products()
    scale_col = scale_one[:, None]
    normed_ordered = to_order((residual * scale_col * norm1_gain[None, :]).astype(BF))
    qpg_far_outer = gather_outer(tf("b28", qpg_far, grad_out_far))
    qpg_far_all = gather_core(qpg_far_outer)
    qpg_far_used = tf("b8", qpg_far_all, grad_out_near)
    if prod_dep < 3:
        qpg_far_used = tf("b29", qpg_far_used, products)
    grad_query_far = dot_tn(normed_ordered, qpg_far_used).astype(BF)
    grad_query_came = swap_col(grad_query_far)
    att_grad_near = tf("b30", att_grad_near, qpg_far_outer)
    att_grad_near = tf("b7", att_grad_near, grad_query_far)
    att_grad_near = tf("b31", att_grad_near, grad_out_came)
    qpg_near, dk, dv = attend_back(
        meta, rot_near, att_grad_near, att_near, lse_near, cosine, sine, kv_all, width, R,
        (dk, dv),
    )
    if prod_dep == 3:
        late_acts = tie(acts, qpg_near)
        products = make_products()
    grad_out_local = add(grad_out_near, tc("b24", grad_out_came, qpg_far, qpg_near))
    grad_out = over_dp(tc("b18", grad_out_local, gate_piece, late_piece))
    qpg_near_outer = gather_outer(tf("b32", qpg_near, grad_out_local))
    qpg_near_all = gather_core(qpg_near_outer)
    qpg_near_used = tf("b19", tie(qpg_near_all, grad_query_came), late_piece)
    grad_query_near = dot_tn(normed_ordered, qpg_near_used)
    grad_query_local = add(grad_query_near, grad_query_came)
    opts = (qpg_far, qpg_near, qpg_near_outer, grad_query_came, grad_query_local)
    pick_opt = lambda k: () if not k else opts[k - 1]
    down_sum = plane_rest(
        plane_core(products),
        after=(pick_opt(FL.get("b13", 0)), pick_opt(FL.get("b14", 0))),
        then=pick_opt(FL.get("b15", 0)),
    )
    output = hidden + down_sum
    dk, dv = tc("b9", (dk, dv), qpg_near_outer, grad_out_local, grad_query_came, grad_query_local)

    dkv = jnp.concatenate([dk * width**-0.5, dv], axis=2).astype(BF)
    cur = {(a, k): dkv[a * R + k] for a in range(2) for k in range(R)}
    for bit in bits:
        cur = {
            (a, k): add(v, swap_row(cur[(a, k ^ bit)], bit))
            for (a, k), v in cur.items()
            if not k & bit
        }
    dkv_own = cur[(0, 0)].astype(F32) + swap_col(cur[(1, 0)]).astype(F32)
    dk_own = dkv_own[:, :width]
    dk_turned = jnp.concatenate([dk_own[:, half_width:], dk_own[:, :half_width]], axis=1)
    kvg_own = jnp.concatenate(
        [dk_own * cosine - dk_turned * sine, dkv_own[:, width:]], axis=1
    ).astype(BF)


    pieces = tc("b17", (gate_piece[0], up_piece, down_piece), qpg_near, grad_query_local, qpg_near_outer)
    moved = exchange([jnp.stack([p[k] for p in pieces]) for k in range(R)]) if shared[1] else ()
    kvg_own = tf("b36", kvg_own, moved)
    kvg_own = tc("b16", kvg_own, qpg_near_outer, grad_query_came, grad_query_local)
    kvg_all = gather_row(kvg_own)
    normed1_grad = from_order(
        dot_nt(qpg_far_all, w_query_far) + dot_nt(qpg_near_all, w_query) + dot_nt(kvg_all, w_kv)
    )
    normed1_grad = tf("b22", normed1_grad, grad_out)
    normed1_grad = tf("b33", normed1_grad, moved)
    normed1_grad = tf("b34", normed1_grad, grad_query_local)
    normed1_grad = tf("b23", normed1_grad, output)
    weighted_one = normed1_grad * norm1_gain[None, :]
    inner_one = psum_row(jnp.sum(weighted_one * residual, axis=1))[:, None]
    input_grad = hidden_grad + (
        scale_col * weighted_one - residual * (scale_col * scale_col * scale_col) * inner_one / D
    )
    gain_one = jnp.sum(normed1_grad * residual * scale_col, axis=0)

    grad_query = over_dp(tf("b20", grad_query_local, grad_out))
    if shared[1]:
        grad_gate, grad_up, grad_down = finish_weight_grads(meta[0], moved, R, dp_n)
    else:
        gate_rows, up_rows = place(pieces[:2])
        grad_gate, grad_up = ff_input_place(gate_rows), ff_input_place(up_rows)
        grad_down = place(pieces[2:])[0].reshape(hidden_n, dslice).astype(F32)

    rest = dslice // (2 * dp_n)
    gains = jnp.concatenate(
        [g.reshape(dp_n, 2, 1, rest) for g in (gain_one, gain_two)]
        + [jnp.zeros((dp_n, 2, 1, 2 * width - 2 * rest), F32)],
        axis=3,
    )
    local = dot_tn(normed_ordered, kvg_all).reshape(dp_n, 2, rest, 2 * width)
    local = jnp.concatenate([local, gains], axis=2)
    mine = lax.dynamic_index_in_dim(local, col, 1, keepdims=False)
    other = lax.dynamic_index_in_dim(local, 1 - col, 1, keepdims=False).astype(BF)
    both = mine + swap_col(other).astype(F32)
    small = lax.dynamic_index_in_dim(both, z, 0, keepdims=False)
    for j in range(1, dp_n):
        share = lax.dynamic_index_in_dim(both, z ^ j, 0, keepdims=False).astype(BF)
        share = lax.ppermute(share, "dp", [(i, i ^ j) for i in range(dp_n)])
        small = small + share.astype(F32)

    return (
        output,
        input_grad,
        grad_query.astype(F32)[None],
        small[None, :rest],
        grad_out.astype(F32)[None],
        grad_gate[None],
        grad_up[None],
        grad_down[None],
        small[rest:, :rest],
        small[rest:, rest : 2 * rest],
    )


def solution(mesh):
    placed = (
        P(("dp", "col"), "row"),
        P("dp"),
        P("dp"),
        P("dp"),
        P("row"),
        P("row"),
        P("row", "col"),
        P("row", None),
        P("col", "row"),
        P("row", "col"),
        P("row", "col"),
        P("col", "row"),
        P(("dp", "col"), "row"),
    )
    return jax.shard_map(
        functools.partial(per_device, mesh.shape["row"]),
        mesh=mesh,
        in_specs=placed,
        out_specs=(
            P(("dp", "col"), "row"),
            P(("dp", "col"), "row"),
            P("row", "dp", "col"),
            P("row", ("dp", "col"), None),
            P("col", "dp", "row"),
            P("row", "dp", "col"),
            P("row", "dp", "col"),
            P("col", "dp", "row"),
            P("row", ("dp", "col")),
            P("row", ("dp", "col")),
        ),
        check_vma=False,
    )
```
